256 devices in a mesh: atom: 8 (over x, core), ka: 32 (over y, z).
Axes of the slice: x: 4, y: 4, z: 8, core: 2. Of those that a mesh axis runs over, the one named last changes fastest.
Arguments:
- positions: float32 [3, 131072], P(None, 'atom'), may hold values from 0 to 1
- features: bfloat16 [64, 131072], P(None, 'atom'), may hold values from -6 to 6
- species: int32 [131072], P('atom'), may hold values from 0 to 7
- miller: int32 [3, 4096], P(None, 'ka'), may hold values from -8 to 8
- species_table: float32 [64, 8], replicated, may hold values from -6 to 6
- filter_weight: float32 [64, 16], replicated, may hold values from -6 to 6
- norm_gain: float32 [64], replicated, may hold values from 0.25 to 1.75
- up_weight: bfloat16 [256, 64], replicated, may hold values from -0.75 to 0.75
- down_weight: bfloat16 [64, 256], replicated, may hold values from -0.375 to 0.375
Outputs:
- updated: bfloat16 [64, 131072], P(None, ('atom', 'ka'))
The draws below stay inside these ranges and needn't reach their ends.
All inputs are finite; a program needn't handle non-finite values.
Results may differ from the reference program's by a relative error of at most 0.006.
Values may be sent and summed in bfloat16 or wider, within the bound.
A program may use at most 64 MiB of HBM per device.

```python
import math
import jax
import jax.numpy as jnp
from jax import lax

C = 64
K = 4096
NRBF = 16
HID = 256
NSPEC = 8
NATOMS = 131072


def plant(result, key, least, high):
    index_at = [jax.random.randint(jax.random.fold_in(key, axis), (), 0, length) for axis, length in enumerate(result.shape)]
    main_axis = result.shape.index(max(result.shape))
    beside = index_at[:main_axis] + [(index_at[main_axis] + 1) % result.shape[main_axis]] + index_at[main_axis + 1:]
    return result.at[tuple(index_at)].set(least).at[tuple(beside)].set(high)


def steps_of(stream_key, shape, pieces, least, high):
    loudness, own = 1.0, jax.random.fold_in(stream_key, 6)
    for position, blocks in pieces:
        draws = jnp.exp(jax.random.uniform(jax.random.fold_in(own, position), (blocks,), jnp.float32, least / len(pieces), high / len(pieces)))
        loudness = loudness * jnp.repeat(draws, shape[position] // blocks).reshape([-1 if axis == position else 1 for axis in range(len(shape))])
    return loudness


def scatter_about(key, shape, deviation, reach, shards=(), kind=jnp.bfloat16):
    entries = deviation * jax.random.normal(key, shape, jnp.float32)
    if shards:
        entries = entries * steps_of(key, shape, shards, -0.22, 0.18)
    return jnp.clip(entries, -reach, reach).astype(kind)


def setup_inputs(seed: int = 0) -> dict:
    splits = jax.random.split(jax.random.key(seed), 10)
    positions = jnp.clip(1.0 * jax.random.uniform(splits[0], (3, NATOMS), jnp.float32) ** steps_of(splits[0], (3, NATOMS), ((1, 8),), -0.2, 0.2), 0.0, 1.0)
    features = scatter_about(splits[1], (C, NATOMS), 1.0, 6.0, ((1, 8),))
    species = plant(jax.random.randint(splits[2], (NATOMS,), 0, NSPEC), jax.random.fold_in(splits[2], 1), 0, NSPEC - 1).astype(jnp.int32)
    miller = plant(jax.random.randint(splits[3], (3, K), -8, 9), jax.random.fold_in(splits[3], 1), -8, 8).astype(jnp.int32)
    species_table = scatter_about(splits[4], (C, NSPEC), 1.0, 6.0, (), jnp.float32)
    filter_weight = scatter_about(splits[5], (C, NRBF), 1.0, 6.0, (), jnp.float32)
    norm_gain = jnp.clip(1.0 + 0.15 * jax.random.normal(splits[6], (C,), jnp.float32), 0.25, 1.75)
    up_weight = scatter_about(splits[7], (HID, C), C ** -0.5, 0.75)
    down_weight = scatter_about(splits[8], (C, HID), HID ** -0.5, 0.375)
    return dict(positions=positions, features=features, species=species, miller=miller, species_table=species_table, filter_weight=filter_weight, norm_gain=norm_gain, up_weight=up_weight, down_weight=down_weight)


two_pi = 2.0 * math.pi
k_cutoff = 14.0
block_width = 128

def phases(coords, vectors):
    values = vectors.astype(jnp.float32)
    angles = two_pi * (coords[0][:, None] * values[0][None, :] + coords[1][:, None] * values[1][None, :] + coords[2][:, None] * values[2][None, :])
    return (jnp.cos(angles).astype(jnp.bfloat16), jnp.sin(angles).astype(jnp.bfloat16))

def radial_filter(vectors, filter_weight):
    values = vectors.astype(jnp.float32)
    magnitude = jnp.sqrt(values[0] * values[0] + values[1] * values[1] + values[2] * values[2])
    centers = jnp.arange(NRBF, dtype=jnp.float32) * (k_cutoff / (NRBF - 1))
    basis = jnp.exp(-jnp.square((magnitude[None, :] - centers[:, None]) / (k_cutoff / NRBF)))
    return jnp.dot(filter_weight, basis, precision=lax.Precision.HIGHEST, preferred_element_type=jnp.float32)

def project_back(filtered, cosines, sines):
    dims = (((1,), (1,)), ((), ()))
    first = lax.dot_general(filtered[0], cosines, dims, preferred_element_type=jnp.float32)
    return first + lax.dot_general(filtered[1], sines, dims, preferred_element_type=jnp.float32)

def reference(positions, features, species, miller, species_table, filter_weight, norm_gain, up_weight, down_weight):
    source = (features.astype(jnp.float32) + species_table[:, species]).astype(jnp.bfloat16)
    blocks = miller.reshape(3, K // block_width, block_width).transpose(1, 0, 2)
    scaling = 1.0 / math.sqrt(NATOMS * K)

    def factor_block(vectors):
        cosines, sines = phases(positions, vectors)
        real_part = jnp.dot(source, cosines, preferred_element_type=jnp.float32)
        imag_part = jnp.dot(source, sines, preferred_element_type=jnp.float32)
        radial = radial_filter(vectors, filter_weight)
        return (jnp.stack([real_part, imag_part]) * radial[None] * scaling).astype(jnp.bfloat16)
    filtered = lax.map(factor_block, blocks)

    def back_step(running, inputs):
        vectors, factor_part = inputs
        cosines, sines = phases(positions, vectors)
        return (running + project_back(factor_part, cosines, sines), None)
    message, _ = lax.scan(back_step, jnp.zeros((C, NATOMS), jnp.float32), (blocks, filtered))
    mean_sq = lax.optimization_barrier(jnp.mean(message * message, axis=0, keepdims=True))
    normed = (message * lax.rsqrt(mean_sq + 1e-06) * norm_gain[:, None]).astype(jnp.bfloat16)
    hidden = jax.nn.silu(jnp.dot(up_weight, normed, preferred_element_type=jnp.float32)).astype(jnp.bfloat16)
    update = jnp.dot(down_weight, hidden, preferred_element_type=jnp.float32)
    return (features.astype(jnp.float32) + update).astype(jnp.bfloat16)
```

```python
import functools
import math

import jax
import jax.numpy as jnp
from jax import lax
from jax.experimental import pallas as pl
from jax.experimental.pallas import tpu as pltpu
from jax.sharding import PartitionSpec as P

MESH = pl.DeviceIdType.MESH
F32, BF16 = jnp.float32, jnp.bfloat16
NRBF = 16
NSPEC = 8
MAXM = 8
XYR = 304
LW = 384
CHUNK = 512
K_CUTOFF = 14.0

def _fit():
    import numpy as np

    n = 400
    u = 0.125 + 0.125 * np.cos(np.pi * (np.arange(n) + 0.5) / n)
    r = np.sqrt(u)
    c = np.polynomial.chebyshev.Chebyshev.fit(u, np.cos(2 * np.pi * r), 5, domain=[0, 0.25])
    s = np.polynomial.chebyshev.Chebyshev.fit(u, np.sin(2 * np.pi * r) / r, 5, domain=[0, 0.25])
    return (
        [float(v) for v in c.convert(kind=np.polynomial.Polynomial).coef],
        [float(v) for v in s.convert(kind=np.polynomial.Polynomial).coef],
    )


COS_COEF, SIN_COEF = _fit()


def poly(u, coef):
    acc = jnp.full_like(u, coef[-1])
    for c in coef[-2::-1]:
        acc = acc * u + c
    return acc


def harmonics(row, orders):
    t = row * orders
    r = t - jnp.round(t)
    u = r * r
    return poly(u, COS_COEF), r * poly(u, SIN_COEF)


def iota(shape, axis):
    return lax.broadcasted_iota(jnp.int32, shape, axis)


def lane_orders(tile, shape, axis):
    lane = iota(shape, axis)
    low = lane & 7
    if tile < 2:
        ta = jnp.full(shape, tile, jnp.int32)
        p = (lane >> 4) + 1
        tb = (lane >> 3) & 1
        q = low + 1
        return ta, p, tb, q, lane >= 0
    odd = (lane >> 3) & 1
    in_x, in_y = lane < 16, (lane >= 16) & (lane < 32)
    zero = jnp.zeros(shape, jnp.int32)
    ta = jnp.where(in_x, odd, zero)
    p = jnp.where(in_x, low + 1, zero)
    tb = jnp.where(in_y, odd, zero)
    q = jnp.where(in_y, low + 1, zero)
    return ta, p, tb, q, lane < 33


def swap8(x):
    lane = iota(x.shape, 1)
    return jnp.where((lane & 8) == 0, pltpu.roll(x, 120, 1), pltpu.roll(x, 8, 1))


def tiles_of(x):
    return [x[:, 128 * t : 128 * (t + 1)] for t in range(3)]


def partners(g):
    s = [swap8(t) for t in g]
    lane = iota(g[0].shape, 1)
    zero = jnp.zeros_like(g[0])
    la = [g[1], g[0], jnp.where(lane < 16, s[2], zero)]
    lb = [s[0], s[1], jnp.where((lane >= 16) & (lane < 32), s[2], zero)]
    return la, lb, [s[1], s[0], zero]


def body_kernel(
    sizes,
    pos_ref,
    feat_hbm,
    species_ref,
    miller_ref,
    tab_ref,
    fw_ref,
    gain_ref,
    up_ref,
    down_ref,
    out_ref,
    feat_blk,
    feat_loc,
    xy,
    zz,
    gacc,
    gsend,
    grecv,
    mil_all,
    codes,
    wacc,
    hmat,
    msgs,
    mrecv,
    mflat,
    local_sem,
    mil_send,
    mil_recv,
    g_send,
    g_recv,
    m_send,
    m_recv,
):
    n_atom, n_ka, atoms, scaling = sizes
    ia, ik = lax.axis_index("atom"), lax.axis_index("ka")
    local = atoms // n_ka
    n_chunks = atoms // CHUNK

    block = pltpu.make_async_copy(
        feat_hbm.at[pl.ds(pl.multiple_of((ik // 4) * 8, 8), 8), :], feat_blk, local_sem.at[0]
    )
    block.start()
    mine = pltpu.make_async_copy(
        feat_hbm.at[:, pl.ds(pl.multiple_of(ik * local, local), local)], feat_loc, local_sem.at[1]
    )
    mine.start()

    barrier = pltpu.get_barrier_semaphore()

    def greet_ka(d, _):
        pl.semaphore_signal(barrier, inc=1, device_id=(ia, lax.rem(ik + d, n_ka)), device_id_type=MESH)
        return 0

    lax.fori_loop(1, n_ka, greet_ka, 0)

    def greet_atom(d, _):
        pl.semaphore_signal(barrier, inc=1, device_id=(lax.rem(ia + d, n_atom), ik), device_id_type=MESH)
        return 0

    lax.fori_loop(1, n_atom, greet_atom, 0)

    mil_all[ik] = jnp.concatenate(
        [miller_ref[...].astype(F32), jnp.zeros((5, 128), F32)], axis=0
    )

    pl.semaphore_wait(barrier, n_ka - 1 + n_atom - 1)

    def mil_copy(slot, to):
        return pltpu.make_async_remote_copy(
            src_ref=mil_all.at[ik],
            dst_ref=mil_all.at[slot],
            send_sem=mil_send.at[to],
            recv_sem=mil_recv.at[slot],
            device_id=(ia, to),
            device_id_type=MESH,
        )

    def send_miller(d, _):
        mil_copy(ik, lax.rem(ik + d, n_ka)).start()
        return 0

    lax.fori_loop(1, n_ka, send_miller, 0)

    sub = iota((8, CHUNK), 0)
    orders = (sub + 1).astype(F32)
    first_row = sub == 0
    tabs = []
    for c in range(2):
        t = jnp.zeros((8, CHUNK), F32)
        for sp in range(NSPEC):
            t = jnp.where(sub == sp, tab_ref[2 * ik + c, sp], t)
        tabs.append(t)
    which = [sub == lax.rem(2 * ik, 8) + c for c in range(2)]
    gacc[...] = jnp.zeros_like(gacc)
    block.wait()

    def gather_chunk(j, _):
        cols = pl.ds(pl.multiple_of(j * CHUNK, CHUNK), CHUNK)
        xc, xs = harmonics(jnp.broadcast_to(pos_ref[0:1, cols], (8, CHUNK)), orders)
        yc, ys = harmonics(jnp.broadcast_to(pos_ref[1:2, cols], (8, CHUNK)), orders)
        zc, zs = harmonics(jnp.broadcast_to(pos_ref[2:3, cols], (8, CHUNK)), orders)
        zz[0:8, cols] = zc
        zz[8:16, cols] = zs
        for half, xx in enumerate((xc, xs)):
            for a in range(8):
                xa = jnp.broadcast_to(xx[a : a + 1, :], (8, CHUNK))
                r0 = 16 * (8 * half + a)
                xy[r0 : r0 + 16, cols] = jnp.concatenate([xa * yc, xa * ys], axis=0).astype(BF16)
        xy[256:272, cols] = jnp.concatenate([xc, xs], axis=0).astype(BF16)
        xy[272:288, cols] = jnp.concatenate([yc, ys], axis=0).astype(BF16)
        one = jnp.where(first_row, 1.0, 0.0)
        xy[288:304, cols] = jnp.concatenate([one, jnp.zeros_like(one)], axis=0).astype(BF16)
        fb = feat_blk[:, cols].astype(F32)
        spc = jnp.broadcast_to(species_ref[0:1, cols], (8, CHUNK))
        hot = spc == sub
        rows, extra = [], []
        for c in range(2):
            s = jnp.where(which[c], fb, 0.0) + jnp.where(hot, tabs[c], 0.0)
            s = jnp.broadcast_to(jnp.sum(s, axis=0, keepdims=True), (8, CHUNK))
            s = s.astype(BF16).astype(F32)
            rows += [s * zc, s * zs]
            extra.append(jnp.where(first_row, s, 0.0))
        sz = jnp.concatenate(rows + extra, axis=0).astype(BF16)
        gacc[0:XYR, 0:48] += lax.dot_general(
            xy[:, cols], sz, (((1,), (1,)), ((), ())), preferred_element_type=F32
        )
        return 0

    lax.fori_loop(0, n_chunks, gather_chunk, 0)

    gt = gacc[...].T[0:48, :]
    gsend[...] = gt.astype(BF16)

    def g_copy(slot, to):
        return pltpu.make_async_remote_copy(
            src_ref=gsend,
            dst_ref=grecv.at[slot],
            send_sem=g_send.at[to],
            recv_sem=g_recv.at[slot],
            device_id=(to, ik),
            device_id_type=MESH,
        )

    def send_g(d, _):
        g_copy(ia, lax.rem(ia + d, n_atom)).start()
        return 0

    lax.fori_loop(1, n_atom, send_g, 0)

    for t in range(3):
        n = min(128, XYR - 128 * t)
        _, p, _, q, used = lane_orders(t, (128, 128), 0)
        codes[128 * t : 128 * t + n, :] = jnp.where(used, p * 9 + q, -1).astype(F32)[0:n, :]
    wacc[...] = jnp.zeros_like(wacc)
    sub1 = iota((8, 128), 0)
    r8 = (sub1 + 1).astype(F32)
    top = sub1 == 0

    def wait_miller(d, _):
        mil_copy(lax.rem(ik + d, n_ka), ik).wait_recv()
        return 0

    lax.fori_loop(1, n_ka, wait_miller, 0)

    def count_block(j, _):
        m = mil_all[j]
        mx, my, mz = [jnp.broadcast_to(m[i : i + 1, :], (8, 128)) for i in range(3)]
        gx, gy, gz = [jnp.where(v < 0, -1.0, 1.0) for v in (mx, my, mz)]
        code = jnp.abs(mx) * 9.0 + jnp.abs(my)
        hot_xy = jnp.where(
            codes[...] == jnp.broadcast_to(code[0:1, :], (XYR, 128)), 1.0, 0.0
        ).astype(BF16)
        az = jnp.abs(mz)
        hz = jnp.where(az == r8, 1.0, 0.0)
        h0 = jnp.where((az == 0.0) & top, 1.0, 0.0)
        wr = jnp.concatenate(
            [hz, hz * (gy * gz), hz * (gx * gz), hz * (gx * gy), h0, h0 * (gx * gy)], axis=0
        ).astype(BF16)
        wacc[0:XYR, 0:48] += lax.dot_general(
            hot_xy, wr, (((1,), (1,)), ((), ())), preferred_element_type=F32
        )
        return 0

    lax.fori_loop(0, n_ka, count_block, 0)
    wt = wacc[...].T
    w_plain, w_yz, w_xz, w_xy, w_plain0, w_xy0 = [
        tiles_of(wt[8 * i : 8 * i + 8, :]) for i in range(6)
    ]

    signs, radials, radials0 = [], [], []
    for t in range(3):
        ta, p, tb, q, _ = lane_orders(t, (8, 128), 1)
        signs.append((ta, tb))
        pq = (p * p + q * q).astype(F32)
        per_channel = []
        for mag in (jnp.sqrt(pq + r8 * r8), jnp.sqrt(pq)):
            acc = [jnp.zeros((8, 128), F32) for _ in range(2)]
            for b in range(NRBF):
                z = (mag - b * (K_CUTOFF / (NRBF - 1))) / (K_CUTOFF / NRBF)
                e = jnp.exp(-(z * z))
                for c in range(2):
                    acc[c] = acc[c] + fw_ref[2 * ik + c, b] * e
            per_channel.append([v * scaling for v in acc])
        radials.append(per_channel[0])
        radials0.append(per_channel[1])

    def wait_g(d, _):
        g_copy(lax.rem(ia + d, n_atom), ia).wait_recv()
        return 0

    lax.fori_loop(1, n_atom, wait_g, 0)
    grecv[ia] = gsend[...]
    g = grecv[0].astype(F32)
    for i in range(1, n_atom):
        g = g + grecv[i].astype(F32)

    rows = []
    for c in range(2):
        gz = [tiles_of(g[16 * c + 8 * tz : 16 * c + 8 * tz + 8, :]) for tz in range(2)]
        swapped = [partners(v) for v in gz]
        for tz in range(2):
            la, lb, _ = swapped[1 - tz]
            _, _, lab = swapped[tz]
            out = []
            for t in range(3):
                ta, tb = signs[t]
                u = jnp.where(tb == tz, -lb[t], lb[t]) * w_yz[t]
                v = jnp.where(ta == tz, -la[t], la[t]) * w_xz[t]
                w = jnp.where(ta == tb, -lab[t], lab[t]) * w_xy[t]
                out.append((gz[tz][t] * w_plain[t] + u + v + w) * radials[t][c])
            rows.append(jnp.concatenate(out, axis=1))
    for c in range(2):
        g0 = tiles_of(g[32 + 8 * c : 40 + 8 * c, :])
        _, _, lab = partners(g0)
        out = []
        for t in range(3):
            ta, tb = signs[t]
            w = jnp.where(ta == tb, -lab[t], lab[t]) * w_xy0[t]
            out.append((g0[t] * w_plain0[t] + w) * radials0[t][c])
        rows.append(jnp.concatenate(out, axis=1))
    hmat[...] = jnp.concatenate(rows, axis=0).astype(BF16)

    def m_copy(slot, to):
        return pltpu.make_async_remote_copy(
            src_ref=msgs.at[to],
            dst_ref=mrecv.at[slot],
            send_sem=m_send.at[to],
            recv_sem=m_recv.at[slot],
            device_id=(ia, to),
            device_id_type=MESH,
        )

    def message_of(j):
        cols = pl.ds(pl.multiple_of(j * CHUNK, CHUNK), CHUNK)
        d = jnp.dot(hmat[:, 0:XYR], xy[:, cols], preferred_element_type=F32)
        zc, zs = zz[0:8, cols], zz[8:16, cols]
        parts = []
        for c in range(2):
            s = d[16 * c : 16 * c + 8, :] * zc + d[16 * c + 8 : 16 * c + 16, :] * zs
            s = s + d[32 + 8 * c : 40 + 8 * c, :]
            s = jnp.sum(s, axis=0, keepdims=True)
            parts += [s[:, 128 * i : 128 * (i + 1)] for i in range(CHUNK // 128)]
        return jnp.concatenate(parts, axis=0).astype(BF16)

    def send_message(d, _):
        j = lax.rem(ik + d, n_ka)
        msgs[j] = message_of(j)
        m_copy(ik, j).start()
        return 0

    lax.fori_loop(1, n_ka, send_message, 0)
    mrecv[ik] = message_of(ik)

    mine.wait()

    def wait_message(d, _):
        m_copy(lax.rem(ik + d, n_ka), ik).wait_recv()
        return 0

    lax.fori_loop(1, n_ka, wait_message, 0)

    mflat[...] = mrecv[...].astype(F32).reshape(mflat.shape)
    message = jnp.concatenate(
        [mflat[pl.ds(i, 64, stride=4), :] for i in range(local // 128)], axis=1
    )
    eye = iota((64, 64), 0) == iota((64, 64), 1)
    gain = jnp.sum(jnp.where(eye, jnp.broadcast_to(gain_ref[...], (64, 64)), 0.0), axis=1, keepdims=True)
    mean_sq = jnp.sum(message * message, axis=0, keepdims=True) * (1.0 / 64.0)
    normed = (message * lax.rsqrt(mean_sq + 1e-06) * gain).astype(BF16)
    hidden = jnp.dot(up_ref[...], normed, preferred_element_type=F32)
    hidden = (hidden / (1.0 + jnp.exp(-hidden))).astype(BF16)
    update = jnp.dot(down_ref[...], hidden, preferred_element_type=F32)
    out_ref[...] = (feat_loc[...].astype(F32) + update).astype(BF16)

    def drain_ka(d, _):
        to = lax.rem(ik + d, n_ka)
        mil_copy(ik, to).wait_send()
        m_copy(ik, to).wait_send()
        return 0

    lax.fori_loop(1, n_ka, drain_ka, 0)

    def drain_atom(d, _):
        g_copy(ia, lax.rem(ia + d, n_atom)).wait_send()
        return 0

    lax.fori_loop(1, n_atom, drain_atom, 0)


def solution(mesh):
    n_atom, n_ka = mesh.shape["atom"], mesh.shape["ka"]

    def body(positions, features, species, miller, species_table, filter_weight, norm_gain, up_weight, down_weight):
        channels, atoms = features.shape
        local = atoms // n_ka
        n_vectors = miller.shape[1] * n_ka
        scaling = 1.0 / math.sqrt(atoms * n_atom * n_vectors)
        vmem = pl.BlockSpec(memory_space=pltpu.VMEM)
        smem = pl.BlockSpec(memory_space=pltpu.SMEM)
        return pl.pallas_call(
            functools.partial(body_kernel, (n_atom, n_ka, atoms, scaling)),
            out_shape=jax.ShapeDtypeStruct((channels, local), BF16),
            in_specs=[vmem, pl.BlockSpec(memory_space=pl.ANY), vmem, vmem, smem, smem, vmem, vmem, vmem],
            out_specs=vmem,
            scratch_shapes=[
                pltpu.VMEM((8, atoms), BF16),
                pltpu.VMEM((channels, local), BF16),
                pltpu.VMEM((XYR, atoms), BF16),
                pltpu.VMEM((16, atoms), F32),
                pltpu.VMEM((LW, 128), F32),
                pltpu.VMEM((48, LW), BF16),
                pltpu.VMEM((n_atom, 48, LW), BF16),
                pltpu.VMEM((n_ka, 8, 128), F32),
                pltpu.VMEM((XYR, 128), F32),
                pltpu.VMEM((LW, 128), F32),
                pltpu.VMEM((48, LW), BF16),
                pltpu.VMEM((n_ka, 8, 128), BF16),
                pltpu.VMEM((n_ka, 8, 128), BF16),
                pltpu.VMEM((n_ka * 8, 128), F32),
                pltpu.SemaphoreType.DMA((2,)),
                pltpu.SemaphoreType.DMA((n_ka,)),
                pltpu.SemaphoreType.DMA((n_ka,)),
                pltpu.SemaphoreType.DMA((n_atom,)),
                pltpu.SemaphoreType.DMA((n_atom,)),
                pltpu.SemaphoreType.DMA((n_ka,)),
                pltpu.SemaphoreType.DMA((n_ka,)),
            ],
            compiler_params=pltpu.CompilerParams(
                collective_id=0, has_side_effects=True, vmem_limit_bytes=60 * 1024 * 1024
            ),
            name="ewald",
        )(
            positions,
            features,
            species.reshape(1, atoms),
            miller,
            species_table,
            filter_weight,
            norm_gain.reshape(1, channels),
            up_weight,
            down_weight,
        )

    in_specs = (P(None, "atom"), P(None, "atom"), P("atom"), P(None, "ka"), P(), P(), P(), P(), P())
    out_specs = P(None, ("atom", "ka"))
    return jax.shard_map(body, mesh=mesh, in_specs=in_specs, out_specs=out_specs, check_vma=False)
```

```python
import functools
import math

import jax
import jax.numpy as jnp
from jax import lax
from jax.experimental import pallas as pl
from jax.experimental.pallas import tpu as pltpu
from jax.sharding import PartitionSpec as P

MESH = pl.DeviceIdType.MESH
F32, BF16 = jnp.float32, jnp.bfloat16
NRBF = 16
NSPEC = 8
MAXM = 8
XYR = 304
LW = 384
CHUNK = 512
K_CUTOFF = 14.0

def _fit():
    import numpy as np

    n = 400
    u = 0.125 + 0.125 * np.cos(np.pi * (np.arange(n) + 0.5) / n)
    r = np.sqrt(u)
    c = np.polynomial.chebyshev.Chebyshev.fit(u, np.cos(2 * np.pi * r), 4, domain=[0, 0.25])
    s = np.polynomial.chebyshev.Chebyshev.fit(u, np.sin(2 * np.pi * r) / r, 4, domain=[0, 0.25])
    return (
        [float(v) for v in c.convert(kind=np.polynomial.Polynomial).coef],
        [float(v) for v in s.convert(kind=np.polynomial.Polynomial).coef],
    )


COS_COEF, SIN_COEF = _fit()


def poly(u, coef):
    acc = jnp.full_like(u, coef[-1])
    for c in coef[-2::-1]:
        acc = acc * u + c
    return acc


def harmonics(row, orders):
    t = row * orders
    r = t - jnp.round(t)
    u = r * r
    return poly(u, COS_COEF), r * poly(u, SIN_COEF)


def iota(shape, axis):
    return lax.broadcasted_iota(jnp.int32, shape, axis)


def lane_orders(tile, shape, axis):
    lane = iota(shape, axis)
    low = lane & 7
    if tile < 2:
        ta = jnp.full(shape, tile, jnp.int32)
        p = (lane >> 4) + 1
        tb = (lane >> 3) & 1
        q = low + 1
        return ta, p, tb, q, lane >= 0
    odd = (lane >> 3) & 1
    in_x, in_y = lane < 16, (lane >= 16) & (lane < 32)
    zero = jnp.zeros(shape, jnp.int32)
    ta = jnp.where(in_x, odd, zero)
    p = jnp.where(in_x, low + 1, zero)
    tb = jnp.where(in_y, odd, zero)
    q = jnp.where(in_y, low + 1, zero)
    return ta, p, tb, q, lane < 33


def swap8(x):
    lane = iota(x.shape, 1)
    return jnp.where((lane & 8) == 0, pltpu.roll(x, 120, 1), pltpu.roll(x, 8, 1))


def tiles_of(x):
    return [x[:, 128 * t : 128 * (t + 1)] for t in range(3)]


def partners(g):
    s = [swap8(t) for t in g]
    lane = iota(g[0].shape, 1)
    zero = jnp.zeros_like(g[0])
    la = [g[1], g[0], jnp.where(lane < 16, s[2], zero)]
    lb = [s[0], s[1], jnp.where((lane >= 16) & (lane < 32), s[2], zero)]
    return la, lb, [s[1], s[0], zero]


GROUP = 4


def body_kernel(
    sizes,
    pos_hbm,
    feat_hbm,
    species_hbm,
    miller_hbm,
    tab_hbm,
    fw_hbm,
    gain_hbm,
    up_hbm,
    down_hbm,
    out_ref,
    pos_ref,
    species_ref,
    miller_ref,
    tab_ref,
    fw_ref,
    gain_ref,
    up_ref,
    down_ref,
    feat_blk,
    feat_loc,
    xy,
    sz,
    zz,
    xrows,
    gacc,
    gsend,
    grecv,
    mil_all,
    hmat,
    msgs,
    mrecv,
    mflat,
    local_sem,
    mil_send,
    mil_recv,
    g_send,
    g_recv,
    m_send,
    m_recv,
):
    n_atom, n_ka, ny, nz, atoms, scaling = sizes
    ia, ik = lax.axis_index("atom"), lax.axis_index("ka")
    local = atoms // n_ka
    n_chunks = atoms // CHUNK
    n_vec = n_ka * 128

    barrier = pltpu.get_barrier_semaphore()

    def greet_ka(d, _):
        pl.semaphore_signal(barrier, inc=1, device_id=(ia, lax.rem(ik + d, n_ka)), device_id_type=MESH)
        return 0

    def greet_atom(d, _):
        pl.semaphore_signal(barrier, inc=1, device_id=(lax.rem(ia + d, n_atom), ik), device_id_type=MESH)
        return 0

    loads = []
    for i, (src, dst) in enumerate(
        [
            (pos_hbm, pos_ref),
            (species_hbm, species_ref),
            (feat_hbm.at[pl.ds(pl.multiple_of((ik // 4) * 8, 8), 8), :], feat_blk),
            (tab_hbm, tab_ref),
            (miller_hbm, miller_ref),
            (fw_hbm, fw_ref),
            (gain_hbm, gain_ref),
            (up_hbm, up_ref),
            (down_hbm, down_ref),
            (feat_hbm.at[:, pl.ds(pl.multiple_of(ik * local, local), local)], feat_loc),
        ]
    ):
        copy = pltpu.make_async_copy(src, dst, local_sem.at[i])
        copy.start()
        loads.append(copy)
    lax.fori_loop(1, n_ka, greet_ka, 0)
    lax.fori_loop(1, n_atom, greet_atom, 0)

    first = pl.ds(0, CHUNK)
    xy[:, first] = jnp.zeros((XYR, CHUNK), BF16)
    sz[:, first] = jnp.zeros((48, CHUNK), BF16)
    gacc[...] = jnp.zeros_like(gacc)

    sub = iota((8, CHUNK), 0)
    orders = (sub + 1).astype(F32)
    for copy in loads[:5]:
        copy.wait()
    mil_all[:, pl.ds(pl.multiple_of(ik * 128, 128), 128)] = jnp.concatenate(
        [miller_ref[...].astype(F32), jnp.zeros((5, 128), F32)], axis=0
    )
    column = iota((NSPEC, 64), 1)
    tabs = [
        jnp.broadcast_to(
            jnp.sum(jnp.where(column == 2 * ik + c, tab_ref[...], 0.0), axis=1, keepdims=True), (8, CHUNK)
        )
        for c in range(2)
    ]
    which = [sub == lax.rem(2 * ik, 8) + c for c in range(2)]

    def products(j):
        cols = pl.ds(pl.multiple_of(j * CHUNK, CHUNK), CHUNK)
        return lax.dot_general(
            sz[:, cols], xy[:, cols], (((1,), (1,)), ((), ())), preferred_element_type=F32
        )

    def gather_chunk(j, _):
        part = products(jnp.maximum(j - 1, 0))
        cols = pl.ds(pl.multiple_of(j * CHUNK, CHUNK), CHUNK)
        xc, xs = harmonics(jnp.broadcast_to(pos_ref[0:1, cols], (8, CHUNK)), orders)
        xrows[0:8, :] = xc
        xrows[8:16, :] = xs
        yc, ys = harmonics(jnp.broadcast_to(pos_ref[1:2, cols], (8, CHUNK)), orders)
        y16 = jnp.concatenate([yc, ys], axis=0).astype(BF16)
        zc, zs = harmonics(jnp.broadcast_to(pos_ref[2:3, cols], (8, CHUNK)), orders)
        zz[0:8, cols] = zc
        zz[8:16, cols] = zs
        z16 = jnp.concatenate([zc, zs], axis=0).astype(BF16)
        for a in range(16):
            xa = jnp.broadcast_to(xrows[a : a + 1, :], (8, CHUNK))
            xy[16 * a : 16 * a + 16, cols] = jnp.concatenate([xa, xa], axis=0).astype(BF16) * y16
        xy[256:272, cols] = jnp.concatenate([xc, xs], axis=0).astype(BF16)
        xy[272:288, cols] = y16
        one = jnp.where(sub == 0, 1.0, 0.0)
        xy[288:304, cols] = jnp.concatenate([one, jnp.zeros_like(one)], axis=0).astype(BF16)
        fb = feat_blk[:, cols].astype(F32)
        hot = jnp.broadcast_to(species_ref[0:1, cols], (8, CHUNK)) == sub
        extra = jnp.zeros((8, CHUNK), F32)
        for c in range(2):
            s = jnp.where(which[c], fb, 0.0) + jnp.where(hot, tabs[c], 0.0)
            s = jnp.broadcast_to(jnp.sum(s, axis=0, keepdims=True), (8, CHUNK))
            extra = jnp.where(sub == c, s, extra)
            sz[16 * c : 16 * c + 16, cols] = jnp.concatenate([s, s], axis=0).astype(BF16) * z16
        sz[32:48, cols] = jnp.concatenate([extra, jnp.zeros_like(extra)], axis=0).astype(BF16)
        gacc[:, 0:XYR] += part
        return 0

    lax.fori_loop(0, n_chunks, gather_chunk, 0)
    gacc[:, 0:XYR] += products(n_chunks - 1)
    gsend[...] = gacc[0:40, :].astype(BF16)

    pl.semaphore_wait(barrier, n_ka - 1 + n_atom - 1)

    def g_copy(slot, to):
        return pltpu.make_async_remote_copy(
            src_ref=gsend,
            dst_ref=grecv.at[slot],
            send_sem=g_send,
            recv_sem=g_recv,
            device_id=(to, ik),
            device_id_type=MESH,
        )

    def send_g(d, _):
        g_copy(ia, lax.rem(ia + d, n_atom)).start()
        return 0

    def mil_copy(ref, dst, to):
        return pltpu.make_async_remote_copy(
            src_ref=ref, dst_ref=dst, send_sem=mil_send, recv_sem=mil_recv, device_id=(ia, to), device_id_type=MESH
        )

    own = mil_all.at[:, pl.ds(pl.multiple_of(ik * 128, 128), 128)]

    def farther(k, n):
        return n // 2 + (1 - 2 * lax.rem(k, 2)) * ((k + 1) // 2)

    def partner(i):
        dz, dy = farther(i // ny, nz), farther(lax.rem(i, ny), ny)
        y, z = lax.rem(ik // nz + dy, ny), lax.rem(lax.rem(ik, nz) + dz, nz)
        return y * nz + z

    def send_miller(i, _):
        mil_copy(own, own, partner(i)).start()
        return 0

    lax.fori_loop(0, n_ka - 1, send_miller, 0)
    lax.fori_loop(1, n_atom, send_g, 0)

    for copy in loads[5:]:
        copy.wait()
    sub1 = iota((8, 128), 0)
    r8 = (sub1 + 1).astype(F32)
    column = iota((NRBF, 64), 1)
    weights = [
        jnp.sum(jnp.where(column == 2 * ik + c, fw_ref[...], 0.0), axis=1, keepdims=True) * scaling
        for c in range(2)
    ]
    signs, radials, radials0 = [], [], []
    for t in range(3):
        ta, p, tb, q, _ = lane_orders(t, (8, 128), 1)
        signs.append((ta, tb))
        pq = (p * p + q * q).astype(F32)
        per_channel = []
        for mag in (jnp.sqrt(pq + r8 * r8), jnp.sqrt(pq)):
            acc = [jnp.zeros((8, 128), F32) for _ in range(2)]
            for b in range(NRBF):
                z = (mag - b * (K_CUTOFF / (NRBF - 1))) * (NRBF / K_CUTOFF)
                e = jnp.exp(-(z * z))
                for c in range(2):
                    acc[c] = acc[c] + weights[c][b : b + 1, :] * e
            per_channel.append(acc)
        radials.append(per_channel[0])
        radials0.append(jnp.where(sub1 == 0, per_channel[1][0], per_channel[1][1]))

    expand = []
    row = iota((96, 128), 0)
    for t in range(3):
        _, p, _, q, used = lane_orders(t, (96, 128), 1)
        expand.append(jnp.where(used & (row == p * 9 + q), 1.0, 0.0))
    expand = jnp.concatenate(expand, axis=1).astype(BF16)

    mil_copy(mil_all.at[:, 0 : n_vec - 128], mil_all.at[:, 0 : n_vec - 128], ik).wait_recv()
    codes = iota((96, CHUNK), 0).astype(F32)
    counts = jnp.zeros((48, 96), F32)
    for j in range(n_vec // CHUNK):
        m = mil_all[:, CHUNK * j : CHUNK * (j + 1)]
        mx, my, mz = [jnp.broadcast_to(m[i : i + 1, :], (8, CHUNK)) for i in range(3)]
        gx, gy, gz = [jnp.where(v < 0, -1.0, 1.0) for v in (mx, my, mz)]
        code = jnp.abs(mx) * 9.0 + jnp.abs(my)
        hot_xy = jnp.where(codes == jnp.broadcast_to(code[0:1, :], (96, CHUNK)), 1.0, 0.0).astype(BF16)
        az = jnp.abs(mz)
        hz = jnp.where(az == orders, 1.0, 0.0)
        h0 = jnp.where((az == 0.0) & (sub < 2), 1.0, 0.0)
        wr = jnp.concatenate(
            [hz, hz * (gy * gz), hz * (gx * gz), hz * (gx * gy), h0, h0 * (gx * gy)], axis=0
        ).astype(BF16)
        counts = counts + lax.dot_general(
            wr, hot_xy, (((1,), (1,)), ((), ())), preferred_element_type=F32
        )
    high = jnp.floor(counts * (1.0 / 256.0))
    low = counts - 256.0 * high
    wt = 256.0 * jnp.dot(high.astype(BF16), expand, preferred_element_type=F32) + jnp.dot(
        low.astype(BF16), expand, preferred_element_type=F32
    )
    w_plain, w_yz, w_xz, w_xy, w_plain0, w_xy0 = [
        tiles_of(wt[8 * i : 8 * i + 8, :]) for i in range(6)
    ]

    pltpu.make_async_remote_copy(
        src_ref=grecv.at[0 : n_atom - 1],
        dst_ref=grecv.at[0 : n_atom - 1],
        send_sem=g_send,
        recv_sem=g_recv,
        device_id=(ia, ik),
        device_id_type=MESH,
    ).wait_recv()
    grecv[ia] = gsend[...]
    g = grecv[0].astype(F32)
    for i in range(1, n_atom):
        g = g + grecv[i].astype(F32)

    rows = []
    for c in range(2):
        gz = [tiles_of(g[16 * c + 8 * tz : 16 * c + 8 * tz + 8, :]) for tz in range(2)]
        swapped = [partners(v) for v in gz]
        for tz in range(2):
            la, lb, _ = swapped[1 - tz]
            _, _, lab = swapped[tz]
            out = []
            for t in range(3):
                ta, tb = signs[t]
                u = jnp.where(tb == tz, -lb[t], lb[t]) * w_yz[t]
                v = jnp.where(ta == tz, -la[t], la[t]) * w_xz[t]
                w = jnp.where(ta == tb, -lab[t], lab[t]) * w_xy[t]
                out.append((gz[tz][t] * w_plain[t] + u + v + w) * radials[t][c])
            rows.append(jnp.concatenate(out, axis=1))
    g0 = tiles_of(g[32:40, :])
    _, _, lab = partners(g0)
    out = []
    for t in range(3):
        ta, tb = signs[t]
        w = jnp.where(ta == tb, -lab[t], lab[t]) * w_xy0[t]
        out.append((g0[t] * w_plain0[t] + w) * radials0[t])
    rows.append(jnp.concatenate(out, axis=1))
    rows.append(jnp.zeros((8, LW), F32))
    hmat[...] = jnp.concatenate(rows, axis=0).astype(BF16)

    def m_copy(slot, to):
        return pltpu.make_async_remote_copy(
            src_ref=msgs.at[to],
            dst_ref=mrecv.at[slot],
            send_sem=m_send,
            recv_sem=m_recv,
            device_id=(ia, to),
            device_id_type=MESH,
        )

    def message_of(d, cols):
        zc, zs = zz[0:8, cols], zz[8:16, cols]
        parts = []
        for c in range(2):
            s = d[16 * c : 16 * c + 8, :] * zc + d[16 * c + 8 : 16 * c + 16, :] * zs
            s = s + jnp.where(sub == c, d[32:40, :], 0.0)
            s = jnp.sum(s, axis=0, keepdims=True)
            parts += [s[:, 128 * i : 128 * (i + 1)] for i in range(CHUNK // 128)]
        return jnp.concatenate(parts, axis=0).astype(BF16)

    def send_messages(i, _):
        to = [partner(GROUP * i + k) for k in range(GROUP)]
        cols = [pl.ds(pl.multiple_of(j * CHUNK, CHUNK), CHUNK) for j in to]
        ds = [jnp.dot(hmat[:, 0:XYR], xy[:, c], preferred_element_type=F32) for c in cols]
        for k in range(GROUP):
            msgs[to[k]] = message_of(ds[k], cols[k])
        for k in range(GROUP):
            @pl.when(to[k] != ik)
            def _():
                m_copy(ik, to[k]).start()
        return 0

    lax.fori_loop(0, n_ka // GROUP, send_messages, 0)
    mrecv[ik] = msgs[ik]
    eye = iota((64, 64), 0) == iota((64, 64), 1)
    gain = jnp.sum(jnp.where(eye, jnp.broadcast_to(gain_ref[...], (64, 64)), 0.0), axis=1, keepdims=True)

    def all_messages():
        return pltpu.make_async_remote_copy(
            src_ref=mrecv.at[0 : n_ka - 1],
            dst_ref=mrecv.at[0 : n_ka - 1],
            send_sem=m_send,
            recv_sem=m_recv,
            device_id=(ia, ik),
            device_id_type=MESH,
        )

    all_messages().wait_recv()

    mflat[...] = mrecv[...].astype(F32).reshape(mflat.shape)
    message = jnp.concatenate(
        [mflat[pl.ds(i, 64, stride=4), :] for i in range(local // 128)], axis=1
    )
    mean_sq = jnp.sum(message * message, axis=0, keepdims=True) * (1.0 / 64.0)
    normed = (message * lax.rsqrt(mean_sq + 1e-06) * gain).astype(BF16)
    hidden = lax.dot_general(up_ref[...], normed, (((0,), (0,)), ((), ())), preferred_element_type=F32)
    hidden = (hidden / (1.0 + jnp.exp(-hidden))).astype(BF16)
    update = jnp.dot(down_ref[...], hidden, preferred_element_type=F32)
    out_ref[...] = (feat_loc[...].astype(F32) + update).astype(BF16)

    mil_copy(mil_all.at[:, 0 : n_vec - 128], mil_all.at[:, 0 : n_vec - 128], ik).wait_send()
    all_messages().wait_send()
    pltpu.make_async_remote_copy(
        src_ref=grecv.at[0 : n_atom - 1],
        dst_ref=grecv.at[0 : n_atom - 1],
        send_sem=g_send,
        recv_sem=g_recv,
        device_id=(ia, ik),
        device_id_type=MESH,
    ).wait_send()


def solution(mesh):
    n_atom, n_ka = mesh.shape["atom"], mesh.shape["ka"]
    ny, nz = 4, n_ka // 4

    def body(positions, features, species, miller, species_table, filter_weight, norm_gain, up_weight, down_weight):
        channels, atoms = features.shape
        local = atoms // n_ka
        n_vectors = miller.shape[1] * n_ka
        hid = up_weight.shape[0]
        scaling = 1.0 / math.sqrt(atoms * n_atom * n_vectors)
        any_space = pl.BlockSpec(memory_space=pl.ANY)
        return pl.pallas_call(
            functools.partial(body_kernel, (n_atom, n_ka, ny, nz, atoms, scaling)),
            out_shape=jax.ShapeDtypeStruct((channels, local), BF16),
            in_specs=[any_space] * 9,
            out_specs=pl.BlockSpec(memory_space=pltpu.VMEM),
            scratch_shapes=[
                pltpu.VMEM((3, atoms), F32),
                pltpu.VMEM((1, atoms), jnp.int32),
                pltpu.VMEM((3, 128), jnp.int32),
                pltpu.VMEM((NSPEC, channels), F32),
                pltpu.VMEM((NRBF, channels), F32),
                pltpu.VMEM((1, channels), F32),
                pltpu.VMEM((channels, hid), BF16),
                pltpu.VMEM((channels, hid), BF16),
                pltpu.VMEM((8, atoms), BF16),
                pltpu.VMEM((channels, local), BF16),
                pltpu.VMEM((XYR, atoms), BF16),
                pltpu.VMEM((48, atoms), BF16),
                pltpu.VMEM((16, atoms), F32),
                pltpu.VMEM((16, CHUNK), F32),
                pltpu.VMEM((48, LW), F32),
                pltpu.VMEM((40, LW), BF16),
                pltpu.VMEM((n_atom, 40, LW), BF16),
                pltpu.VMEM((8, n_vectors), F32),
                pltpu.VMEM((48, LW), BF16),
                pltpu.VMEM((n_ka, 8, 128), BF16),
                pltpu.VMEM((n_ka, 8, 128), BF16),
                pltpu.VMEM((n_ka * 8, 128), F32),
                pltpu.SemaphoreType.DMA((10,)),
                pltpu.SemaphoreType.DMA,
                pltpu.SemaphoreType.DMA,
                pltpu.SemaphoreType.DMA,
                pltpu.SemaphoreType.DMA,
                pltpu.SemaphoreType.DMA,
                pltpu.SemaphoreType.DMA,
            ],
            compiler_params=pltpu.CompilerParams(
                collective_id=0, has_side_effects=True, vmem_limit_bytes=24 * 1024 * 1024
            ),
            name="ewald",
        )(
            positions,
            features,
            species.reshape(1, atoms),
            miller,
            species_table.T,
            filter_weight.T,
            norm_gain.reshape(1, channels),
            up_weight.T,
            down_weight,
        )

    in_specs = (P(None, "atom"), P(None, "atom"), P("atom"), P(None, "ka"), P(), P(), P(), P(), P())
    out_specs = P(None, ("atom", "ka"))
    return jax.shard_map(body, mesh=mesh, in_specs=in_specs, out_specs=out_specs, check_vma=False)
```

```python
import functools
import math

import jax
import jax.numpy as jnp
from jax import lax
from jax.experimental import pallas as pl
from jax.experimental.pallas import tpu as pltpu
from jax.sharding import PartitionSpec as P

MESH = pl.DeviceIdType.MESH
F32, BF16 = jnp.float32, jnp.bfloat16
NRBF = 16
NSPEC = 8
MAXM = 8
XYR = 304
LW = 384
CHUNK = 512
K_CUTOFF = 14.0

def _fit():
    import numpy as np

    n = 400
    u = 0.125 + 0.125 * np.cos(np.pi * (np.arange(n) + 0.5) / n)
    r = np.sqrt(u)
    c = np.polynomial.chebyshev.Chebyshev.fit(u, np.cos(2 * np.pi * r), 4, domain=[0, 0.25])
    s = np.polynomial.chebyshev.Chebyshev.fit(u, np.sin(2 * np.pi * r) / r, 4, domain=[0, 0.25])
    return (
        [float(v) for v in c.convert(kind=np.polynomial.Polynomial).coef],
        [float(v) for v in s.convert(kind=np.polynomial.Polynomial).coef],
    )


COS_COEF, SIN_COEF = _fit()


def poly(u, coef):
    acc = jnp.full_like(u, coef[-1])
    for c in coef[-2::-1]:
        acc = acc * u + c
    return acc


def harmonics(row, orders):
    t = row * orders
    r = t - jnp.round(t)
    u = r * r
    return poly(u, COS_COEF), r * poly(u, SIN_COEF)


def iota(shape, axis):
    return lax.broadcasted_iota(jnp.int32, shape, axis)


def lane_orders(tile, shape, axis):
    lane = iota(shape, axis)
    low = lane & 7
    if tile < 2:
        ta = jnp.full(shape, tile, jnp.int32)
        p = (lane >> 4) + 1
        tb = (lane >> 3) & 1
        q = low + 1
        return ta, p, tb, q, lane >= 0
    odd = (lane >> 3) & 1
    in_x, in_y = lane < 16, (lane >= 16) & (lane < 32)
    zero = jnp.zeros(shape, jnp.int32)
    ta = jnp.where(in_x, odd, zero)
    p = jnp.where(in_x, low + 1, zero)
    tb = jnp.where(in_y, odd, zero)
    q = jnp.where(in_y, low + 1, zero)
    return ta, p, tb, q, lane < 33


def swap8(x):
    lane = iota(x.shape, 1)
    return jnp.where((lane & 8) == 0, pltpu.roll(x, 120, 1), pltpu.roll(x, 8, 1))


def tiles_of(x):
    return [x[:, 128 * t : 128 * (t + 1)] for t in range(3)]


def partners(g):
    s = [swap8(t) for t in g]
    lane = iota(g[0].shape, 1)
    zero = jnp.zeros_like(g[0])
    la = [g[1], g[0], jnp.where(lane < 16, s[2], zero)]
    lb = [s[0], s[1], jnp.where((lane >= 16) & (lane < 32), s[2], zero)]
    return la, lb, [s[1], s[0], zero]


GROUP = 4


def body_kernel(
    sizes,
    pos_hbm,
    feat_hbm,
    species_hbm,
    miller_hbm,
    tab_hbm,
    fw_hbm,
    gain_hbm,
    up_hbm,
    down_hbm,
    out_ref,
    pos_ref,
    species_ref,
    miller_ref,
    tab_ref,
    fw_ref,
    gain_ref,
    up_ref,
    down_ref,
    feat_blk,
    feat_loc,
    xy,
    sz,
    zz,
    xrows,
    gacc,
    gsend,
    grecv,
    mil_all,
    hmat,
    msgs,
    mrecv,
    mflat,
    local_sem,
    mil_send,
    mil_recv,
    g_send,
    g_recv,
    m_send,
    m_recv,
):
    n_atom, n_ka, ny, nz, atoms, scaling = sizes
    ia, ik = lax.axis_index("atom"), lax.axis_index("ka")
    local = atoms // n_ka
    n_chunks = atoms // CHUNK
    n_vec = n_ka * 128

    barrier = pltpu.get_barrier_semaphore()

    def greet_ka(d, _):
        pl.semaphore_signal(barrier, inc=1, device_id=(ia, lax.rem(ik + d, n_ka)), device_id_type=MESH)
        return 0

    def greet_atom(d, _):
        pl.semaphore_signal(barrier, inc=1, device_id=(lax.rem(ia + d, n_atom), ik), device_id_type=MESH)
        return 0

    loads = []
    for i, (src, dst) in enumerate(
        [
            (pos_hbm, pos_ref),
            (species_hbm, species_ref),
            (feat_hbm.at[pl.ds(pl.multiple_of((ik // 4) * 8, 8), 8), :], feat_blk),
            (tab_hbm, tab_ref),
            (miller_hbm, miller_ref),
            (fw_hbm, fw_ref),
            (gain_hbm, gain_ref),
            (up_hbm, up_ref),
            (down_hbm, down_ref),
            (feat_hbm.at[:, pl.ds(pl.multiple_of(ik * local, local), local)], feat_loc),
        ]
    ):
        copy = pltpu.make_async_copy(src, dst, local_sem.at[i])
        copy.start()
        loads.append(copy)
    lax.fori_loop(1, n_ka, greet_ka, 0)
    lax.fori_loop(1, n_atom, greet_atom, 0)

    first = pl.ds(0, CHUNK)
    xy[:, first] = jnp.zeros((XYR, CHUNK), BF16)
    sz[:, first] = jnp.zeros((48, CHUNK), BF16)
    gacc[...] = jnp.zeros_like(gacc)

    sub = iota((8, CHUNK), 0)
    orders = (sub + 1).astype(F32)
    for copy in loads[:5]:
        copy.wait()
    mil_all[:, pl.ds(pl.multiple_of(ik * 128, 128), 128)] = jnp.concatenate(
        [miller_ref[...].astype(F32), jnp.zeros((5, 128), F32)], axis=0
    )
    column = iota((NSPEC, 64), 1)
    tabs = [
        jnp.broadcast_to(
            jnp.sum(jnp.where(column == 2 * ik + c, tab_ref[...], 0.0), axis=1, keepdims=True), (8, CHUNK)
        )
        for c in range(2)
    ]
    which = [sub == lax.rem(2 * ik, 8) + c for c in range(2)]

    def products(j):
        cols = pl.ds(pl.multiple_of(j * CHUNK, CHUNK), CHUNK)
        return lax.dot_general(
            sz[:, cols], xy[:, cols], (((1,), (1,)), ((), ())), preferred_element_type=F32
        )

    def gather_chunk(j, _):
        part = products(jnp.maximum(j - 1, 0))
        cols = pl.ds(pl.multiple_of(j * CHUNK, CHUNK), CHUNK)
        xc, xs = harmonics(jnp.broadcast_to(pos_ref[0:1, cols], (8, CHUNK)), orders)
        xrows[0:8, :] = xc
        xrows[8:16, :] = xs
        yc, ys = harmonics(jnp.broadcast_to(pos_ref[1:2, cols], (8, CHUNK)), orders)
        y16 = jnp.concatenate([yc, ys], axis=0).astype(BF16)
        zc, zs = harmonics(jnp.broadcast_to(pos_ref[2:3, cols], (8, CHUNK)), orders)
        zz[0:8, cols] = zc
        zz[8:16, cols] = zs
        z16 = jnp.concatenate([zc, zs], axis=0).astype(BF16)
        for a in range(16):
            xa = jnp.broadcast_to(xrows[a : a + 1, :], (8, CHUNK))
            xy[16 * a : 16 * a + 16, cols] = jnp.concatenate([xa, xa], axis=0).astype(BF16) * y16
        xy[256:272, cols] = jnp.concatenate([xc, xs], axis=0).astype(BF16)
        xy[272:288, cols] = y16
        one = jnp.where(sub == 0, 1.0, 0.0)
        xy[288:304, cols] = jnp.concatenate([one, jnp.zeros_like(one)], axis=0).astype(BF16)
        fb = feat_blk[:, cols].astype(F32)
        hot = jnp.broadcast_to(species_ref[0:1, cols], (8, CHUNK)) == sub
        extra = jnp.zeros((8, CHUNK), F32)
        for c in range(2):
            s = jnp.where(which[c], fb, 0.0) + jnp.where(hot, tabs[c], 0.0)
            s = jnp.broadcast_to(jnp.sum(s, axis=0, keepdims=True), (8, CHUNK))
            extra = jnp.where(sub == c, s, extra)
            sz[16 * c : 16 * c + 16, cols] = jnp.concatenate([s, s], axis=0).astype(BF16) * z16
        sz[32:48, cols] = jnp.concatenate([extra, jnp.zeros_like(extra)], axis=0).astype(BF16)
        gacc[:, 0:XYR] += part
        return 0

    lax.fori_loop(0, n_chunks, gather_chunk, 0)
    gacc[:, 0:XYR] += products(n_chunks - 1)
    gsend[...] = gacc[0:40, :].astype(BF16)

    pl.semaphore_wait(barrier, n_ka - 1 + n_atom - 1)

    def g_copy(slot, to):
        return pltpu.make_async_remote_copy(
            src_ref=gsend,
            dst_ref=grecv.at[slot],
            send_sem=g_send,
            recv_sem=g_recv,
            device_id=(to, ik),
            device_id_type=MESH,
        )

    def send_g(d, _):
        g_copy(ia, lax.rem(ia + d, n_atom)).start()
        return 0

    def mil_copy(ref, dst, to):
        return pltpu.make_async_remote_copy(
            src_ref=ref, dst_ref=dst, send_sem=mil_send, recv_sem=mil_recv, device_id=(ia, to), device_id_type=MESH
        )

    own = mil_all.at[:, pl.ds(pl.multiple_of(ik * 128, 128), 128)]

    def farther(k, n):
        return n // 2 + (1 - 2 * lax.rem(k, 2)) * ((k + 1) // 2)

    def partner(i):
        dz, dy = farther(i // ny, nz), farther(lax.rem(i, ny), ny)
        y, z = lax.rem(ik // nz + dy, ny), lax.rem(lax.rem(ik, nz) + dz, nz)
        return y * nz + z

    def send_miller(i, _):
        mil_copy(own, own, partner(i)).start()
        return 0

    lax.fori_loop(0, n_ka - 1, send_miller, 0)
    lax.fori_loop(1, n_atom, send_g, 0)

    for copy in loads[5:]:
        copy.wait()
    sub1 = iota((8, 128), 0)
    r8 = (sub1 + 1).astype(F32)
    column = iota((NRBF, 64), 1)
    weights = [
        jnp.sum(jnp.where(column == 2 * ik + c, fw_ref[...], 0.0), axis=1, keepdims=True) * scaling
        for c in range(2)
    ]
    signs, radials, radials0 = [], [], []
    for t in range(3):
        ta, p, tb, q, _ = lane_orders(t, (8, 128), 1)
        signs.append((ta, tb))
        pq = (p * p + q * q).astype(F32)
        per_channel = []
        for mag in (jnp.sqrt(pq + r8 * r8), jnp.sqrt(pq)):
            acc = [jnp.zeros((8, 128), F32) for _ in range(2)]
            for b in range(NRBF):
                z = (mag - b * (K_CUTOFF / (NRBF - 1))) * (NRBF / K_CUTOFF)
                e = jnp.exp(-(z * z))
                for c in range(2):
                    acc[c] = acc[c] + weights[c][b : b + 1, :] * e
            per_channel.append(acc)
        radials.append(per_channel[0])
        radials0.append(jnp.where(sub1 == 0, per_channel[1][0], per_channel[1][1]))

    expand = []
    row = iota((96, 128), 0)
    for t in range(3):
        _, p, _, q, used = lane_orders(t, (96, 128), 1)
        expand.append(jnp.where(used & (row == p * 9 + q), 1.0, 0.0))
    expand = jnp.concatenate(expand, axis=1).astype(BF16)

    mil_copy(mil_all.at[:, 0 : n_vec - 128], mil_all.at[:, 0 : n_vec - 128], ik).wait_recv()
    codes = iota((96, CHUNK), 0).astype(F32)
    counts = jnp.zeros((48, 96), F32)
    for j in range(n_vec // CHUNK):
        m = mil_all[:, CHUNK * j : CHUNK * (j + 1)]
        mx, my, mz = [jnp.broadcast_to(m[i : i + 1, :], (8, CHUNK)) for i in range(3)]
        gx, gy, gz = [jnp.where(v < 0, -1.0, 1.0) for v in (mx, my, mz)]
        code = jnp.abs(mx) * 9.0 + jnp.abs(my)
        hot_xy = jnp.where(codes == jnp.broadcast_to(code[0:1, :], (96, CHUNK)), 1.0, 0.0).astype(BF16)
        az = jnp.abs(mz)
        hz = jnp.where(az == orders, 1.0, 0.0)
        h0 = jnp.where((az == 0.0) & (sub < 2), 1.0, 0.0)
        wr = jnp.concatenate(
            [hz, hz * (gy * gz), hz * (gx * gz), hz * (gx * gy), h0, h0 * (gx * gy)], axis=0
        ).astype(BF16)
        counts = counts + lax.dot_general(
            wr, hot_xy, (((1,), (1,)), ((), ())), preferred_element_type=F32
        )
    high = jnp.floor(counts * (1.0 / 256.0))
    low = counts - 256.0 * high
    wt = 256.0 * jnp.dot(high.astype(BF16), expand, preferred_element_type=F32) + jnp.dot(
        low.astype(BF16), expand, preferred_element_type=F32
    )
    w_plain, w_yz, w_xz, w_xy, w_plain0, w_xy0 = [
        tiles_of(wt[8 * i : 8 * i + 8, :]) for i in range(6)
    ]

    pltpu.make_async_remote_copy(
        src_ref=grecv.at[0 : n_atom - 1],
        dst_ref=grecv.at[0 : n_atom - 1],
        send_sem=g_send,
        recv_sem=g_recv,
        device_id=(ia, ik),
        device_id_type=MESH,
    ).wait_recv()
    grecv[ia] = gsend[...]
    g = grecv[0].astype(F32)
    for i in range(1, n_atom):
        g = g + grecv[i].astype(F32)

    rows = []
    for c in range(2):
        gz = [tiles_of(g[16 * c + 8 * tz : 16 * c + 8 * tz + 8, :]) for tz in range(2)]
        swapped = [partners(v) for v in gz]
        for tz in range(2):
            la, lb, _ = swapped[1 - tz]
            _, _, lab = swapped[tz]
            out = []
            for t in range(3):
                ta, tb = signs[t]
                u = jnp.where(tb == tz, -lb[t], lb[t]) * w_yz[t]
                v = jnp.where(ta == tz, -la[t], la[t]) * w_xz[t]
                w = jnp.where(ta == tb, -lab[t], lab[t]) * w_xy[t]
                out.append((gz[tz][t] * w_plain[t] + u + v + w) * radials[t][c])
            rows.append(jnp.concatenate(out, axis=1))
    g0 = tiles_of(g[32:40, :])
    _, _, lab = partners(g0)
    out = []
    for t in range(3):
        ta, tb = signs[t]
        w = jnp.where(ta == tb, -lab[t], lab[t]) * w_xy0[t]
        out.append((g0[t] * w_plain0[t] + w) * radials0[t])
    rows.append(jnp.concatenate(out, axis=1))
    rows.append(jnp.zeros((8, LW), F32))
    hmat[...] = jnp.concatenate(rows, axis=0).astype(BF16)

    def m_copy(slot, to):
        return pltpu.make_async_remote_copy(
            src_ref=msgs.at[to],
            dst_ref=mrecv.at[slot],
            send_sem=m_send,
            recv_sem=m_recv,
            device_id=(ia, to),
            device_id_type=MESH,
        )

    def message_of(d, cols):
        zc, zs = zz[0:8, cols], zz[8:16, cols]
        parts = []
        for c in range(2):
            s = d[16 * c : 16 * c + 8, :] * zc + d[16 * c + 8 : 16 * c + 16, :] * zs
            s = s + jnp.where(sub == c, d[32:40, :], 0.0)
            s = jnp.sum(s, axis=0, keepdims=True)
            parts += [s[:, 128 * i : 128 * (i + 1)] for i in range(CHUNK // 128)]
        return jnp.concatenate(parts, axis=0).astype(BF16)

    def send_messages(i, _):
        to = [partner(GROUP * i + k) for k in range(GROUP)]
        cols = [pl.ds(pl.multiple_of(j * CHUNK, CHUNK), CHUNK) for j in to]
        ds = [jnp.dot(hmat[:, 0:XYR], xy[:, c], preferred_element_type=F32) for c in cols]
        for k in range(GROUP):
            msgs[to[k]] = message_of(ds[k], cols[k])
        for k in range(GROUP):
            @pl.when(to[k] != ik)
            def _():
                m_copy(ik, to[k]).start()
        return 0

    lax.fori_loop(0, n_ka // GROUP, send_messages, 0)
    mrecv[ik] = msgs[ik]
    eye = iota((64, 64), 0) == iota((64, 64), 1)
    gain = jnp.sum(jnp.where(eye, jnp.broadcast_to(gain_ref[...], (64, 64)), 0.0), axis=1, keepdims=True)

    def all_messages():
        return pltpu.make_async_remote_copy(
            src_ref=mrecv.at[0 : n_ka - 1],
            dst_ref=mrecv.at[0 : n_ka - 1],
            send_sem=m_send,
            recv_sem=m_recv,
            device_id=(ia, ik),
            device_id_type=MESH,
        )

    all_messages().wait_recv()

    mflat[...] = mrecv[...].astype(F32).reshape(mflat.shape)
    message = jnp.concatenate(
        [mflat[pl.ds(i, 64, stride=4), :] for i in range(local // 128)], axis=1
    )
    mean_sq = jnp.sum(message * message, axis=0, keepdims=True) * (1.0 / 64.0)
    normed = (message * lax.rsqrt(mean_sq + 1e-06) * gain).astype(BF16)
    hidden = lax.dot_general(up_ref[...], normed, (((0,), (0,)), ((), ())), preferred_element_type=F32)
    hidden = (hidden / (1.0 + jnp.exp(-hidden))).astype(BF16)
    update = jnp.dot(down_ref[...], hidden, preferred_element_type=F32)
    out_ref[...] = (feat_loc[...].astype(F32) + update).astype(BF16)

    mil_copy(mil_all.at[:, 0 : n_vec - 128], mil_all.at[:, 0 : n_vec - 128], ik).wait_send()
    all_messages().wait_send()
    pltpu.make_async_remote_copy(
        src_ref=grecv.at[0 : n_atom - 1],
        dst_ref=grecv.at[0 : n_atom - 1],
        send_sem=g_send,
        recv_sem=g_recv,
        device_id=(ia, ik),
        device_id_type=MESH,
    ).wait_send()


def solution(mesh):
    n_atom, n_ka = mesh.shape["atom"], mesh.shape["ka"]
    ny, nz = 4, n_ka // 4

    def body(positions, features, species, miller, species_table, filter_weight, norm_gain, up_weight, down_weight):
        channels, atoms = features.shape
        local = atoms // n_ka
        n_vectors = miller.shape[1] * n_ka
        hid = up_weight.shape[0]
        scaling = 1.0 / math.sqrt(atoms * n_atom * n_vectors)
        any_space = pl.BlockSpec(memory_space=pltpu.HBM)
        return pl.pallas_call(
            functools.partial(body_kernel, (n_atom, n_ka, ny, nz, atoms, scaling)),
            out_shape=jax.ShapeDtypeStruct((channels, local), BF16),
            in_specs=[any_space] * 9,
            out_specs=pl.BlockSpec(memory_space=pltpu.VMEM),
            scratch_shapes=[
                pltpu.VMEM((3, atoms), F32),
                pltpu.VMEM((1, atoms), jnp.int32),
                pltpu.VMEM((3, 128), jnp.int32),
                pltpu.VMEM((NSPEC, channels), F32),
                pltpu.VMEM((NRBF, channels), F32),
                pltpu.VMEM((1, channels), F32),
                pltpu.VMEM((channels, hid), BF16),
                pltpu.VMEM((channels, hid), BF16),
                pltpu.VMEM((8, atoms), BF16),
                pltpu.VMEM((channels, local), BF16),
                pltpu.VMEM((XYR, atoms), BF16),
                pltpu.VMEM((48, atoms), BF16),
                pltpu.VMEM((16, atoms), F32),
                pltpu.VMEM((16, CHUNK), F32),
                pltpu.VMEM((48, LW), F32),
                pltpu.VMEM((40, LW), BF16),
                pltpu.VMEM((n_atom, 40, LW), BF16),
                pltpu.VMEM((8, n_vectors), F32),
                pltpu.VMEM((48, LW), BF16),
                pltpu.VMEM((n_ka, 8, 128), BF16),
                pltpu.VMEM((n_ka, 8, 128), BF16),
                pltpu.VMEM((n_ka * 8, 128), F32),
                pltpu.SemaphoreType.DMA((10,)),
                pltpu.SemaphoreType.DMA,
                pltpu.SemaphoreType.DMA,
                pltpu.SemaphoreType.DMA,
                pltpu.SemaphoreType.DMA,
                pltpu.SemaphoreType.DMA,
                pltpu.SemaphoreType.DMA,
            ],
            compiler_params=pltpu.CompilerParams(
                collective_id=0, has_side_effects=True, vmem_limit_bytes=24 * 1024 * 1024
            ),
            name="ewald",
        )(*[pltpu.with_memory_space_constraint(v, pltpu.HBM) for v in (
            positions,
            features,
            species.reshape(1, atoms),
            miller,
            species_table.T,
            filter_weight.T,
            norm_gain.reshape(1, channels),
            up_weight.T,
            down_weight,
        )])

    in_specs = (P(None, "atom"), P(None, "atom"), P("atom"), P(None, "ka"), P(), P(), P(), P(), P())
    out_specs = P(None, ("atom", "ka"))
    return jax.shard_map(body, mesh=mesh, in_specs=in_specs, out_specs=out_specs, check_vma=False)
```

```python
import functools
import math

import jax
import jax.numpy as jnp
from jax import lax
from jax.experimental import pallas as pl
from jax.experimental.pallas import tpu as pltpu
from jax.sharding import PartitionSpec as P

MESH = pl.DeviceIdType.MESH
F32, BF16 = jnp.float32, jnp.bfloat16
NRBF = 16
NSPEC = 8
MAXM = 8
LW = 128
SR = 112
GR = 104
CHUNK = 512
K_CUTOFF = 14.0

def _fit():
    import numpy as np

    n = 400
    u = 0.125 + 0.125 * np.cos(np.pi * (np.arange(n) + 0.5) / n)
    r = np.sqrt(u)
    c = np.polynomial.chebyshev.Chebyshev.fit(u, np.cos(2 * np.pi * r), 4, domain=[0, 0.25])
    s = np.polynomial.chebyshev.Chebyshev.fit(u, np.sin(2 * np.pi * r) / r, 4, domain=[0, 0.25])
    return (
        [float(v) for v in c.convert(kind=np.polynomial.Polynomial).coef],
        [float(v) for v in s.convert(kind=np.polynomial.Polynomial).coef],
    )


COS_COEF, SIN_COEF = _fit()


def poly(u, coef):
    acc = jnp.full_like(u, coef[-1])
    for c in coef[-2::-1]:
        acc = acc * u + c
    return acc


def harmonics(row, orders):
    t = row * orders
    r = t - jnp.round(t)
    u = r * r
    return poly(u, COS_COEF), r * poly(u, SIN_COEF)


def iota(shape, axis):
    return lax.broadcasted_iota(jnp.int32, shape, axis)


def lane_orders(shape, axis):
    lane = iota(shape, axis)
    main = lane < 112
    u = jnp.where(main, lane >> 4, lane - 112)
    tu = jnp.where((u >= 3) & (u < 6), 1, 0)
    a = jnp.where(u < 3, u + 1, jnp.where(u < 6, u - 2, 0))
    ty = jnp.where(main, (lane >> 3) & 1, 0)
    q = jnp.where(main, (lane & 7) + 1, 0)
    return tu, a, ty, q, lane < 119


def swap_y(x):
    lane = iota(x.shape, 1)
    s = jnp.where((lane & 8) == 0, pltpu.roll(x, 120, 1), pltpu.roll(x, 8, 1))
    return jnp.where(lane < 112, s, 0.0)


def swap_u(x):
    lane = iota(x.shape, 1)
    s = jnp.where(lane < 48, pltpu.roll(x, 80, 1), jnp.where(lane < 96, pltpu.roll(x, 48, 1), 0.0))
    s = jnp.where((lane >= 112) & (lane < 115), pltpu.roll(x, 125, 1), s)
    return jnp.where((lane >= 115) & (lane < 118), pltpu.roll(x, 3, 1), s)


def signed(same, w):
    return jnp.where(same, -w, w)


GROUP = 4


def body_kernel(
    sizes,
    pos_hbm,
    feat_hbm,
    species_hbm,
    miller_hbm,
    tab_hbm,
    fw_hbm,
    gain_hbm,
    up_hbm,
    down_hbm,
    out_ref,
    pos_ref,
    species_ref,
    miller_ref,
    tab_ref,
    fw_ref,
    gain_ref,
    up_ref,
    down_ref,
    feat_blk,
    feat_loc,
    yu,
    sz,
    zz,
    vb,
    vv,
    xrows,
    gacc,
    gsend,
    grecv,
    mil_all,
    hmat,
    msgs,
    mrecv,
    mflat,
    local_sem,
    mil_send,
    mil_recv,
    g_send,
    g_recv,
    m_send,
    m_recv,
):
    n_atom, n_ka, ny, nz, atoms, scaling = sizes
    ia, ik = lax.axis_index("atom"), lax.axis_index("ka")
    local = atoms // n_ka
    n_chunks = atoms // CHUNK
    n_vec = n_ka * 128

    barrier = pltpu.get_barrier_semaphore()

    def greet_ka(d, _):
        pl.semaphore_signal(barrier, inc=1, device_id=(ia, lax.rem(ik + d, n_ka)), device_id_type=MESH)
        return 0

    def greet_atom(d, _):
        pl.semaphore_signal(barrier, inc=1, device_id=(lax.rem(ia + d, n_atom), ik), device_id_type=MESH)
        return 0

    loads = []
    for i, (src, dst) in enumerate(
        [
            (pos_hbm, pos_ref),
            (species_hbm, species_ref),
            (feat_hbm.at[pl.ds(pl.multiple_of((ik // 4) * 8, 8), 8), :], feat_blk),
            (tab_hbm, tab_ref),
            (miller_hbm, miller_ref),
            (fw_hbm, fw_ref),
            (gain_hbm, gain_ref),
            (up_hbm, up_ref),
            (down_hbm, down_ref),
            (feat_hbm.at[:, pl.ds(pl.multiple_of(ik * local, local), local)], feat_loc),
        ]
    ):
        copy = pltpu.make_async_copy(src, dst, local_sem.at[i])
        copy.start()
        loads.append(copy)
    lax.fori_loop(1, n_ka, greet_ka, 0)
    lax.fori_loop(1, n_atom, greet_atom, 0)

    first = pl.ds(0, CHUNK)
    yu[:, first] = jnp.zeros((LW, CHUNK), BF16)
    sz[:, first] = jnp.zeros((SR, CHUNK), BF16)
    gacc[...] = jnp.zeros_like(gacc)

    sub = iota((8, CHUNK), 0)
    orders = (sub + 1).astype(F32)
    third = jnp.where(sub < 3, sub, sub - 3)
    x_orders = jnp.where(sub < 6, 3 * third + 3, 1).astype(F32)
    for copy in loads[:5]:
        copy.wait()
    mil_all[:, pl.ds(pl.multiple_of(ik * 128, 128), 128)] = jnp.concatenate(
        [miller_ref[...].astype(F32), jnp.zeros((5, 128), F32)], axis=0
    ).astype(BF16)
    column = iota((NSPEC, 64), 1)
    tabs = [
        jnp.broadcast_to(
            jnp.sum(jnp.where(column == 2 * ik + c, tab_ref[...], 0.0), axis=1, keepdims=True), (8, CHUNK)
        )
        for c in range(2)
    ]
    which = [sub == lax.rem(2 * ik, 8) + c for c in range(2)]

    def products(j):
        cols = pl.ds(pl.multiple_of(j * CHUNK, CHUNK), CHUNK)
        return lax.dot_general(
            sz[:, cols], yu[:, cols], (((1,), (1,)), ((), ())), preferred_element_type=F32
        )

    def row_of(i):
        return jnp.broadcast_to(xrows[i : i + 1, :], (8, CHUNK))

    def store(ref, r0, cols, upper, lower):
        ref[r0 : r0 + 16, cols] = jnp.concatenate([upper, lower], axis=0).astype(BF16)

    def gather_chunk(j, _):
        part = products(jnp.maximum(j - 1, 0))
        cols = pl.ds(pl.multiple_of(j * CHUNK, CHUNK), CHUNK)
        xc, xs = harmonics(jnp.broadcast_to(pos_ref[0:1, cols], (8, CHUNK)), x_orders)
        xrows[0:8, :] = xc
        xrows[8:16, :] = xs
        yc, ys = harmonics(jnp.broadcast_to(pos_ref[1:2, cols], (8, CHUNK)), orders)
        zc, zs = harmonics(jnp.broadcast_to(pos_ref[2:3, cols], (8, CHUNK)), orders)
        vc, vs = row_of(6), row_of(14)
        ones = jnp.where(third == 1, vc, jnp.where(third == 2, vs, 1.0))
        ones = jnp.where(sub < 6, ones, 0.0)
        zero = jnp.zeros((8, CHUNK), F32)
        zz[0:8, cols] = zc
        zz[8:16, cols] = zs
        vb[0:8, cols] = vc
        vb[8:16, cols] = vs
        vv[:, cols] = ones
        for i, r in enumerate((0, 1, 2, 11, 12, 13)):
            u = row_of(r)
            store(yu, 16 * i, cols, u * yc, u * ys)
        store(yu, 96, cols, yc, ys)
        store(
            yu, 112, cols, jnp.where(sub < 3, xc, jnp.where(sub < 6, xs, jnp.where(sub == 6, 1.0, 0.0))), zero
        )
        fb = feat_blk[:, cols].astype(F32)
        hot = jnp.broadcast_to(species_ref[0:1, cols], (8, CHUNK)) == sub
        sources = []
        for c in range(2):
            s = jnp.where(which[c], fb, 0.0) + jnp.where(hot, tabs[c], 0.0)
            s = jnp.broadcast_to(jnp.sum(s, axis=0, keepdims=True), (8, CHUNK))
            s = s.astype(BF16).astype(F32)
            sources.append(s)
            szc, szs = s * zc, s * zs
            store(sz, 48 * c, cols, szc, szs)
            store(sz, 48 * c + 16, cols, szc * vc, szs * vc)
            store(sz, 48 * c + 32, cols, szc * vs, szs * vs)
        store(sz, 96, cols, jnp.where(sub < 3, sources[0], sources[1]) * ones, zero)
        gacc[...] += part
        return 0

    lax.fori_loop(0, n_chunks, gather_chunk, 0)
    gacc[...] += products(n_chunks - 1)
    gsend[...] = gacc[0:GR, :].astype(BF16)

    pl.semaphore_wait(barrier, n_ka - 1 + n_atom - 1)

    def g_copy(slot, to):
        return pltpu.make_async_remote_copy(
            src_ref=gsend,
            dst_ref=grecv.at[slot],
            send_sem=g_send,
            recv_sem=g_recv,
            device_id=(to, ik),
            device_id_type=MESH,
        )

    def send_g(d, _):
        g_copy(ia, lax.rem(ia + d, n_atom)).start()
        return 0

    def mil_copy(ref, dst, to):
        return pltpu.make_async_remote_copy(
            src_ref=ref, dst_ref=dst, send_sem=mil_send, recv_sem=mil_recv, device_id=(ia, to), device_id_type=MESH
        )

    own = mil_all.at[:, pl.ds(pl.multiple_of(ik * 128, 128), 128)]

    def farther(k, n):
        return n // 2 + (1 - 2 * lax.rem(k, 2)) * ((k + 1) // 2)

    def partner(i):
        dz, dy = farther(i // ny, nz), farther(lax.rem(i, ny), ny)
        y, z = lax.rem(ik // nz + dy, ny), lax.rem(lax.rem(ik, nz) + dz, nz)
        return y * nz + z

    def send_miller(i, _):
        mil_copy(own, own, partner(i)).start()
        return 0

    lax.fori_loop(0, n_ka - 1, send_miller, 0)
    lax.fori_loop(1, n_atom, send_g, 0)

    for copy in loads[5:]:
        copy.wait()
    sub1 = iota((8, 128), 0)
    r8 = (sub1 + 1).astype(F32)
    column = iota((NRBF, 64), 1)
    weights = [
        jnp.sum(jnp.where(column == 2 * ik + c, fw_ref[...], 0.0), axis=1, keepdims=True) * scaling
        for c in range(2)
    ]
    tu, a, ty, q, _ = lane_orders((8, 128), 1)
    af, qq = a.astype(F32) * 3.0, (q * q).astype(F32)
    third1 = jnp.where(sub1 < 3, sub1, sub1 - 3)
    b_row = jnp.where((third1 > 0) & (sub1 < 6), 1.0, 0.0)
    tv_row = jnp.where(third1 == 2, 1, 0)

    def radial_of(m, r):
        mag = jnp.sqrt(m * m + qq + r * r)
        acc = [jnp.zeros((8, 128), F32) for _ in range(2)]
        for b in range(NRBF):
            z = (mag - b * (K_CUTOFF / (NRBF - 1))) * (NRBF / K_CUTOFF)
            e = jnp.exp(-(z * z))
            for c in range(2):
                acc[c] = acc[c] + weights[c][b : b + 1, :] * e
        return acc

    zero1 = jnp.zeros((8, 128), F32)
    rad_0 = radial_of(af, r8)
    rad_p, rad_m = radial_of(af + 1.0, r8), radial_of(af - 1.0, r8)
    single_p, single_m = [
        jnp.where(sub1 < 3, v[0], v[1]) for v in (radial_of(af + b_row, zero1), radial_of(af - b_row, zero1))
    ]

    mil_copy(mil_all.at[:, 0 : n_vec - 128], mil_all.at[:, 0 : n_vec - 128], ik).wait_recv()
    _, a_r, _, q_r, used = lane_orders((LW, CHUNK), 0)
    codes = jnp.where(used, a_r * 9 + q_r, -1).astype(F32)
    b_sub = jnp.where(third == 0, 0.0, 1.0)
    b_sub = jnp.where(sub < 6, b_sub, -1.0)
    counts = jnp.zeros((128, LW), F32)
    for j in range(n_vec // CHUNK):
        m = mil_all[:, CHUNK * j : CHUNK * (j + 1)].astype(F32)
        mx, my, mz = [jnp.broadcast_to(m[i : i + 1, :], (8, CHUNK)) for i in range(3)]
        ma = jnp.round(mx * (1.0 / 3.0))
        mb = mx - 3.0 * ma
        ga, gb, gy, gz = [jnp.where(v < 0, -1.0, 1.0) for v in (ma, mb, my, mz)]
        code = jnp.abs(ma) * 9.0 + jnp.abs(my)
        hot_uy = jnp.where(codes == jnp.broadcast_to(code[0:1, :], (LW, CHUNK)), 1.0, 0.0).astype(BF16)
        ab, ar, br, aq, bq, qr = ga * gb, ga * gz, gb * gz, ga * gy, gb * gy, gy * gz
        az, absb = jnp.abs(mz), jnp.abs(mb)
        hz = jnp.where(az == orders, 1.0, 0.0)
        h1 = hz * absb
        h0 = hz - h1
        hs = jnp.where((az == 0.0) & (absb == b_sub), 1.0, 0.0)
        wr = jnp.concatenate(
            [h1, h1 * ab, h1 * ar, h1 * br, h1 * aq, h1 * bq, h1 * qr, h1 * (ab * qr)]
            + [h0, h0 * aq, h0 * ar, h0 * qr]
            + [hs, hs * ab, hs * aq, hs * bq],
            axis=0,
        ).astype(BF16)
        counts = counts + lax.dot_general(
            wr, hot_uy, (((1,), (1,)), ((), ())), preferred_element_type=F32
        )
    w = [counts[8 * i : 8 * i + 8, :] for i in range(16)]

    pltpu.make_async_remote_copy(
        src_ref=grecv.at[0 : n_atom - 1],
        dst_ref=grecv.at[0 : n_atom - 1],
        send_sem=g_send,
        recv_sem=g_recv,
        device_id=(ia, ik),
        device_id_type=MESH,
    ).wait_recv()
    grecv[ia] = gsend[...]
    g = grecv[0].astype(F32)
    for i in range(1, n_atom):
        g = g + grecv[i].astype(F32)

    def mixed(plus, minus, plain, crossed):
        half_s, half_d = 0.5 * (plus + minus), 0.5 * (plus - minus)
        return half_s * plain + half_d * crossed, half_s * crossed + half_d * plain

    same_uy = tu == ty
    rows = []
    for c in range(2):
        gb = [[g[48 * c + 16 * v + 8 * t : 48 * c + 16 * v + 8 * t + 8, :] for t in range(2)] for v in range(3)]
        gu = [[swap_u(x) for x in pair] for pair in gb]
        gy = [[swap_y(x) for x in pair] for pair in gb]
        guy = [[swap_u(x) for x in pair] for pair in gy]
        for t in range(2):
            h = w[8] * gb[0][t] + signed(same_uy, w[9]) * guy[0][t]
            h = h + signed(tu == t, w[10]) * gu[0][1 - t] + signed(ty == t, w[11]) * gy[0][1 - t]
            rows.append(h * rad_0[c])
        c_0, c_ab = mixed(rad_p[c], rad_m[c], w[0], w[1])
        c_ar, c_br = mixed(rad_p[c], rad_m[c], w[2], w[3])
        c_aq, c_bq = mixed(rad_p[c], rad_m[c], w[4], w[5])
        c_qr, c_all = mixed(rad_p[c], rad_m[c], w[6], w[7])
        for v in (1, 2):
            tv, o = v - 1, 3 - v
            for t in range(2):
                h = c_0 * gb[v][t] + signed(same_uy, c_aq) * guy[v][t]
                h = h + signed(tu == t, c_ar) * gu[v][1 - t] + signed(ty == t, c_qr) * gy[v][1 - t]
                h = h + signed(tu == tv, c_ab) * gu[o][t] + signed(ty == tv, c_bq) * gy[o][t]
                h = h + (-c_br if tv == t else c_br) * gb[o][1 - t]
                odd = same_uy if (tv + t) % 2 == 1 else tu != ty
                rows.append(h + signed(odd, c_all) * guy[o][1 - t])
    g0 = g[96:104, :]
    over = jnp.where(third1 == 1, pltpu.roll(g0, 7, 0), pltpu.roll(g0, 1, 0))
    over = jnp.where(b_row > 0.0, over, 0.0)
    c_0, c_ab = mixed(single_p, single_m, w[12], w[13])
    c_aq, c_bq = mixed(single_p, single_m, w[14], w[15])
    h = c_0 * g0 + signed(same_uy, c_aq) * swap_u(swap_y(g0))
    h = h + signed(tu == tv_row, c_ab) * swap_u(over) + signed(ty == tv_row, c_bq) * swap_y(over)
    rows += [h, jnp.zeros((8, LW), F32)]
    hmat[...] = jnp.concatenate(rows, axis=0).astype(BF16)

    def m_copy(slot, to):
        return pltpu.make_async_remote_copy(
            src_ref=msgs.at[to],
            dst_ref=mrecv.at[slot],
            send_sem=m_send,
            recv_sem=m_recv,
            device_id=(ia, to),
            device_id_type=MESH,
        )

    def message_of(d, cols):
        zc, zs = zz[0:8, cols], zz[8:16, cols]
        vs = (None, vb[0:8, cols], vb[8:16, cols])
        single = d[96:104, :] * vv[:, cols]
        parts = []
        for c in range(2):
            s = jnp.where((sub < 3) == (c == 0), single, 0.0)
            for v in range(3):
                r = 48 * c + 16 * v
                e = d[r : r + 8, :] * zc + d[r + 8 : r + 16, :] * zs
                s = s + (e if v == 0 else e * vs[v])
            s = jnp.sum(s, axis=0, keepdims=True)
            parts += [s[:, 128 * i : 128 * (i + 1)] for i in range(CHUNK // 128)]
        return jnp.concatenate(parts, axis=0).astype(BF16)

    def send_messages(i, _):
        to = [partner(GROUP * i + k) for k in range(GROUP)]
        cols = [pl.ds(pl.multiple_of(j * CHUNK, CHUNK), CHUNK) for j in to]
        ds = [jnp.dot(hmat[...], yu[:, c], preferred_element_type=F32) for c in cols]
        for k in range(GROUP):
            msgs[to[k]] = message_of(ds[k], cols[k])
        for k in range(GROUP):
            @pl.when(to[k] != ik)
            def _():
                m_copy(ik, to[k]).start()
        return 0

    lax.fori_loop(0, n_ka // GROUP, send_messages, 0)
    mrecv[ik] = msgs[ik]
    eye = iota((64, 64), 0) == iota((64, 64), 1)
    gain = jnp.sum(jnp.where(eye, jnp.broadcast_to(gain_ref[...], (64, 64)), 0.0), axis=1, keepdims=True)

    def all_messages():
        return pltpu.make_async_remote_copy(
            src_ref=mrecv.at[0 : n_ka - 1],
            dst_ref=mrecv.at[0 : n_ka - 1],
            send_sem=m_send,
            recv_sem=m_recv,
            device_id=(ia, ik),
            device_id_type=MESH,
        )

    all_messages().wait_recv()

    mflat[...] = mrecv[...].astype(F32).reshape(mflat.shape)
    message = jnp.concatenate(
        [mflat[pl.ds(i, 64, stride=4), :] for i in range(local // 128)], axis=1
    )
    mean_sq = jnp.sum(message * message, axis=0, keepdims=True) * (1.0 / 64.0)
    normed = (message * lax.rsqrt(mean_sq + 1e-06) * gain).astype(BF16)
    hidden = lax.dot_general(up_ref[...], normed, (((0,), (0,)), ((), ())), preferred_element_type=F32)
    hidden = (hidden / (1.0 + jnp.exp(-hidden))).astype(BF16)
    update = jnp.dot(down_ref[...], hidden, preferred_element_type=F32)
    out_ref[...] = (feat_loc[...].astype(F32) + update).astype(BF16)

    mil_copy(mil_all.at[:, 0 : n_vec - 128], mil_all.at[:, 0 : n_vec - 128], ik).wait_send()
    all_messages().wait_send()
    pltpu.make_async_remote_copy(
        src_ref=grecv.at[0 : n_atom - 1],
        dst_ref=grecv.at[0 : n_atom - 1],
        send_sem=g_send,
        recv_sem=g_recv,
        device_id=(ia, ik),
        device_id_type=MESH,
    ).wait_send()


def solution(mesh):
    n_atom, n_ka = mesh.shape["atom"], mesh.shape["ka"]
    ny, nz = 4, n_ka // 4

    def body(positions, features, species, miller, species_table, filter_weight, norm_gain, up_weight, down_weight):
        channels, atoms = features.shape
        local = atoms // n_ka
        n_vectors = miller.shape[1] * n_ka
        hid = up_weight.shape[0]
        scaling = 1.0 / math.sqrt(atoms * n_atom * n_vectors)
        any_space = pl.BlockSpec(memory_space=pltpu.HBM)
        return pl.pallas_call(
            functools.partial(body_kernel, (n_atom, n_ka, ny, nz, atoms, scaling)),
            out_shape=jax.ShapeDtypeStruct((channels, local), BF16),
            in_specs=[any_space] * 9,
            out_specs=pl.BlockSpec(memory_space=pltpu.VMEM),
            scratch_shapes=[
                pltpu.VMEM((3, atoms), F32),
                pltpu.VMEM((1, atoms), jnp.int32),
                pltpu.VMEM((3, 128), jnp.int32),
                pltpu.VMEM((NSPEC, channels), F32),
                pltpu.VMEM((NRBF, channels), F32),
                pltpu.VMEM((1, channels), F32),
                pltpu.VMEM((channels, hid), BF16),
                pltpu.VMEM((channels, hid), BF16),
                pltpu.VMEM((8, atoms), BF16),
                pltpu.VMEM((channels, local), BF16),
                pltpu.VMEM((LW, atoms), BF16),
                pltpu.VMEM((SR, atoms), BF16),
                pltpu.VMEM((16, atoms), F32),
                pltpu.VMEM((16, atoms), F32),
                pltpu.VMEM((8, atoms), F32),
                pltpu.VMEM((16, CHUNK), F32),
                pltpu.VMEM((SR, LW), F32),
                pltpu.VMEM((GR, LW), BF16),
                pltpu.VMEM((n_atom, GR, LW), BF16),
                pltpu.VMEM((8, n_vectors), BF16),
                pltpu.VMEM((SR, LW), BF16),
                pltpu.VMEM((n_ka, 8, 128), BF16),
                pltpu.VMEM((n_ka, 8, 128), BF16),
                pltpu.VMEM((n_ka * 8, 128), F32),
                pltpu.SemaphoreType.DMA((10,)),
                pltpu.SemaphoreType.DMA,
                pltpu.SemaphoreType.DMA,
                pltpu.SemaphoreType.DMA,
                pltpu.SemaphoreType.DMA,
                pltpu.SemaphoreType.DMA,
                pltpu.SemaphoreType.DMA,
            ],
            compiler_params=pltpu.CompilerParams(
                collective_id=0, has_side_effects=True, vmem_limit_bytes=24 * 1024 * 1024
            ),
            name="ewald",
        )(*[pltpu.with_memory_space_constraint(v, pltpu.HBM) for v in (
            positions,
            features,
            species.reshape(1, atoms),
            miller,
            species_table.T,
            filter_weight.T,
            norm_gain.reshape(1, channels),
            up_weight.T,
            down_weight,
        )])

    in_specs = (P(None, "atom"), P(None, "atom"), P("atom"), P(None, "ka"), P(), P(), P(), P(), P())
    out_specs = P(None, ("atom", "ka"))
    return jax.shard_map(body, mesh=mesh, in_specs=in_specs, out_specs=out_specs, check_vma=False)
```

```python
import functools
import math

import jax
import jax.numpy as jnp
from jax import lax
from jax.experimental import pallas as pl
from jax.experimental.pallas import tpu as pltpu
from jax.sharding import PartitionSpec as P

MESH = pl.DeviceIdType.MESH
F32, BF16 = jnp.float32, jnp.bfloat16
NRBF = 16
NSPEC = 8
MAXM = 8
LW = 128
SR = 112
GR = 104
CHUNK = 512
DEPTH = 4096
K_CUTOFF = 14.0

def _fit():
    import numpy as np

    n = 400
    u = 0.125 + 0.125 * np.cos(np.pi * (np.arange(n) + 0.5) / n)
    r = np.sqrt(u)
    c = np.polynomial.chebyshev.Chebyshev.fit(u, np.cos(2 * np.pi * r), 4, domain=[0, 0.25])
    s = np.polynomial.chebyshev.Chebyshev.fit(u, np.sin(2 * np.pi * r) / r, 4, domain=[0, 0.25])
    return (
        [float(v) for v in c.convert(kind=np.polynomial.Polynomial).coef],
        [float(v) for v in s.convert(kind=np.polynomial.Polynomial).coef],
    )


COS_COEF, SIN_COEF = _fit()


def poly(u, coef):
    acc = jnp.full_like(u, coef[-1])
    for c in coef[-2::-1]:
        acc = acc * u + c
    return acc


def harmonics(row, orders):
    t = row * orders
    r = t - jnp.round(t)
    u = r * r
    return poly(u, COS_COEF), r * poly(u, SIN_COEF)


def iota(shape, axis):
    return lax.broadcasted_iota(jnp.int32, shape, axis)


def lane_orders(shape, axis):
    lane = iota(shape, axis)
    main = lane < 112
    u = jnp.where(main, lane >> 4, lane - 112)
    tu = jnp.where((u >= 3) & (u < 6), 1, 0)
    a = jnp.where(u < 3, u + 1, jnp.where(u < 6, u - 2, 0))
    ty = jnp.where(main, (lane >> 3) & 1, 0)
    q = jnp.where(main, (lane & 7) + 1, 0)
    return tu, a, ty, q, lane < 119


def swap_y(x):
    lane = iota(x.shape, 1)
    s = jnp.where((lane & 8) == 0, pltpu.roll(x, 120, 1), pltpu.roll(x, 8, 1))
    return jnp.where(lane < 112, s, 0.0)


def swap_u(x):
    lane = iota(x.shape, 1)
    s = jnp.where(lane < 48, pltpu.roll(x, 80, 1), jnp.where(lane < 96, pltpu.roll(x, 48, 1), 0.0))
    s = jnp.where((lane >= 112) & (lane < 115), pltpu.roll(x, 125, 1), s)
    return jnp.where((lane >= 115) & (lane < 118), pltpu.roll(x, 3, 1), s)


def signed(same, w):
    return jnp.where(same, -w, w)


GROUP = 4


def body_kernel(
    sizes,
    pos_hbm,
    feat_hbm,
    species_hbm,
    miller_hbm,
    tab_hbm,
    fw_hbm,
    gain_hbm,
    up_hbm,
    down_hbm,
    out_ref,
    pos_ref,
    species_ref,
    miller_ref,
    tab_ref,
    fw_ref,
    gain_ref,
    up_ref,
    down_ref,
    feat_blk,
    feat_loc,
    yu,
    sz,
    zz,
    vb,
    vv,
    xrows,
    gacc,
    gsend,
    grecv,
    mil_all,
    hmat,
    msgs,
    mrecv,
    mflat,
    local_sem,
    mil_send,
    mil_recv,
    g_send,
    g_recv,
    m_send,
    m_recv,
):
    n_atom, n_ka, ny, nz, atoms, scaling = sizes
    ia, ik = lax.axis_index("atom"), lax.axis_index("ka")
    local = atoms // n_ka
    n_chunks = atoms // CHUNK
    n_vec = n_ka * 128

    barrier = pltpu.get_barrier_semaphore()

    iy, iz = ik // nz, lax.rem(ik, nz)

    def along_y(d):
        return lax.rem(iy + d, ny) * nz + iz

    def along_z(d):
        return iy * nz + lax.rem(iz + d, nz)

    def greet_z(d, _):
        pl.semaphore_signal(barrier, inc=1, device_id=(ia, along_z(d)), device_id_type=MESH)
        return 0

    def greet_y(d, _):
        pl.semaphore_signal(barrier, inc=1, device_id=(ia, along_y(d)), device_id_type=MESH)
        return 0

    def greet_atom(d, _):
        pl.semaphore_signal(barrier, inc=1, device_id=(lax.rem(ia + d, n_atom), ik), device_id_type=MESH)
        return 0

    loads = []
    for i, (src, dst) in enumerate(
        [
            (pos_hbm, pos_ref),
            (species_hbm, species_ref),
            (feat_hbm.at[pl.ds(pl.multiple_of((ik // 4) * 8, 8), 8), :], feat_blk),
            (tab_hbm, tab_ref),
            (miller_hbm, miller_ref),
            (fw_hbm, fw_ref),
            (gain_hbm, gain_ref),
            (up_hbm, up_ref),
            (down_hbm, down_ref),
            (feat_hbm.at[:, pl.ds(pl.multiple_of(ik * local, local), local)], feat_loc),
        ]
    ):
        copy = pltpu.make_async_copy(src, dst, local_sem.at[i])
        copy.start()
        loads.append(copy)
    lax.fori_loop(1, nz, greet_z, 0)
    lax.fori_loop(1, ny, greet_y, 0)
    lax.fori_loop(1, n_atom, greet_atom, 0)

    gacc[...] = jnp.zeros_like(gacc)
    sub = iota((8, CHUNK), 0)
    orders = (sub + 1).astype(F32)
    third = jnp.where(sub < 3, sub, sub - 3)
    x_orders = jnp.where(sub < 6, 3 * third + 3, 1).astype(F32)
    for copy in loads[:5]:
        copy.wait()
    mil_all[:, pl.ds(pl.multiple_of(ik * 128, 128), 128)] = jnp.concatenate(
        [miller_ref[...].astype(F32), jnp.zeros((5, 128), F32)], axis=0
    ).astype(BF16)
    column = iota((NSPEC, 64), 1)
    tabs = [
        jnp.broadcast_to(
            jnp.sum(jnp.where(column == 2 * ik + c, tab_ref[...], 0.0), axis=1, keepdims=True), (8, CHUNK)
        )
        for c in range(2)
    ]
    which = [sub == lax.rem(2 * ik, 8) + c for c in range(2)]

    def row_of(i):
        return jnp.broadcast_to(xrows[i : i + 1, :], (8, CHUNK))

    def store(ref, r0, cols, upper, lower):
        ref[r0 : r0 + 16, cols] = jnp.concatenate([upper, lower], axis=0).astype(BF16)

    def gather_chunk(j, _):
        cols = pl.ds(pl.multiple_of(j * CHUNK, CHUNK), CHUNK)
        xc, xs = harmonics(jnp.broadcast_to(pos_ref[0:1, cols], (8, CHUNK)), x_orders)
        xrows[0:8, :] = xc
        xrows[8:16, :] = xs
        yc, ys = harmonics(jnp.broadcast_to(pos_ref[1:2, cols], (8, CHUNK)), orders)
        zc, zs = harmonics(jnp.broadcast_to(pos_ref[2:3, cols], (8, CHUNK)), orders)
        vc, vs = row_of(6), row_of(14)
        ones = jnp.where(third == 1, vc, jnp.where(third == 2, vs, 1.0))
        ones = jnp.where(sub < 6, ones, 0.0)
        zero = jnp.zeros((8, CHUNK), F32)
        zz[0:8, cols] = zc
        zz[8:16, cols] = zs
        vb[0:8, cols] = vc
        vb[8:16, cols] = vs
        vv[:, cols] = ones
        for i, r in enumerate((0, 1, 2, 11, 12, 13)):
            u = row_of(r)
            store(yu, 16 * i, cols, u * yc, u * ys)
        store(yu, 96, cols, yc, ys)
        store(
            yu, 112, cols, jnp.where(sub < 3, xc, jnp.where(sub < 6, xs, jnp.where(sub == 6, 1.0, 0.0))), zero
        )
        fb = feat_blk[:, cols].astype(F32)
        hot = jnp.broadcast_to(species_ref[0:1, cols], (8, CHUNK)) == sub
        sources = []
        for c in range(2):
            s = jnp.where(which[c], fb, 0.0) + jnp.where(hot, tabs[c], 0.0)
            s = jnp.broadcast_to(jnp.sum(s, axis=0, keepdims=True), (8, CHUNK))
            s = s.astype(BF16).astype(F32)
            sources.append(s)
            szc, szs = s * zc, s * zs
            store(sz, 48 * c, cols, szc, szs)
            store(sz, 48 * c + 16, cols, szc * vc, szs * vc)
            store(sz, 48 * c + 32, cols, szc * vs, szs * vs)
        store(sz, 96, cols, jnp.where(sub < 3, sources[0], sources[1]) * ones, zero)
        return 0

    lax.fori_loop(0, n_chunks, gather_chunk, 0)

    def add_products(j, _):
        cols = pl.ds(pl.multiple_of(j * DEPTH, DEPTH), DEPTH)
        gacc[...] += lax.dot_general(
            sz[:, cols], yu[:, cols], (((1,), (1,)), ((), ())), preferred_element_type=F32
        )
        return 0

    lax.fori_loop(0, atoms // DEPTH, add_products, 0)
    gsend[...] = gacc[0:GR, :].astype(BF16)

    pl.semaphore_wait(barrier, nz - 1 + ny - 1 + n_atom - 1)

    def g_copy(slot, to):
        return pltpu.make_async_remote_copy(
            src_ref=gsend,
            dst_ref=grecv.at[slot],
            send_sem=g_send,
            recv_sem=g_recv,
            device_id=(to, ik),
            device_id_type=MESH,
        )

    def send_g(d, _):
        g_copy(ia, lax.rem(ia + d, n_atom)).start()
        return 0

    def mil_copy(ref, to, stage):
        return pltpu.make_async_remote_copy(
            src_ref=ref,
            dst_ref=ref,
            send_sem=mil_send.at[stage],
            recv_sem=mil_recv.at[stage],
            device_id=(ia, to),
            device_id_type=MESH,
        )

    own = mil_all.at[:, pl.ds(pl.multiple_of(ik * 128, 128), 128)]
    own_row = mil_all.at[:, pl.ds(pl.multiple_of(iy * (nz * 128), nz * 128), nz * 128)]
    all_z = mil_copy(mil_all.at[:, 0 : (nz - 1) * 128], ik, 0)
    all_y = mil_copy(mil_all.at[:, 0 : (ny - 1) * nz * 128], ik, 1)

    def farther(k, n):
        return n // 2 + (1 - 2 * lax.rem(k, 2)) * ((k + 1) // 2)

    def partner(i):
        dz, dy = farther(i // ny, nz), farther(lax.rem(i, ny), ny)
        y, z = lax.rem(ik // nz + dy, ny), lax.rem(lax.rem(ik, nz) + dz, nz)
        return y * nz + z

    def send_z(i, _):
        mil_copy(own, along_z(farther(i, nz)), 0).start()
        return 0

    def send_y(d, _):
        mil_copy(own_row, along_y(d), 1).start()
        return 0

    lax.fori_loop(0, nz - 1, send_z, 0)
    lax.fori_loop(1, n_atom, send_g, 0)

    for copy in loads[5:]:
        copy.wait()
    sub1 = iota((8, 128), 0)
    r8 = (sub1 + 1).astype(F32)
    column = iota((NRBF, 64), 1)
    weights = [
        jnp.sum(jnp.where(column == 2 * ik + c, fw_ref[...], 0.0), axis=1, keepdims=True) * scaling
        for c in range(2)
    ]
    tu, a, ty, q, _ = lane_orders((8, 128), 1)
    af, qq = a.astype(F32) * 3.0, (q * q).astype(F32)
    third1 = jnp.where(sub1 < 3, sub1, sub1 - 3)
    b_row = jnp.where((third1 > 0) & (sub1 < 6), 1.0, 0.0)
    tv_row = jnp.where(third1 == 2, 1, 0)

    def radial_of(m, r):
        mag = jnp.sqrt(m * m + qq + r * r)
        acc = [jnp.zeros((8, 128), F32) for _ in range(2)]
        for b in range(NRBF):
            z = (mag - b * (K_CUTOFF / (NRBF - 1))) * (NRBF / K_CUTOFF)
            e = jnp.exp(-(z * z))
            for c in range(2):
                acc[c] = acc[c] + weights[c][b : b + 1, :] * e
        return acc

    zero1 = jnp.zeros((8, 128), F32)
    rad_0 = radial_of(af, r8)
    rad_p, rad_m = radial_of(af + 1.0, r8), radial_of(af - 1.0, r8)
    single_p, single_m = [
        jnp.where(sub1 < 3, v[0], v[1]) for v in (radial_of(af + b_row, zero1), radial_of(af - b_row, zero1))
    ]

    all_z.wait_recv()
    lax.fori_loop(1, ny, send_y, 0)

    pltpu.make_async_remote_copy(
        src_ref=grecv.at[0 : n_atom - 1],
        dst_ref=grecv.at[0 : n_atom - 1],
        send_sem=g_send,
        recv_sem=g_recv,
        device_id=(ia, ik),
        device_id_type=MESH,
    ).wait_recv()
    grecv[ia] = gsend[...]
    g = grecv[0].astype(F32)
    for i in range(1, n_atom):
        g = g + grecv[i].astype(F32)

    all_y.wait_recv()
    _, a_r, _, q_r, used = lane_orders((LW, CHUNK), 0)
    codes = jnp.where(used, a_r * 9 + q_r, -1).astype(F32)
    b_sub = jnp.where(third == 0, 0.0, 1.0)
    b_sub = jnp.where(sub < 6, b_sub, -1.0)
    counts = jnp.zeros((128, LW), F32)
    for j in range(n_vec // CHUNK):
        m = mil_all[:, CHUNK * j : CHUNK * (j + 1)].astype(F32)
        mx, my, mz = [jnp.broadcast_to(m[i : i + 1, :], (8, CHUNK)) for i in range(3)]
        ma = jnp.round(mx * (1.0 / 3.0))
        mb = mx - 3.0 * ma
        ga, gb, gy, gz = [jnp.where(v < 0, -1.0, 1.0) for v in (ma, mb, my, mz)]
        code = jnp.abs(ma) * 9.0 + jnp.abs(my)
        hot_uy = jnp.where(codes == jnp.broadcast_to(code[0:1, :], (LW, CHUNK)), 1.0, 0.0).astype(BF16)
        ab, ar, br, aq, bq, qr = ga * gb, ga * gz, gb * gz, ga * gy, gb * gy, gy * gz
        az, absb = jnp.abs(mz), jnp.abs(mb)
        hz = jnp.where(az == orders, 1.0, 0.0)
        h1 = hz * absb
        h0 = hz - h1
        hs = jnp.where((az == 0.0) & (absb == b_sub), 1.0, 0.0)
        wr = jnp.concatenate(
            [h1, h1 * ab, h1 * ar, h1 * br, h1 * aq, h1 * bq, h1 * qr, h1 * (ab * qr)]
            + [h0, h0 * aq, h0 * ar, h0 * qr]
            + [hs, hs * ab, hs * aq, hs * bq],
            axis=0,
        ).astype(BF16)
        counts = counts + lax.dot_general(
            wr, hot_uy, (((1,), (1,)), ((), ())), preferred_element_type=F32
        )
    w = [counts[8 * i : 8 * i + 8, :] for i in range(16)]

    def mixed(plus, minus, plain, crossed):
        half_s, half_d = 0.5 * (plus + minus), 0.5 * (plus - minus)
        return half_s * plain + half_d * crossed, half_s * crossed + half_d * plain

    same_uy = tu == ty
    rows = []
    for c in range(2):
        gb = [[g[48 * c + 16 * v + 8 * t : 48 * c + 16 * v + 8 * t + 8, :] for t in range(2)] for v in range(3)]
        gu = [[swap_u(x) for x in pair] for pair in gb]
        gy = [[swap_y(x) for x in pair] for pair in gb]
        guy = [[swap_u(x) for x in pair] for pair in gy]
        for t in range(2):
            h = w[8] * gb[0][t] + signed(same_uy, w[9]) * guy[0][t]
            h = h + signed(tu == t, w[10]) * gu[0][1 - t] + signed(ty == t, w[11]) * gy[0][1 - t]
            rows.append(h * rad_0[c])
        c_0, c_ab = mixed(rad_p[c], rad_m[c], w[0], w[1])
        c_ar, c_br = mixed(rad_p[c], rad_m[c], w[2], w[3])
        c_aq, c_bq = mixed(rad_p[c], rad_m[c], w[4], w[5])
        c_qr, c_all = mixed(rad_p[c], rad_m[c], w[6], w[7])
        for v in (1, 2):
            tv, o = v - 1, 3 - v
            for t in range(2):
                h = c_0 * gb[v][t] + signed(same_uy, c_aq) * guy[v][t]
                h = h + signed(tu == t, c_ar) * gu[v][1 - t] + signed(ty == t, c_qr) * gy[v][1 - t]
                h = h + signed(tu == tv, c_ab) * gu[o][t] + signed(ty == tv, c_bq) * gy[o][t]
                h = h + (-c_br if tv == t else c_br) * gb[o][1 - t]
                odd = same_uy if (tv + t) % 2 == 1 else tu != ty
                rows.append(h + signed(odd, c_all) * guy[o][1 - t])
    g0 = g[96:104, :]
    over = jnp.where(third1 == 1, pltpu.roll(g0, 7, 0), pltpu.roll(g0, 1, 0))
    over = jnp.where(b_row > 0.0, over, 0.0)
    c_0, c_ab = mixed(single_p, single_m, w[12], w[13])
    c_aq, c_bq = mixed(single_p, single_m, w[14], w[15])
    h = c_0 * g0 + signed(same_uy, c_aq) * swap_u(swap_y(g0))
    h = h + signed(tu == tv_row, c_ab) * swap_u(over) + signed(ty == tv_row, c_bq) * swap_y(over)
    rows += [h, jnp.zeros((8, LW), F32)]
    hmat[...] = jnp.concatenate(rows, axis=0).astype(BF16)

    def m_copy(slot, to):
        return pltpu.make_async_remote_copy(
            src_ref=msgs.at[to],
            dst_ref=mrecv.at[slot],
            send_sem=m_send,
            recv_sem=m_recv,
            device_id=(ia, to),
            device_id_type=MESH,
        )

    def message_of(d, cols):
        zc, zs = zz[0:8, cols], zz[8:16, cols]
        vs = (None, vb[0:8, cols], vb[8:16, cols])
        single = d[96:104, :] * vv[:, cols]
        parts = []
        for c in range(2):
            s = jnp.where((sub < 3) == (c == 0), single, 0.0)
            for v in range(3):
                r = 48 * c + 16 * v
                e = d[r : r + 8, :] * zc + d[r + 8 : r + 16, :] * zs
                s = s + (e if v == 0 else e * vs[v])
            s = jnp.sum(s, axis=0, keepdims=True)
            parts += [s[:, 128 * i : 128 * (i + 1)] for i in range(CHUNK // 128)]
        return jnp.concatenate(parts, axis=0).astype(BF16)

    def send_messages(i, _):
        to = [partner(GROUP * i + k) for k in range(GROUP)]
        cols = [pl.ds(pl.multiple_of(j * CHUNK, CHUNK), CHUNK) for j in to]
        ds = [jnp.dot(hmat[...], yu[:, c], preferred_element_type=F32) for c in cols]
        for k in range(GROUP):
            msgs[to[k]] = message_of(ds[k], cols[k])
        for k in range(GROUP):
            @pl.when(to[k] != ik)
            def _():
                m_copy(ik, to[k]).start()
        return 0

    lax.fori_loop(0, n_ka // GROUP, send_messages, 0)
    mrecv[ik] = msgs[ik]
    eye = iota((64, 64), 0) == iota((64, 64), 1)
    gain = jnp.sum(jnp.where(eye, jnp.broadcast_to(gain_ref[...], (64, 64)), 0.0), axis=1, keepdims=True)

    def all_messages():
        return pltpu.make_async_remote_copy(
            src_ref=mrecv.at[0 : n_ka - 1],
            dst_ref=mrecv.at[0 : n_ka - 1],
            send_sem=m_send,
            recv_sem=m_recv,
            device_id=(ia, ik),
            device_id_type=MESH,
        )

    all_messages().wait_recv()

    mflat[...] = mrecv[...].astype(F32).reshape(mflat.shape)
    message = jnp.concatenate(
        [mflat[pl.ds(i, 64, stride=4), :] for i in range(local // 128)], axis=1
    )
    mean_sq = jnp.sum(message * message, axis=0, keepdims=True) * (1.0 / 64.0)
    normed = (message * lax.rsqrt(mean_sq + 1e-06) * gain).astype(BF16)
    hidden = lax.dot_general(up_ref[...], normed, (((0,), (0,)), ((), ())), preferred_element_type=F32)
    hidden = (hidden / (1.0 + jnp.exp(-hidden))).astype(BF16)
    update = jnp.dot(down_ref[...], hidden, preferred_element_type=F32)
    out_ref[...] = (feat_loc[...].astype(F32) + update).astype(BF16)

    all_z.wait_send()
    all_y.wait_send()
    all_messages().wait_send()
    pltpu.make_async_remote_copy(
        src_ref=grecv.at[0 : n_atom - 1],
        dst_ref=grecv.at[0 : n_atom - 1],
        send_sem=g_send,
        recv_sem=g_recv,
        device_id=(ia, ik),
        device_id_type=MESH,
    ).wait_send()


def solution(mesh):
    n_atom, n_ka = mesh.shape["atom"], mesh.shape["ka"]
    ny, nz = 4, n_ka // 4

    def body(positions, features, species, miller, species_table, filter_weight, norm_gain, up_weight, down_weight):
        channels, atoms = features.shape
        local = atoms // n_ka
        n_vectors = miller.shape[1] * n_ka
        hid = up_weight.shape[0]
        scaling = 1.0 / math.sqrt(atoms * n_atom * n_vectors)
        any_space = pl.BlockSpec(memory_space=pltpu.HBM)
        return pl.pallas_call(
            functools.partial(body_kernel, (n_atom, n_ka, ny, nz, atoms, scaling)),
            out_shape=jax.ShapeDtypeStruct((channels, local), BF16),
            in_specs=[any_space] * 9,
            out_specs=pl.BlockSpec(memory_space=pltpu.VMEM),
            scratch_shapes=[
                pltpu.VMEM((3, atoms), F32),
                pltpu.VMEM((1, atoms), jnp.int32),
                pltpu.VMEM((3, 128), jnp.int32),
                pltpu.VMEM((NSPEC, channels), F32),
                pltpu.VMEM((NRBF, channels), F32),
                pltpu.VMEM((1, channels), F32),
                pltpu.VMEM((channels, hid), BF16),
                pltpu.VMEM((channels, hid), BF16),
                pltpu.VMEM((8, atoms), BF16),
                pltpu.VMEM((channels, local), BF16),
                pltpu.VMEM((LW, atoms), BF16),
                pltpu.VMEM((SR, atoms), BF16),
                pltpu.VMEM((16, atoms), F32),
                pltpu.VMEM((16, atoms), F32),
                pltpu.VMEM((8, atoms), F32),
                pltpu.VMEM((16, CHUNK), F32),
                pltpu.VMEM((SR, LW), F32),
                pltpu.VMEM((GR, LW), BF16),
                pltpu.VMEM((n_atom, GR, LW), BF16),
                pltpu.VMEM((8, n_vectors), BF16),
                pltpu.VMEM((SR, LW), BF16),
                pltpu.VMEM((n_ka, 8, 128), BF16),
                pltpu.VMEM((n_ka, 8, 128), BF16),
                pltpu.VMEM((n_ka * 8, 128), F32),
                pltpu.SemaphoreType.DMA((10,)),
                pltpu.SemaphoreType.DMA((2,)),
                pltpu.SemaphoreType.DMA((2,)),
                pltpu.SemaphoreType.DMA,
                pltpu.SemaphoreType.DMA,
                pltpu.SemaphoreType.DMA,
                pltpu.SemaphoreType.DMA,
            ],
            compiler_params=pltpu.CompilerParams(
                collective_id=0, has_side_effects=True, vmem_limit_bytes=24 * 1024 * 1024
            ),
            name="ewald",
        )(*[pltpu.with_memory_space_constraint(v, pltpu.HBM) for v in (
            positions,
            features,
            species.reshape(1, atoms),
            miller,
            species_table.T,
            filter_weight.T,
            norm_gain.reshape(1, channels),
            up_weight.T,
            down_weight,
        )])

    in_specs = (P(None, "atom"), P(None, "atom"), P("atom"), P(None, "ka"), P(), P(), P(), P(), P())
    out_specs = P(None, ("atom", "ka"))
    return jax.shard_map(body, mesh=mesh, in_specs=in_specs, out_specs=out_specs, check_vma=False)
```

```python
import functools
import math

import jax
import jax.numpy as jnp
from jax import lax
from jax.experimental import pallas as pl
from jax.experimental.pallas import tpu as pltpu
from jax.sharding import PartitionSpec as P

MESH = pl.DeviceIdType.MESH
F32, BF16 = jnp.float32, jnp.bfloat16
NRBF = 16
NSPEC = 8
MAXM = 8
LW = 128
SR = 112
GR = 104
CHUNK = 512
DEPTH = 8192
EARLY = 14
K_CUTOFF = 14.0

def _fit():
    import numpy as np

    n = 400
    u = 0.125 + 0.125 * np.cos(np.pi * (np.arange(n) + 0.5) / n)
    r = np.sqrt(u)
    c = np.polynomial.chebyshev.Chebyshev.fit(u, np.cos(2 * np.pi * r), 4, domain=[0, 0.25])
    s = np.polynomial.chebyshev.Chebyshev.fit(u, np.sin(2 * np.pi * r) / r, 4, domain=[0, 0.25])
    return (
        [float(v) for v in c.convert(kind=np.polynomial.Polynomial).coef],
        [float(v) for v in s.convert(kind=np.polynomial.Polynomial).coef],
    )


COS_COEF, SIN_COEF = _fit()


def poly(u, coef):
    acc = jnp.full_like(u, coef[-1])
    for c in coef[-2::-1]:
        acc = acc * u + c
    return acc


def harmonics(row, orders):
    t = row * orders
    r = t - jnp.round(t)
    u = r * r
    return poly(u, COS_COEF), r * poly(u, SIN_COEF)


def iota(shape, axis):
    return lax.broadcasted_iota(jnp.int32, shape, axis)


def lane_orders(shape, axis):
    lane = iota(shape, axis)
    main = lane < 112
    u = jnp.where(main, lane >> 4, lane - 112)
    tu = jnp.where((u >= 3) & (u < 6), 1, 0)
    a = jnp.where(u < 3, u + 1, jnp.where(u < 6, u - 2, 0))
    ty = jnp.where(main, (lane >> 3) & 1, 0)
    q = jnp.where(main, (lane & 7) + 1, 0)
    return tu, a, ty, q, lane < 119


def swap_y(x):
    lane = iota(x.shape, 1)
    s = jnp.where((lane & 8) == 0, pltpu.roll(x, 120, 1), pltpu.roll(x, 8, 1))
    return jnp.where(lane < 112, s, 0.0)


def swap_u(x):
    lane = iota(x.shape, 1)
    s = jnp.where(lane < 48, pltpu.roll(x, 80, 1), jnp.where(lane < 96, pltpu.roll(x, 48, 1), 0.0))
    s = jnp.where((lane >= 112) & (lane < 115), pltpu.roll(x, 125, 1), s)
    return jnp.where((lane >= 115) & (lane < 118), pltpu.roll(x, 3, 1), s)


def signed(same, w):
    return jnp.where(same, -w, w)


GROUP = 4


def body_kernel(
    sizes,
    pos_hbm,
    feat_hbm,
    species_hbm,
    miller_hbm,
    tab_hbm,
    fw_hbm,
    gain_hbm,
    up_hbm,
    down_hbm,
    out_ref,
    pos_ref,
    species_ref,
    miller_ref,
    tab_ref,
    fw_ref,
    gain_ref,
    up_ref,
    down_ref,
    feat_blk,
    feat_loc,
    yu,
    sz,
    zz,
    vb,
    vv,
    xrows,
    gacc,
    gsend,
    grecv,
    mil_all,
    hmat,
    msgs,
    mrecv,
    mflat,
    local_sem,
    mil_send,
    mil_recv,
    g_send,
    g_recv,
    m_send,
    m_recv,
):
    n_atom, n_ka, ny, nz, atoms, scaling = sizes
    ia, ik = lax.axis_index("atom"), lax.axis_index("ka")
    local = atoms // n_ka
    n_chunks = atoms // CHUNK
    n_vec = n_ka * 128

    barrier = pltpu.get_barrier_semaphore()

    iy, iz = ik // nz, lax.rem(ik, nz)

    def along_y(d):
        return lax.rem(iy + d, ny) * nz + iz

    def along_z(d):
        return iy * nz + lax.rem(iz + d, nz)

    def greet_z(d, _):
        pl.semaphore_signal(barrier, inc=1, device_id=(ia, along_z(d)), device_id_type=MESH)
        return 0

    def greet_y(d, _):
        pl.semaphore_signal(barrier, inc=1, device_id=(ia, along_y(d)), device_id_type=MESH)
        return 0

    def greet_atom(d, _):
        pl.semaphore_signal(barrier, inc=1, device_id=(lax.rem(ia + d, n_atom), ik), device_id_type=MESH)
        return 0

    loads = []
    for i, (src, dst) in enumerate(
        [
            (pos_hbm, pos_ref),
            (species_hbm, species_ref),
            (feat_hbm.at[pl.ds(pl.multiple_of((ik // 4) * 8, 8), 8), :], feat_blk),
            (tab_hbm, tab_ref),
            (miller_hbm, miller_ref),
            (fw_hbm, fw_ref),
            (gain_hbm, gain_ref),
            (up_hbm, up_ref),
            (down_hbm, down_ref),
            (feat_hbm.at[:, pl.ds(pl.multiple_of(ik * local, local), local)], feat_loc),
        ]
    ):
        copy = pltpu.make_async_copy(src, dst, local_sem.at[i])
        copy.start()
        loads.append(copy)
    lax.fori_loop(1, nz, greet_z, 0)
    lax.fori_loop(1, ny, greet_y, 0)
    lax.fori_loop(1, n_atom, greet_atom, 0)

    gacc[...] = jnp.zeros_like(gacc)
    sub = iota((8, CHUNK), 0)
    orders = (sub + 1).astype(F32)
    third = jnp.where(sub < 3, sub, sub - 3)
    x_orders = jnp.where(sub < 6, 3 * third + 3, 1).astype(F32)
    for copy in loads[:5]:
        copy.wait()
    mil_all[:, pl.ds(pl.multiple_of(ik * 128, 128), 128)] = jnp.concatenate(
        [miller_ref[...].astype(F32), jnp.zeros((5, 128), F32)], axis=0
    ).astype(BF16)
    column = iota((NSPEC, 64), 1)
    tabs = [
        jnp.broadcast_to(
            jnp.sum(jnp.where(column == 2 * ik + c, tab_ref[...], 0.0), axis=1, keepdims=True), (8, CHUNK)
        )
        for c in range(2)
    ]
    which = [sub == lax.rem(2 * ik, 8) + c for c in range(2)]

    def row_of(i):
        return jnp.broadcast_to(xrows[i : i + 1, :], (8, CHUNK))

    def store(ref, r0, cols, upper, lower):
        ref[r0 : r0 + 16, cols] = jnp.concatenate([upper, lower], axis=0).astype(BF16)

    def gather_chunk(j, _):
        cols = pl.ds(pl.multiple_of(j * CHUNK, CHUNK), CHUNK)
        xc, xs = harmonics(jnp.broadcast_to(pos_ref[0:1, cols], (8, CHUNK)), x_orders)
        xrows[0:8, :] = xc
        xrows[8:16, :] = xs
        yc, ys = harmonics(jnp.broadcast_to(pos_ref[1:2, cols], (8, CHUNK)), orders)
        zc, zs = harmonics(jnp.broadcast_to(pos_ref[2:3, cols], (8, CHUNK)), orders)
        vc, vs = row_of(6), row_of(14)
        ones = jnp.where(third == 1, vc, jnp.where(third == 2, vs, 1.0))
        ones = jnp.where(sub < 6, ones, 0.0)
        zero = jnp.zeros((8, CHUNK), F32)
        zz[0:8, cols] = zc
        zz[8:16, cols] = zs
        vb[0:8, cols] = vc
        vb[8:16, cols] = vs
        vv[:, cols] = ones
        for i, r in enumerate((0, 1, 2, 11, 12, 13)):
            u = row_of(r)
            store(yu, 16 * i, cols, u * yc, u * ys)
        store(yu, 96, cols, yc, ys)
        store(
            yu, 112, cols, jnp.where(sub < 3, xc, jnp.where(sub < 6, xs, jnp.where(sub == 6, 1.0, 0.0))), zero
        )
        fb = feat_blk[:, cols].astype(F32)
        hot = jnp.broadcast_to(species_ref[0:1, cols], (8, CHUNK)) == sub
        sources = []
        for c in range(2):
            s = jnp.where(which[c], fb, 0.0) + jnp.where(hot, tabs[c], 0.0)
            s = jnp.broadcast_to(jnp.sum(s, axis=0, keepdims=True), (8, CHUNK))
            s = s.astype(BF16).astype(F32)
            sources.append(s)
            szc, szs = s * zc, s * zs
            store(sz, 48 * c, cols, szc, szs)
            store(sz, 48 * c + 16, cols, szc * vc, szs * vc)
            store(sz, 48 * c + 32, cols, szc * vs, szs * vs)
        store(sz, 96, cols, jnp.where(sub < 3, sources[0], sources[1]) * ones, zero)
        return 0

    def mil_copy(ref, to, stage):
        return pltpu.make_async_remote_copy(
            src_ref=ref,
            dst_ref=ref,
            send_sem=mil_send.at[stage],
            recv_sem=mil_recv.at[stage],
            device_id=(ia, to),
            device_id_type=MESH,
        )

    own = mil_all.at[:, pl.ds(pl.multiple_of(ik * 128, 128), 128)]
    own_row = mil_all.at[:, pl.ds(pl.multiple_of(iy * (nz * 128), nz * 128), nz * 128)]
    all_z = mil_copy(mil_all.at[:, 0 : (nz - 1) * 128], ik, 0)
    all_y = mil_copy(mil_all.at[:, 0 : (ny - 1) * nz * 128], ik, 1)

    def farther(k, n):
        return n // 2 + (1 - 2 * lax.rem(k, 2)) * ((k + 1) // 2)

    def partner(i):
        dz, dy = farther(i // ny, nz), farther(lax.rem(i, ny), ny)
        y, z = lax.rem(ik // nz + dy, ny), lax.rem(lax.rem(ik, nz) + dz, nz)
        return y * nz + z

    def send_z(i, _):
        mil_copy(own, along_z(farther(i, nz)), 0).start()
        return 0

    def send_y(d, _):
        mil_copy(own_row, along_y(d), 1).start()
        return 0

    lax.fori_loop(0, EARLY, gather_chunk, 0)
    pl.semaphore_wait(barrier, nz - 1 + ny - 1 + n_atom - 1)
    lax.fori_loop(0, nz - 1, send_z, 0)
    lax.fori_loop(EARLY, n_chunks, gather_chunk, 0)

    halves = ((0, SR, GR),)

    def g_copy(half, slot, to):
        lo, _, hi = halves[half]
        return pltpu.make_async_remote_copy(
            src_ref=gsend.at[lo:hi],
            dst_ref=grecv.at[slot, lo:hi],
            send_sem=g_send.at[half],
            recv_sem=g_recv.at[half],
            device_id=(to, ik),
            device_id_type=MESH,
        )

    def all_g(half):
        lo, _, hi = halves[half]
        part = grecv.at[0 : n_atom - 1, lo:hi]
        return pltpu.make_async_remote_copy(
            src_ref=part,
            dst_ref=part,
            send_sem=g_send.at[half],
            recv_sem=g_recv.at[half],
            device_id=(ia, ik),
            device_id_type=MESH,
        )

    for half, (lo, up_to, hi) in enumerate(halves):

        def add_products(j, _, lo=lo, up_to=up_to):
            cols = pl.ds(pl.multiple_of(j * DEPTH, DEPTH), DEPTH)
            gacc[lo:up_to, :] += lax.dot_general(
                sz[lo:up_to, cols], yu[:, cols], (((1,), (1,)), ((), ())), preferred_element_type=F32
            )
            return 0

        lax.fori_loop(0, atoms // DEPTH, add_products, 0)
        gsend[lo:hi, :] = gacc[lo:hi, :].astype(BF16)

        def send_g(i, _, half=half):
            g_copy(half, ia, lax.rem(ia + 1 + lax.rem(i + 2, n_atom - 1), n_atom)).start()
            return 0

        lax.fori_loop(0, n_atom - 1, send_g, 0)

    for copy in loads[5:]:
        copy.wait()
    sub1 = iota((8, 128), 0)
    r8 = (sub1 + 1).astype(F32)
    column = iota((NRBF, 64), 1)
    weights = [
        jnp.sum(jnp.where(column == 2 * ik + c, fw_ref[...], 0.0), axis=1, keepdims=True) * scaling
        for c in range(2)
    ]
    tu, a, ty, q, _ = lane_orders((8, 128), 1)
    af, qq = a.astype(F32) * 3.0, (q * q).astype(F32)
    third1 = jnp.where(sub1 < 3, sub1, sub1 - 3)
    b_row = jnp.where((third1 > 0) & (sub1 < 6), 1.0, 0.0)
    tv_row = jnp.where(third1 == 2, 1, 0)

    def radial_of(m, r):
        mag = jnp.sqrt(m * m + qq + r * r)
        acc = [jnp.zeros((8, 128), F32) for _ in range(2)]
        for b in range(NRBF):
            z = (mag - b * (K_CUTOFF / (NRBF - 1))) * (NRBF / K_CUTOFF)
            e = jnp.exp(-(z * z))
            for c in range(2):
                acc[c] = acc[c] + weights[c][b : b + 1, :] * e
        return acc

    zero1 = jnp.zeros((8, 128), F32)
    rad_0 = radial_of(af, r8)
    rad_p, rad_m = radial_of(af + 1.0, r8), radial_of(af - 1.0, r8)
    single_p, single_m = [
        jnp.where(sub1 < 3, v[0], v[1]) for v in (radial_of(af + b_row, zero1), radial_of(af - b_row, zero1))
    ]

    all_z.wait_recv()
    lax.fori_loop(1, ny, send_y, 0)

    all_y.wait_recv()
    _, a_r, _, q_r, used = lane_orders((LW, CHUNK), 0)
    codes = jnp.where(used, a_r * 9 + q_r, -1).astype(F32)
    b_sub = jnp.where(third == 0, 0.0, 1.0)
    b_sub = jnp.where(sub < 6, b_sub, -1.0)
    counts = jnp.zeros((128, LW), F32)
    for j in range(n_vec // CHUNK):
        m = mil_all[:, CHUNK * j : CHUNK * (j + 1)].astype(F32)
        mx, my, mz = [jnp.broadcast_to(m[i : i + 1, :], (8, CHUNK)) for i in range(3)]
        ma = jnp.round(mx * (1.0 / 3.0))
        mb = mx - 3.0 * ma
        ga, gb, gy, gz = [jnp.where(v < 0, -1.0, 1.0) for v in (ma, mb, my, mz)]
        code = jnp.abs(ma) * 9.0 + jnp.abs(my)
        hot_uy = jnp.where(codes == jnp.broadcast_to(code[0:1, :], (LW, CHUNK)), 1.0, 0.0).astype(BF16)
        ab, ar, br, aq, bq, qr = ga * gb, ga * gz, gb * gz, ga * gy, gb * gy, gy * gz
        az, absb = jnp.abs(mz), jnp.abs(mb)
        hz = jnp.where(az == orders, 1.0, 0.0)
        h1 = hz * absb
        h0 = hz - h1
        hs = jnp.where((az == 0.0) & (absb == b_sub), 1.0, 0.0)
        wr = jnp.concatenate(
            [h1, h1 * ab, h1 * ar, h1 * br, h1 * aq, h1 * bq, h1 * qr, h1 * (ab * qr)]
            + [h0, h0 * aq, h0 * ar, h0 * qr]
            + [hs, hs * ab, hs * aq, hs * bq],
            axis=0,
        ).astype(BF16)
        counts = counts + lax.dot_general(
            wr, hot_uy, (((1,), (1,)), ((), ())), preferred_element_type=F32
        )
    w = [counts[8 * i : 8 * i + 8, :] for i in range(16)]

    all_g(0).wait_recv()
    grecv[ia] = gsend[...]
    g = grecv[0].astype(F32)
    for i in range(1, n_atom):
        g = g + grecv[i].astype(F32)

    def mixed(plus, minus, plain, crossed):
        half_s, half_d = 0.5 * (plus + minus), 0.5 * (plus - minus)
        return half_s * plain + half_d * crossed, half_s * crossed + half_d * plain

    same_uy = tu == ty
    rows = []
    for c in range(2):
        gb = [[g[48 * c + 16 * v + 8 * t : 48 * c + 16 * v + 8 * t + 8, :] for t in range(2)] for v in range(3)]
        gu = [[swap_u(x) for x in pair] for pair in gb]
        gy = [[swap_y(x) for x in pair] for pair in gb]
        guy = [[swap_u(x) for x in pair] for pair in gy]
        for t in range(2):
            h = w[8] * gb[0][t] + signed(same_uy, w[9]) * guy[0][t]
            h = h + signed(tu == t, w[10]) * gu[0][1 - t] + signed(ty == t, w[11]) * gy[0][1 - t]
            rows.append(h * rad_0[c])
        c_0, c_ab = mixed(rad_p[c], rad_m[c], w[0], w[1])
        c_ar, c_br = mixed(rad_p[c], rad_m[c], w[2], w[3])
        c_aq, c_bq = mixed(rad_p[c], rad_m[c], w[4], w[5])
        c_qr, c_all = mixed(rad_p[c], rad_m[c], w[6], w[7])
        for v in (1, 2):
            tv, o = v - 1, 3 - v
            for t in range(2):
                h = c_0 * gb[v][t] + signed(same_uy, c_aq) * guy[v][t]
                h = h + signed(tu == t, c_ar) * gu[v][1 - t] + signed(ty == t, c_qr) * gy[v][1 - t]
                h = h + signed(tu == tv, c_ab) * gu[o][t] + signed(ty == tv, c_bq) * gy[o][t]
                h = h + (-c_br if tv == t else c_br) * gb[o][1 - t]
                odd = same_uy if (tv + t) % 2 == 1 else tu != ty
                rows.append(h + signed(odd, c_all) * guy[o][1 - t])
    g0 = g[96:104, :]
    over = jnp.where(third1 == 1, pltpu.roll(g0, 7, 0), pltpu.roll(g0, 1, 0))
    over = jnp.where(b_row > 0.0, over, 0.0)
    c_0, c_ab = mixed(single_p, single_m, w[12], w[13])
    c_aq, c_bq = mixed(single_p, single_m, w[14], w[15])
    h = c_0 * g0 + signed(same_uy, c_aq) * swap_u(swap_y(g0))
    h = h + signed(tu == tv_row, c_ab) * swap_u(over) + signed(ty == tv_row, c_bq) * swap_y(over)
    rows += [h, jnp.zeros((8, LW), F32)]
    hmat[...] = jnp.concatenate(rows, axis=0).astype(BF16)

    def m_copy(slot, to):
        return pltpu.make_async_remote_copy(
            src_ref=msgs.at[to],
            dst_ref=mrecv.at[slot],
            send_sem=m_send,
            recv_sem=m_recv,
            device_id=(ia, to),
            device_id_type=MESH,
        )

    def message_of(d, cols):
        zc, zs = zz[0:8, cols], zz[8:16, cols]
        vs = (None, vb[0:8, cols], vb[8:16, cols])
        single = d[96:104, :] * vv[:, cols]
        parts = []
        for c in range(2):
            s = jnp.where((sub < 3) == (c == 0), single, 0.0)
            for v in range(3):
                r = 48 * c + 16 * v
                e = d[r : r + 8, :] * zc + d[r + 8 : r + 16, :] * zs
                s = s + (e if v == 0 else e * vs[v])
            s = jnp.sum(s, axis=0, keepdims=True)
            parts += [s[:, 128 * i : 128 * (i + 1)] for i in range(CHUNK // 128)]
        return jnp.concatenate(parts, axis=0).astype(BF16)

    def send_messages(i, _):
        to = [partner(GROUP * i + k) for k in range(GROUP)]
        cols = [pl.ds(pl.multiple_of(j * CHUNK, CHUNK), CHUNK) for j in to]
        ds = [jnp.dot(hmat[...], yu[:, c], preferred_element_type=F32) for c in cols]
        for k in range(GROUP):
            msgs[to[k]] = message_of(ds[k], cols[k])

            @pl.when(to[k] != ik)
            def _():
                m_copy(ik, to[k]).start()
        return 0

    lax.fori_loop(0, n_ka // GROUP, send_messages, 0)
    mrecv[ik] = msgs[ik]
    eye = iota((64, 64), 0) == iota((64, 64), 1)
    gain = jnp.sum(jnp.where(eye, jnp.broadcast_to(gain_ref[...], (64, 64)), 0.0), axis=1, keepdims=True)

    def all_messages():
        return pltpu.make_async_remote_copy(
            src_ref=mrecv.at[0 : n_ka - 1],
            dst_ref=mrecv.at[0 : n_ka - 1],
            send_sem=m_send,
            recv_sem=m_recv,
            device_id=(ia, ik),
            device_id_type=MESH,
        )

    all_messages().wait_recv()

    mflat[...] = mrecv[...].astype(F32).reshape(mflat.shape)
    message = jnp.concatenate(
        [mflat[pl.ds(i, 64, stride=4), :] for i in range(local // 128)], axis=1
    )
    mean_sq = jnp.sum(message * message, axis=0, keepdims=True) * (1.0 / 64.0)
    normed = (message * lax.rsqrt(mean_sq + 1e-06) * gain).astype(BF16)
    hidden = lax.dot_general(up_ref[...], normed, (((0,), (0,)), ((), ())), preferred_element_type=F32)
    hidden = (hidden / (1.0 + jnp.exp(-hidden))).astype(BF16)
    update = jnp.dot(down_ref[...], hidden, preferred_element_type=F32)
    out_ref[...] = (feat_loc[...].astype(F32) + update).astype(BF16)

    all_z.wait_send()
    all_y.wait_send()
    all_messages().wait_send()
    all_g(0).wait_send()


def solution(mesh):
    n_atom, n_ka = mesh.shape["atom"], mesh.shape["ka"]
    ny, nz = 4, n_ka // 4

    def body(positions, features, species, miller, species_table, filter_weight, norm_gain, up_weight, down_weight):
        channels, atoms = features.shape
        local = atoms // n_ka
        n_vectors = miller.shape[1] * n_ka
        hid = up_weight.shape[0]
        scaling = 1.0 / math.sqrt(atoms * n_atom * n_vectors)
        any_space = pl.BlockSpec(memory_space=pltpu.HBM)
        return pl.pallas_call(
            functools.partial(body_kernel, (n_atom, n_ka, ny, nz, atoms, scaling)),
            out_shape=jax.ShapeDtypeStruct((channels, local), BF16),
            in_specs=[any_space] * 9,
            out_specs=pl.BlockSpec(memory_space=pltpu.VMEM),
            scratch_shapes=[
                pltpu.VMEM((3, atoms), F32),
                pltpu.VMEM((1, atoms), jnp.int32),
                pltpu.VMEM((3, 128), jnp.int32),
                pltpu.VMEM((NSPEC, channels), F32),
                pltpu.VMEM((NRBF, channels), F32),
                pltpu.VMEM((1, channels), F32),
                pltpu.VMEM((channels, hid), BF16),
                pltpu.VMEM((channels, hid), BF16),
                pltpu.VMEM((8, atoms), BF16),
                pltpu.VMEM((channels, local), BF16),
                pltpu.VMEM((LW, atoms), BF16),
                pltpu.VMEM((SR, atoms), BF16),
                pltpu.VMEM((16, atoms), F32),
                pltpu.VMEM((16, atoms), F32),
                pltpu.VMEM((8, atoms), F32),
                pltpu.VMEM((16, CHUNK), F32),
                pltpu.VMEM((SR, LW), F32),
                pltpu.VMEM((GR, LW), BF16),
                pltpu.VMEM((n_atom, GR, LW), BF16),
                pltpu.VMEM((8, n_vectors), BF16),
                pltpu.VMEM((SR, LW), BF16),
                pltpu.VMEM((n_ka, 8, 128), BF16),
                pltpu.VMEM((n_ka, 8, 128), BF16),
                pltpu.VMEM((n_ka * 8, 128), F32),
                pltpu.SemaphoreType.DMA((10,)),
                pltpu.SemaphoreType.DMA((2,)),
                pltpu.SemaphoreType.DMA((2,)),
                pltpu.SemaphoreType.DMA((1,)),
                pltpu.SemaphoreType.DMA((1,)),
                pltpu.SemaphoreType.DMA,
                pltpu.SemaphoreType.DMA,
            ],
            compiler_params=pltpu.CompilerParams(
                collective_id=0, has_side_effects=True, vmem_limit_bytes=24 * 1024 * 1024
            ),
            name="ewald",
        )(*[pltpu.with_memory_space_constraint(v, pltpu.HBM) for v in (
            positions,
            features,
            species.reshape(1, atoms),
            miller,
            species_table.T,
            filter_weight.T,
            norm_gain.reshape(1, channels),
            up_weight.T,
            down_weight,
        )])

    in_specs = (P(None, "atom"), P(None, "atom"), P("atom"), P(None, "ka"), P(), P(), P(), P(), P())
    out_specs = P(None, ("atom", "ka"))
    return jax.shard_map(body, mesh=mesh, in_specs=in_specs, out_specs=out_specs, check_vma=False)
```

```python
import functools
import math

import jax
import jax.numpy as jnp
from jax import lax
from jax.experimental import pallas as pl
from jax.experimental.pallas import tpu as pltpu
from jax.sharding import PartitionSpec as P

MESH = pl.DeviceIdType.MESH
F32, BF16 = jnp.float32, jnp.bfloat16
NRBF = 16
NSPEC = 8
MAXM = 8
LW = 128
SR = 112
GR = 104
CHUNK = 512
EARLY = 6
K_CUTOFF = 14.0

def _fit():
    import numpy as np

    n = 400
    u = 0.125 + 0.125 * np.cos(np.pi * (np.arange(n) + 0.5) / n)
    r = np.sqrt(u)
    c = np.polynomial.chebyshev.Chebyshev.fit(u, np.cos(2 * np.pi * r), 4, domain=[0, 0.25])
    s = np.polynomial.chebyshev.Chebyshev.fit(u, np.sin(2 * np.pi * r) / r, 4, domain=[0, 0.25])
    return (
        [float(v) for v in c.convert(kind=np.polynomial.Polynomial).coef],
        [float(v) for v in s.convert(kind=np.polynomial.Polynomial).coef],
    )


COS_COEF, SIN_COEF = _fit()


def poly(u, coef):
    acc = jnp.full_like(u, coef[-1])
    for c in coef[-2::-1]:
        acc = acc * u + c
    return acc


def harmonics(row, orders):
    t = row * orders
    r = t - jnp.round(t)
    u = r * r
    return poly(u, COS_COEF), r * poly(u, SIN_COEF)


def iota(shape, axis):
    return lax.broadcasted_iota(jnp.int32, shape, axis)


def lane_orders(shape, axis):
    lane = iota(shape, axis)
    main = lane < 112
    u = jnp.where(main, lane >> 4, lane - 112)
    tu = jnp.where((u >= 3) & (u < 6), 1, 0)
    a = jnp.where(u < 3, u + 1, jnp.where(u < 6, u - 2, 0))
    ty = jnp.where(main, (lane >> 3) & 1, 0)
    q = jnp.where(main, (lane & 7) + 1, 0)
    return tu, a, ty, q, lane < 119


def swap_y(x):
    lane = iota(x.shape, 1)
    s = jnp.where((lane & 8) == 0, pltpu.roll(x, 120, 1), pltpu.roll(x, 8, 1))
    return jnp.where(lane < 112, s, 0.0)


def swap_u(x):
    lane = iota(x.shape, 1)
    s = jnp.where(lane < 48, pltpu.roll(x, 80, 1), jnp.where(lane < 96, pltpu.roll(x, 48, 1), 0.0))
    s = jnp.where((lane >= 112) & (lane < 115), pltpu.roll(x, 125, 1), s)
    return jnp.where((lane >= 115) & (lane < 118), pltpu.roll(x, 3, 1), s)


def signed(same, w):
    return jnp.where(same, -w, w)


GROUP = 4
PAD = 128


def body_kernel(
    sizes,
    pos_hbm,
    feat_hbm,
    species_hbm,
    miller_hbm,
    tab_hbm,
    fw_hbm,
    gain_hbm,
    up_hbm,
    down_hbm,
    out_ref,
    pos_ref,
    species_ref,
    miller_ref,
    tab_ref,
    fw_ref,
    gain_ref,
    up_ref,
    down_ref,
    feat_blk,
    feat_loc,
    yu,
    sz,
    zz,
    vb,
    vv,
    xrows,
    counts_ref,
    up_pad,
    hmat_b,
    gsend,
    grecv,
    mil_all,
    hmat,
    msgs,
    mrecv,
    mflat,
    local_sem,
    mil_send,
    mil_recv,
    g_send,
    g_recv,
    m_send,
    m_recv,
):
    n_atom, n_ka, ny, nz, atoms, scaling = sizes
    ia, ik = lax.axis_index("atom"), lax.axis_index("ka")
    local = atoms // n_ka
    n_chunks = atoms // CHUNK
    n_vec = n_ka * 128

    barrier = pltpu.get_barrier_semaphore()

    iy, iz = ik // nz, lax.rem(ik, nz)

    def along_y(d):
        return lax.rem(iy + d, ny) * nz + iz

    def along_z(d):
        return iy * nz + lax.rem(iz + d, nz)

    def greet_z(d, _):
        pl.semaphore_signal(barrier, inc=1, device_id=(ia, along_z(d)), device_id_type=MESH)
        return 0

    def greet_y(d, _):
        pl.semaphore_signal(barrier, inc=1, device_id=(ia, along_y(d)), device_id_type=MESH)
        return 0

    def greet_atom(d, _):
        pl.semaphore_signal(barrier, inc=1, device_id=(lax.rem(ia + d, n_atom), ik), device_id_type=MESH)
        return 0

    loads = []
    for i, (src, dst) in enumerate(
        [
            (pos_hbm, pos_ref),
            (species_hbm, species_ref),
            (feat_hbm.at[pl.ds(pl.multiple_of((ik // 4) * 8, 8), 8), :], feat_blk),
            (tab_hbm, tab_ref),
            (miller_hbm, miller_ref),
            (fw_hbm, fw_ref),
            (gain_hbm, gain_ref),
            (up_hbm, up_ref),
            (down_hbm, down_ref),
            (feat_hbm.at[:, pl.ds(pl.multiple_of(ik * local, local), local)], feat_loc),
        ]
    ):
        copy = pltpu.make_async_copy(src, dst, local_sem.at[i])
        copy.start()
        loads.append(copy)
    lax.fori_loop(1, nz, greet_z, 0)
    lax.fori_loop(1, ny, greet_y, 0)
    lax.fori_loop(1, n_atom, greet_atom, 0)

    first = pl.ds(0, 2 * CHUNK)
    yu[:, first] = jnp.zeros((LW, 2 * CHUNK), BF16)
    sz[:, first] = jnp.zeros((SR, 2 * CHUNK), BF16)
    sub = iota((8, CHUNK), 0)
    orders = (sub + 1).astype(F32)
    third = jnp.where(sub < 3, sub, sub - 3)
    x_orders = jnp.where(sub < 6, 3 * third + 3, 1).astype(F32)
    for copy in loads[:5]:
        copy.wait()
    mil_all[:, pl.ds(pl.multiple_of(ik * 128, 128), 128)] = jnp.concatenate(
        [miller_ref[...].astype(F32), jnp.zeros((5, 128), F32)], axis=0
    ).astype(BF16)
    column = iota((NSPEC, 64), 1)
    tabs = [
        jnp.broadcast_to(
            jnp.sum(jnp.where(column == 2 * ik + c, tab_ref[...], 0.0), axis=1, keepdims=True), (8, CHUNK)
        )
        for c in range(2)
    ]
    which = [sub == lax.rem(2 * ik, 8) + c for c in range(2)]

    def row_of(i):
        return jnp.broadcast_to(xrows[i : i + 1, :], (8, CHUNK))

    def store(ref, r0, cols, upper, lower):
        ref[r0 : r0 + 16, cols] = jnp.concatenate([upper, lower], axis=0).astype(BF16)

    def twice(x):
        return jnp.concatenate([x, x], axis=0).astype(BF16)

    def tile(ref, j):
        return ref[:, pl.ds(pl.multiple_of(j * 256, 256), 256)]

    def multiply(accs, j):
        for i in range(2):
            pltpu.matmul_push_rhs(
                jnp.concatenate([tile(yu, 4 * j + 2 * i), tile(yu, 4 * j + 2 * i + 1)], axis=0), 0, i, transpose=True
            )
            pltpu.matmul_acc_lhs(accs[2 * i], tile(sz, 4 * j + 2 * i), load_staged_rhs=0)
            pltpu.matmul_acc_lhs(accs[2 * i + 1], tile(sz, 4 * j + 2 * i + 1))

    def diagonal(accs):
        total = 0.0
        for i, acc in enumerate(accs):
            total = total + pltpu.matmul_pop(acc)[:, LW * (i % 2) : LW * (i % 2) + LW]
        return total

    def gather_chunk(j, _):
        cols = pl.ds(pl.multiple_of(j * CHUNK, CHUNK), CHUNK)
        xc, xs = harmonics(jnp.broadcast_to(pos_ref[0:1, cols], (8, CHUNK)), x_orders)
        xrows[0:8, :] = xc
        xrows[8:16, :] = xs
        yc, ys = harmonics(jnp.broadcast_to(pos_ref[1:2, cols], (8, CHUNK)), orders)
        zc, zs = harmonics(jnp.broadcast_to(pos_ref[2:3, cols], (8, CHUNK)), orders)
        vc, vs = row_of(6), row_of(14)
        ones = jnp.where(third == 1, vc, jnp.where(third == 2, vs, 1.0))
        ones = jnp.where(sub < 6, ones, 0.0)
        zero = jnp.zeros((8, CHUNK), F32)
        y16 = jnp.concatenate([yc, ys], axis=0).astype(BF16)
        zz[0:8, cols] = zc
        zz[8:16, cols] = zs
        vb[0:8, cols] = vc
        vb[8:16, cols] = vs
        vv[:, cols] = ones
        for i, r in enumerate((0, 1, 2, 11, 12, 13)):
            u = row_of(r)
            yu[16 * i : 16 * i + 16, cols] = twice(u) * y16
        yu[96:112, cols] = y16
        store(
            yu, 112, cols, jnp.where(sub < 3, xc, jnp.where(sub < 6, xs, jnp.where(sub == 6, 1.0, 0.0))), zero
        )
        fb = feat_blk[:, cols].astype(F32)
        hot = jnp.broadcast_to(species_ref[0:1, cols], (8, CHUNK)) == sub
        sources = []
        vc16, vs16 = twice(vc), twice(vs)
        for c in range(2):
            s = jnp.where(which[c], fb, 0.0) + jnp.where(hot, tabs[c], 0.0)
            s = jnp.broadcast_to(jnp.sum(s, axis=0, keepdims=True), (8, CHUNK))
            s = s.astype(BF16).astype(F32)
            sources.append(s)
            szc, szs = s * zc, s * zs
            s16 = jnp.concatenate([szc, szs], axis=0).astype(BF16)
            sz[48 * c : 48 * c + 16, cols] = s16
            sz[48 * c + 16 : 48 * c + 32, cols] = s16 * vc16
            sz[48 * c + 32 : 48 * c + 48, cols] = s16 * vs16
        store(sz, 96, cols, jnp.where(sub < 3, sources[0], sources[1]) * ones, zero)
        return 0

    def mil_copy(ref, to, stage):
        return pltpu.make_async_remote_copy(
            src_ref=ref,
            dst_ref=ref,
            send_sem=mil_send.at[stage],
            recv_sem=mil_recv.at[stage],
            device_id=(ia, to),
            device_id_type=MESH,
        )

    own = mil_all.at[:, pl.ds(pl.multiple_of(ik * 128, 128), 128)]
    own_row = mil_all.at[:, pl.ds(pl.multiple_of(iy * (nz * 128), nz * 128), nz * 128)]
    all_z = mil_copy(mil_all.at[:, 0 : (nz - 1) * 128], ik, 0)
    all_y = mil_copy(mil_all.at[:, 0 : (ny - 1) * nz * 128], ik, 1)

    def farther(k, n):
        return n // 2 + (1 - 2 * lax.rem(k, 2)) * ((k + 1) // 2)

    def partner(i):
        dz, dy = farther(i // ny, nz), farther(lax.rem(i, ny), ny)
        y, z = lax.rem(ik // nz + dy, ny), lax.rem(lax.rem(ik, nz) + dz, nz)
        return y * nz + z

    def send_z(i, _):
        mil_copy(own, along_z(farther(i, nz)), 0).start()
        return 0

    def send_y(d, _):
        mil_copy(own_row, along_y(d), 1).start()
        return 0

    def gather(*accs):
        def step(j, _):
            multiply(accs, jnp.maximum(j - 1, 0))
            gather_chunk(2 * j, 0)
            gather_chunk(2 * j + 1, 0)
            return 0

        lax.fori_loop(0, EARLY, step, 0)
        pl.semaphore_wait(barrier, nz - 1 + ny - 1 + n_atom - 1)
        lax.fori_loop(0, nz - 1, send_z, 0)
        lax.fori_loop(EARLY, n_chunks // 2, step, 0)
        multiply(accs, n_chunks // 2 - 1)
        gsend[...] = diagonal(accs)[0:GR, :].astype(BF16)

    def accumulators(rows, times):
        return [pltpu.ACC(i)((rows, 256), F32) for i in range(2) for _ in range(times)]

    pl.run_scoped(gather, *accumulators(SR, 2))

    halves = ((0, SR, GR),)

    def g_copy(half, slot, to):
        lo, _, hi = halves[half]
        return pltpu.make_async_remote_copy(
            src_ref=gsend.at[lo:hi],
            dst_ref=grecv.at[slot, lo:hi],
            send_sem=g_send.at[half],
            recv_sem=g_recv.at[half],
            device_id=(to, ik),
            device_id_type=MESH,
        )

    def all_g(half):
        lo, _, hi = halves[half]
        part = grecv.at[0 : n_atom - 1, lo:hi]
        return pltpu.make_async_remote_copy(
            src_ref=part,
            dst_ref=part,
            send_sem=g_send.at[half],
            recv_sem=g_recv.at[half],
            device_id=(ia, ik),
            device_id_type=MESH,
        )

    def send_g(i, _):
        g_copy(0, ia, lax.rem(ia + 1 + lax.rem(i + 2, n_atom - 1), n_atom)).start()
        return 0

    lax.fori_loop(0, n_atom - 1, send_g, 0)

    for copy in loads[5:]:
        copy.wait()
    sub1 = iota((8, 128), 0)
    r8 = (sub1 + 1).astype(F32)
    column = iota((NRBF, 64), 1)
    weights = [
        jnp.sum(jnp.where(column == 2 * ik + c, fw_ref[...], 0.0), axis=1, keepdims=True) * scaling
        for c in range(2)
    ]
    tu, a, ty, q, _ = lane_orders((8, 128), 1)
    af, qq = a.astype(F32) * 3.0, (q * q).astype(F32)
    third1 = jnp.where(sub1 < 3, sub1, sub1 - 3)
    b_row = jnp.where((third1 > 0) & (sub1 < 6), 1.0, 0.0)
    tv_row = jnp.where(third1 == 2, 1, 0)

    def radial_of(m, r):
        mag = jnp.sqrt(m * m + qq + r * r)
        acc = [jnp.zeros((8, 128), F32) for _ in range(2)]
        for b in range(NRBF):
            z = (mag - b * (K_CUTOFF / (NRBF - 1))) * (NRBF / K_CUTOFF)
            e = jnp.exp(-(z * z))
            for c in range(2):
                acc[c] = acc[c] + weights[c][b : b + 1, :] * e
        return acc

    zero1 = jnp.zeros((8, 128), F32)
    rad_0 = radial_of(af, r8)
    rad_p, rad_m = radial_of(af + 1.0, r8), radial_of(af - 1.0, r8)
    single_p, single_m = [
        jnp.where(sub1 < 3, v[0], v[1]) for v in (radial_of(af + b_row, zero1), radial_of(af - b_row, zero1))
    ]

    all_z.wait_recv()
    lax.fori_loop(1, ny, send_y, 0)

    all_y.wait_recv()
    _, a_r, _, q_r, used = lane_orders((LW, CHUNK), 0)
    codes = jnp.where(used, a_r * 9 + q_r, -1).astype(F32)
    b_sub = jnp.where(third == 0, 0.0, 1.0)
    b_sub = jnp.where(sub < 6, b_sub, -1.0)
    def count(*accs):
        for j in range(n_vec // CHUNK):
            m = mil_all[:, CHUNK * j : CHUNK * (j + 1)].astype(F32)
            mx, my, mz = [jnp.broadcast_to(m[i : i + 1, :], (8, CHUNK)) for i in range(3)]
            ma = jnp.round(mx * (1.0 / 3.0))
            mb = mx - 3.0 * ma
            ga, gb, gy, gz = [jnp.where(v < 0, -1.0, 1.0) for v in (ma, mb, my, mz)]
            code = jnp.abs(ma) * 9.0 + jnp.abs(my)
            hot_uy = jnp.where(codes == jnp.broadcast_to(code[0:1, :], (LW, CHUNK)), 1.0, 0.0).astype(BF16)
            ab, ar, br, aq, bq, qr = ga * gb, ga * gz, gb * gz, ga * gy, gb * gy, gy * gz
            az, absb = jnp.abs(mz), jnp.abs(mb)
            hz = jnp.where(az == orders, 1.0, 0.0)
            h1 = hz * absb
            h0 = hz - h1
            hs = jnp.where((az == 0.0) & (absb == b_sub), 1.0, 0.0)
            wr = jnp.concatenate(
                [h1, h1 * ab, h1 * ar, h1 * br, h1 * aq, h1 * bq, h1 * qr, h1 * (ab * qr)]
                + [h0, h0 * aq, h0 * ar, h0 * qr]
                + [hs, hs * ab, hs * aq, hs * bq],
                axis=0,
            ).astype(BF16)
            pltpu.matmul_push_rhs(
                jnp.concatenate([hot_uy[:, 0:256], hot_uy[:, 256:512]], axis=0), (j // 2) % 2, j % 2, transpose=True
            )
            pltpu.matmul_acc_lhs(accs[2 * (j % 2)], wr[:, 0:256], load_staged_rhs=(j // 2) % 2)
            pltpu.matmul_acc_lhs(accs[2 * (j % 2) + 1], wr[:, 256:512])
        counts_ref[...] = diagonal(accs)

    pl.run_scoped(count, *accumulators(128, 2))
    counts = counts_ref[...]
    w = [counts[8 * i : 8 * i + 8, :] for i in range(16)]

    def mixed(plus, minus, plain, crossed):
        half_s, half_d = 0.5 * (plus + minus), 0.5 * (plus - minus)
        return half_s * plain + half_d * crossed, half_s * crossed + half_d * plain

    same_uy = tu == ty
    plain, coefs = [], []
    for t in range(2):
        plain.append((w[8], signed(same_uy, w[9]), signed(tu == t, w[10]), signed(ty == t, w[11])))
    for c in range(2):
        c_0, c_ab = mixed(rad_p[c], rad_m[c], w[0], w[1])
        c_ar, c_br = mixed(rad_p[c], rad_m[c], w[2], w[3])
        c_aq, c_bq = mixed(rad_p[c], rad_m[c], w[4], w[5])
        c_qr, c_all = mixed(rad_p[c], rad_m[c], w[6], w[7])
        at = lambda types, x: [signed(types == t, x) for t in range(2)]
        coefs.append(
            (c_0, signed(same_uy, c_aq), at(tu, c_ar), at(ty, c_qr), at(tu, c_ab), at(ty, c_bq), c_br)
            + ([signed(tu != ty, c_all), signed(same_uy, c_all)],)
        )
    s_0, s_ab = mixed(single_p, single_m, w[12], w[13])
    s_aq, s_bq = mixed(single_p, single_m, w[14], w[15])
    s_aq, s_ab, s_bq = signed(same_uy, s_aq), signed(tu == tv_row, s_ab), signed(ty == tv_row, s_bq)

    all_g(0).wait_recv()
    grecv[ia] = gsend[...]
    g = grecv[0].astype(F32)
    for i in range(1, n_atom):
        g = g + grecv[i].astype(F32)

    rows = []
    for c in range(2):
        gb = [[g[48 * c + 16 * v + 8 * t : 48 * c + 16 * v + 8 * t + 8, :] for t in range(2)] for v in range(3)]
        gu = [[swap_u(x) for x in pair] for pair in gb]
        gy = [[swap_y(x) for x in pair] for pair in gb]
        guy = [[swap_u(x) for x in pair] for pair in gy]
        for t in range(2):
            p_0, p_aq, p_ar, p_qr = plain[t]
            h = p_0 * gb[0][t] + p_aq * guy[0][t] + p_ar * gu[0][1 - t] + p_qr * gy[0][1 - t]
            rows.append(h * rad_0[c])
        c_0, c_aq, c_ar, c_qr, c_ab, c_bq, c_br, c_all = coefs[c]
        for v in (1, 2):
            tv, o = v - 1, 3 - v
            for t in range(2):
                h = c_0 * gb[v][t] + c_aq * guy[v][t] + c_ar[t] * gu[v][1 - t] + c_qr[t] * gy[v][1 - t]
                h = h + c_ab[tv] * gu[o][t] + c_bq[tv] * gy[o][t]
                cross = c_br * gb[o][1 - t]
                h = h - cross if tv == t else h + cross
                rows.append(h + c_all[(tv + t) % 2] * guy[o][1 - t])
    g0 = g[96:104, :]
    over = jnp.where(third1 == 1, pltpu.roll(g0, 7, 0), pltpu.roll(g0, 1, 0))
    over = jnp.where(b_row > 0.0, over, 0.0)
    h = s_0 * g0 + s_aq * swap_u(swap_y(g0)) + s_ab * swap_u(over) + s_bq * swap_y(over)
    rows += [h, jnp.zeros((8, LW), F32)]
    h16 = jnp.concatenate(rows, axis=0).astype(BF16)
    hmat[...] = jnp.concatenate([h16, jnp.zeros_like(h16)], axis=1)
    hmat_b[...] = jnp.concatenate([jnp.zeros_like(h16), h16], axis=1)

    def m_copy(slot, to):
        return pltpu.make_async_remote_copy(
            src_ref=msgs.at[to],
            dst_ref=mrecv.at[slot],
            send_sem=m_send,
            recv_sem=m_recv,
            device_id=(ia, to),
            device_id_type=MESH,
        )

    def message_of(d, cols):
        zc, zs = zz[0:8, cols], zz[8:16, cols]
        vs = (None, vb[0:8, cols], vb[8:16, cols])
        single = d[96:104, :] * vv[:, cols]
        parts = []
        for c in range(2):
            s = jnp.where((sub < 3) == (c == 0), single, 0.0)
            for v in range(3):
                r = 48 * c + 16 * v
                e = d[r : r + 8, :] * zc + d[r + 8 : r + 16, :] * zs
                s = s + (e if v == 0 else e * vs[v])
            s = jnp.sum(s, axis=0, keepdims=True)
            parts += [s[:, 128 * i : 128 * (i + 1)] for i in range(CHUNK // 128)]
        return jnp.concatenate(parts, axis=0).astype(BF16)

    def send_messages(accs, i, _):
        to = [partner(GROUP * i + k) for k in range(GROUP)]
        cols = [pl.ds(pl.multiple_of(j * CHUNK, CHUNK), CHUNK) for j in to]
        for k in range(GROUP):
            pltpu.matmul_push_rhs(
                jnp.concatenate([tile(yu, 2 * to[k]), tile(yu, 2 * to[k] + 1)], axis=0), k // 2, k % 2
            )
            pair = accs[4 * (k % 2) + 2 * (k // 2) : 4 * (k % 2) + 2 * (k // 2) + 2]
            pltpu.matmul_acc_lhs(pair[0], hmat[...], load_staged_rhs=k // 2)
            pltpu.matmul_acc_lhs(pair[1], hmat_b[...])
        for k in range(GROUP):
            pair = accs[4 * (k % 2) + 2 * (k // 2) : 4 * (k % 2) + 2 * (k // 2) + 2]
            d = jnp.concatenate([pltpu.matmul_pop(v) for v in pair], axis=1)
            msgs[to[k]] = message_of(d, cols[k])

            @pl.when(to[k] != ik)
            def _():
                m_copy(ik, to[k]).start()
        return 0

    def send_all(*accs):
        lax.fori_loop(0, n_ka // GROUP, functools.partial(send_messages, accs), 0)

    pl.run_scoped(send_all, *accumulators(SR, 4))
    mrecv[ik] = msgs[ik]
    up_t = up_ref[...].astype(F32).T.astype(BF16)
    up_pad[...] = jnp.concatenate([up_t, jnp.zeros((up_t.shape[0], 192), BF16)], axis=1)
    eye = iota((64, 64), 0) == iota((64, 64), 1)
    gain = jnp.sum(jnp.where(eye, jnp.broadcast_to(gain_ref[...], (64, 64)), 0.0), axis=1, keepdims=True)

    def all_messages():
        return pltpu.make_async_remote_copy(
            src_ref=mrecv.at[0 : n_ka - 1],
            dst_ref=mrecv.at[0 : n_ka - 1],
            send_sem=m_send,
            recv_sem=m_recv,
            device_id=(ia, ik),
            device_id_type=MESH,
        )

    all_messages().wait_recv()

    mflat[...] = mrecv[...].astype(F32).reshape(mflat.shape)
    message = jnp.concatenate(
        [mflat[pl.ds(i, 64, stride=4), :] for i in range(local // 128)], axis=1
    )
    mean_sq = jnp.sum(message * message, axis=0, keepdims=True) * (1.0 / 64.0)
    normed = (message * lax.rsqrt(mean_sq + 1e-06) * gain).astype(BF16)
    normed = jnp.concatenate([normed, jnp.zeros((192, local), BF16)], axis=0)

    def node_update(*accs):
        for i in range(2):
            pltpu.matmul_push_rhs(normed[:, 256 * i : 256 * i + 256], 0, i)
            pltpu.matmul_acc_lhs(accs[2 * i], up_pad[...], load_staged_rhs=0)
        for i in range(2):
            half = 0.5 * pltpu.matmul_pop(accs[2 * i])
            hidden = (half + half * jnp.tanh(half)).astype(BF16)
            pltpu.matmul_push_rhs(hidden, 1, i)
            pltpu.matmul_acc_lhs(accs[2 * i + 1], down_ref[...], load_staged_rhs=1)
        for i in range(2):
            part = slice(256 * i, 256 * i + 256)
            out_ref[:, part] = (feat_loc[:, part].astype(F32) + pltpu.matmul_pop(accs[2 * i + 1])).astype(BF16)

    pl.run_scoped(
        node_update, *[pltpu.ACC(i)((n, 256), F32) for i in range(2) for n in (up_pad.shape[0], 64)]
    )
    all_z.wait_send()
    all_y.wait_send()
    all_messages().wait_send()
    all_g(0).wait_send()


def solution(mesh):
    n_atom, n_ka = mesh.shape["atom"], mesh.shape["ka"]
    ny, nz = 4, n_ka // 4

    def body(positions, features, species, miller, species_table, filter_weight, norm_gain, up_weight, down_weight):
        channels, atoms = features.shape
        local = atoms // n_ka
        n_vectors = miller.shape[1] * n_ka
        hid = up_weight.shape[0]
        scaling = 1.0 / math.sqrt(atoms * n_atom * n_vectors)
        any_space = pl.BlockSpec(memory_space=pltpu.HBM)
        return pl.pallas_call(
            functools.partial(body_kernel, (n_atom, n_ka, ny, nz, atoms, scaling)),
            out_shape=jax.ShapeDtypeStruct((channels, local), BF16),
            in_specs=[any_space] * 9,
            out_specs=pl.BlockSpec(memory_space=pltpu.VMEM),
            scratch_shapes=[
                pltpu.VMEM((3, atoms), F32),
                pltpu.VMEM((1, atoms), jnp.int32),
                pltpu.VMEM((3, 128), jnp.int32),
                pltpu.VMEM((NSPEC, channels), F32),
                pltpu.VMEM((NRBF, channels), F32),
                pltpu.VMEM((1, channels), F32),
                pltpu.VMEM((channels, hid), BF16),
                pltpu.VMEM((channels, hid), BF16),
                pltpu.VMEM((8, atoms), BF16),
                pltpu.VMEM((channels, local), BF16),
                pltpu.VMEM((LW, atoms + PAD), BF16),
                pltpu.VMEM((SR, atoms + PAD), BF16),
                pltpu.VMEM((16, atoms + PAD), F32),
                pltpu.VMEM((16, atoms + PAD), F32),
                pltpu.VMEM((8, atoms + PAD), F32),
                pltpu.VMEM((16, CHUNK), F32),
                pltpu.VMEM((128, LW), F32),
                pltpu.VMEM((hid, 256), BF16),
                pltpu.VMEM((SR, 256), BF16),
                pltpu.VMEM((GR, LW), BF16),
                pltpu.VMEM((n_atom, GR, LW), BF16),
                pltpu.VMEM((8, n_vectors), BF16),
                pltpu.VMEM((SR, 256), BF16),
                pltpu.VMEM((n_ka, 8, 128), BF16),
                pltpu.VMEM((n_ka, 8, 128), BF16),
                pltpu.VMEM((n_ka * 8, 128), F32),
                pltpu.SemaphoreType.DMA((10,)),
                pltpu.SemaphoreType.DMA((2,)),
                pltpu.SemaphoreType.DMA((2,)),
                pltpu.SemaphoreType.DMA((1,)),
                pltpu.SemaphoreType.DMA((1,)),
                pltpu.SemaphoreType.DMA,
                pltpu.SemaphoreType.DMA,
            ],
            compiler_params=pltpu.CompilerParams(
                collective_id=0, has_side_effects=True, vmem_limit_bytes=24 * 1024 * 1024
            ),
            name="ewald",
        )(*[pltpu.with_memory_space_constraint(v, pltpu.HBM) for v in (
            positions,
            features,
            species.reshape(1, atoms),
            miller,
            species_table.T,
            filter_weight.T,
            norm_gain.reshape(1, channels),
            up_weight.T,
            down_weight,
        )])

    in_specs = (P(None, "atom"), P(None, "atom"), P("atom"), P(None, "ka"), P(), P(), P(), P(), P())
    out_specs = P(None, ("atom", "ka"))
    return jax.shard_map(body, mesh=mesh, in_specs=in_specs, out_specs=out_specs, check_vma=False)
```

```python
import functools
import math

import jax
import jax.numpy as jnp
from jax import lax
from jax.experimental import pallas as pl
from jax.experimental.pallas import tpu as pltpu
from jax.sharding import PartitionSpec as P

MESH = pl.DeviceIdType.MESH
F32, BF16 = jnp.float32, jnp.bfloat16
NRBF = 16
NSPEC = 8
MAXM = 8
LW = 128
SR = 112
GR = 104
CHUNK = 512
EARLY = 6
K_CUTOFF = 14.0

def _fit():
    import numpy as np

    n = 400
    u = 0.125 + 0.125 * np.cos(np.pi * (np.arange(n) + 0.5) / n)
    r = np.sqrt(u)
    c = np.polynomial.chebyshev.Chebyshev.fit(u, np.cos(2 * np.pi * r), 4, domain=[0, 0.25])
    s = np.polynomial.chebyshev.Chebyshev.fit(u, np.sin(2 * np.pi * r) / r, 4, domain=[0, 0.25])
    return (
        [float(v) for v in c.convert(kind=np.polynomial.Polynomial).coef],
        [float(v) for v in s.convert(kind=np.polynomial.Polynomial).coef],
    )


COS_COEF, SIN_COEF = _fit()


def poly(u, coef):
    acc = jnp.full_like(u, coef[-1])
    for c in coef[-2::-1]:
        acc = acc * u + c
    return acc


def harmonics(row, orders):
    t = row * orders
    r = t - jnp.round(t)
    u = r * r
    return poly(u, COS_COEF), r * poly(u, SIN_COEF)


def iota(shape, axis):
    return lax.broadcasted_iota(jnp.int32, shape, axis)


def lane_orders(shape, axis):
    lane = iota(shape, axis)
    main = lane < 112
    u = jnp.where(main, lane >> 4, lane - 112)
    tu = jnp.where((u >= 3) & (u < 6), 1, 0)
    a = jnp.where(u < 3, u + 1, jnp.where(u < 6, u - 2, 0))
    ty = jnp.where(main, (lane >> 3) & 1, 0)
    q = jnp.where(main, (lane & 7) + 1, 0)
    return tu, a, ty, q, lane < 119


def swap_y(x):
    lane = iota(x.shape, 1)
    s = jnp.where((lane & 8) == 0, pltpu.roll(x, 120, 1), pltpu.roll(x, 8, 1))
    return jnp.where(lane < 112, s, 0.0)


def swap_u(x):
    lane = iota(x.shape, 1)
    s = jnp.where(lane < 48, pltpu.roll(x, 80, 1), jnp.where(lane < 96, pltpu.roll(x, 48, 1), 0.0))
    s = jnp.where((lane >= 112) & (lane < 115), pltpu.roll(x, 125, 1), s)
    return jnp.where((lane >= 115) & (lane < 118), pltpu.roll(x, 3, 1), s)


def signed(same, w):
    return jnp.where(same, -w, w)


PAD = 128


def body_kernel(
    sizes,
    pos_hbm,
    feat_hbm,
    species_hbm,
    miller_hbm,
    tab_hbm,
    fw_hbm,
    gain_hbm,
    up_hbm,
    down_hbm,
    out_ref,
    pos_ref,
    species_ref,
    miller_ref,
    tab_ref,
    fw_ref,
    gain_ref,
    up_ref,
    down_ref,
    feat_blk,
    feat_loc,
    yu,
    sz,
    zz,
    vb,
    vv,
    xrows,
    counts_ref,
    up_pad,
    hmat_b,
    gsend,
    grecv,
    mil_all,
    hmat,
    msgs,
    mrecv,
    mflat,
    local_sem,
    mil_send,
    mil_recv,
    g_send,
    g_recv,
    m_send,
    m_recv,
):
    n_atom, n_ka, ny, nz, atoms, scaling = sizes
    ia, ik = lax.axis_index("atom"), lax.axis_index("ka")
    local = atoms // n_ka
    n_chunks = atoms // CHUNK
    n_vec = n_ka * 128

    barrier = pltpu.get_barrier_semaphore()

    iy, iz = ik // nz, lax.rem(ik, nz)

    def along_y(d):
        return lax.rem(iy + d, ny) * nz + iz

    def along_z(d):
        return iy * nz + lax.rem(iz + d, nz)

    def greet_z(d, _):
        pl.semaphore_signal(barrier, inc=1, device_id=(ia, along_z(d)), device_id_type=MESH)
        return 0

    def greet_y(d, _):
        pl.semaphore_signal(barrier, inc=1, device_id=(ia, along_y(d)), device_id_type=MESH)
        return 0

    def greet_atom(d, _):
        pl.semaphore_signal(barrier, inc=1, device_id=(lax.rem(ia + d, n_atom), ik), device_id_type=MESH)
        return 0

    loads = []
    for i, (src, dst) in enumerate(
        [
            (pos_hbm, pos_ref),
            (species_hbm, species_ref),
            (feat_hbm.at[pl.ds(pl.multiple_of((ik // 4) * 8, 8), 8), :], feat_blk),
            (tab_hbm, tab_ref),
            (miller_hbm, miller_ref),
            (fw_hbm, fw_ref),
            (gain_hbm, gain_ref),
            (up_hbm, up_ref),
            (down_hbm, down_ref),
            (feat_hbm.at[:, pl.ds(pl.multiple_of(ik * local, local), local)], feat_loc),
        ]
    ):
        copy = pltpu.make_async_copy(src, dst, local_sem.at[i])
        copy.start()
        loads.append(copy)
    lax.fori_loop(1, nz, greet_z, 0)
    lax.fori_loop(1, ny, greet_y, 0)
    lax.fori_loop(1, n_atom, greet_atom, 0)

    first = pl.ds(0, 2 * CHUNK)
    yu[:, first] = jnp.zeros((LW, 2 * CHUNK), BF16)
    sz[:, first] = jnp.zeros((SR, 2 * CHUNK), BF16)
    sub = iota((8, CHUNK), 0)
    orders = (sub + 1).astype(F32)
    third = jnp.where(sub < 3, sub, sub - 3)
    x_orders = jnp.where(sub < 6, 3 * third + 3, 1).astype(F32)
    for copy in loads[:5]:
        copy.wait()
    mil_all[:, pl.ds(pl.multiple_of(ik * 128, 128), 128)] = jnp.concatenate(
        [miller_ref[...].astype(F32), jnp.zeros((5, 128), F32)], axis=0
    ).astype(BF16)
    column = iota((NSPEC, 64), 1)
    tabs = [
        jnp.broadcast_to(
            jnp.sum(jnp.where(column == 2 * ik + c, tab_ref[...], 0.0), axis=1, keepdims=True), (8, CHUNK)
        )
        for c in range(2)
    ]
    which = [sub == lax.rem(2 * ik, 8) + c for c in range(2)]

    def row_of(i):
        return jnp.broadcast_to(xrows[i : i + 1, :], (8, CHUNK))

    def store(ref, r0, cols, upper, lower):
        ref[r0 : r0 + 16, cols] = jnp.concatenate([upper, lower], axis=0).astype(BF16)

    def twice(x):
        return jnp.concatenate([x, x], axis=0).astype(BF16)

    def tile(ref, j):
        return ref[:, pl.ds(pl.multiple_of(j * 256, 256), 256)]

    def push(j):
        for i in range(2):
            pltpu.matmul_push_rhs(
                jnp.concatenate([tile(yu, 4 * j + 2 * i), tile(yu, 4 * j + 2 * i + 1)], axis=0), 0, i, transpose=True
            )

    def multiply(accs, j):
        for i in range(2):
            pltpu.matmul_acc_lhs(accs[2 * i], tile(sz, 4 * j + 2 * i), load_staged_rhs=0)
            pltpu.matmul_acc_lhs(accs[2 * i + 1], tile(sz, 4 * j + 2 * i + 1))

    def diagonal(accs):
        total = 0.0
        for i, acc in enumerate(accs):
            total = total + pltpu.matmul_pop(acc)[:, LW * (i % 2) : LW * (i % 2) + LW]
        return total

    def gather_chunk(j, _):
        cols = pl.ds(pl.multiple_of(j * CHUNK, CHUNK), CHUNK)
        xc, xs = harmonics(jnp.broadcast_to(pos_ref[0:1, cols], (8, CHUNK)), x_orders)
        xrows[0:8, :] = xc
        xrows[8:16, :] = xs
        yc, ys = harmonics(jnp.broadcast_to(pos_ref[1:2, cols], (8, CHUNK)), orders)
        zc, zs = harmonics(jnp.broadcast_to(pos_ref[2:3, cols], (8, CHUNK)), orders)
        vc, vs = row_of(6), row_of(14)
        ones = jnp.where(third == 1, vc, jnp.where(third == 2, vs, 1.0))
        ones = jnp.where(sub < 6, ones, 0.0)
        zero = jnp.zeros((8, CHUNK), F32)
        zz[0:8, cols] = zc
        zz[8:16, cols] = zs
        vb[0:8, cols] = vc
        vb[8:16, cols] = vs
        vv[:, cols] = ones
        for i, r in enumerate((0, 1, 2, 11, 12, 13)):
            u = row_of(r)
            store(yu, 16 * i, cols, u * yc, u * ys)
        store(yu, 96, cols, yc, ys)
        store(
            yu, 112, cols, jnp.where(sub < 3, xc, jnp.where(sub < 6, xs, jnp.where(sub == 6, 1.0, 0.0))), zero
        )
        fb = feat_blk[:, cols].astype(F32)
        hot = jnp.broadcast_to(species_ref[0:1, cols], (8, CHUNK)) == sub
        sources = []
        vc16, vs16 = twice(vc), twice(vs)
        for c in range(2):
            s = jnp.where(which[c], fb, 0.0) + jnp.where(hot, tabs[c], 0.0)
            s = jnp.broadcast_to(jnp.sum(s, axis=0, keepdims=True), (8, CHUNK))
            s = s.astype(BF16).astype(F32)
            sources.append(s)
            szc, szs = s * zc, s * zs
            s16 = jnp.concatenate([szc, szs], axis=0).astype(BF16)
            sz[48 * c : 48 * c + 16, cols] = s16
            sz[48 * c + 16 : 48 * c + 32, cols] = s16 * vc16
            sz[48 * c + 32 : 48 * c + 48, cols] = s16 * vs16
        store(sz, 96, cols, jnp.where(sub < 3, sources[0], sources[1]) * ones, zero)
        return 0

    def mil_copy(ref, to, stage):
        return pltpu.make_async_remote_copy(
            src_ref=ref,
            dst_ref=ref,
            send_sem=mil_send.at[stage],
            recv_sem=mil_recv.at[stage],
            device_id=(ia, to),
            device_id_type=MESH,
        )

    own = mil_all.at[:, pl.ds(pl.multiple_of(ik * 128, 128), 128)]
    own_row = mil_all.at[:, pl.ds(pl.multiple_of(iy * (nz * 128), nz * 128), nz * 128)]
    all_z = mil_copy(mil_all.at[:, 0 : (nz - 1) * 128], ik, 0)
    all_y = mil_copy(mil_all.at[:, 0 : (ny - 1) * nz * 128], ik, 1)

    def farther(k, n):
        return n // 2 + (1 - 2 * lax.rem(k, 2)) * ((k + 1) // 2)

    def send_z(i, _):
        mil_copy(own, along_z(farther(i, nz)), 0).start()
        return 0

    def send_y(d, _):
        mil_copy(own_row, along_y(d), 1).start()
        return 0

    def gather(*accs):
        def step(j, _):
            push(jnp.maximum(j - 1, 0))
            multiply(accs, jnp.maximum(j - 1, 0))
            gather_chunk(2 * j, 0)
            gather_chunk(2 * j + 1, 0)
            return 0

        lax.fori_loop(0, EARLY, step, 0)
        pl.semaphore_wait(barrier, nz - 1 + ny - 1 + n_atom - 1)
        lax.fori_loop(0, nz - 1, send_z, 0)
        lax.fori_loop(EARLY, n_chunks // 2, step, 0)
        push(n_chunks // 2 - 1)
        multiply(accs, n_chunks // 2 - 1)
        gsend[...] = diagonal(accs)[0:GR, :].astype(BF16)

    def accumulators(rows, times):
        return [pltpu.ACC(i)((rows, 256), F32) for i in range(2) for _ in range(times)]

    pl.run_scoped(gather, *accumulators(SR, 2))

    halves = ((0, SR, GR),)

    def g_copy(half, slot, to):
        lo, _, hi = halves[half]
        return pltpu.make_async_remote_copy(
            src_ref=gsend.at[lo:hi],
            dst_ref=grecv.at[slot, lo:hi],
            send_sem=g_send.at[half],
            recv_sem=g_recv.at[half],
            device_id=(to, ik),
            device_id_type=MESH,
        )

    def all_g(half):
        lo, _, hi = halves[half]
        part = grecv.at[0 : n_atom - 1, lo:hi]
        return pltpu.make_async_remote_copy(
            src_ref=part,
            dst_ref=part,
            send_sem=g_send.at[half],
            recv_sem=g_recv.at[half],
            device_id=(ia, ik),
            device_id_type=MESH,
        )

    def send_g(i, _):
        g_copy(0, ia, lax.rem(ia + 1 + lax.rem(i + 2, n_atom - 1), n_atom)).start()
        return 0

    lax.fori_loop(0, n_atom - 1, send_g, 0)

    for copy in loads[5:]:
        copy.wait()
    sub1 = iota((8, 128), 0)
    r8 = (sub1 + 1).astype(F32)
    column = iota((NRBF, 64), 1)
    weights = [
        jnp.sum(jnp.where(column == 2 * ik + c, fw_ref[...], 0.0), axis=1, keepdims=True) * scaling
        for c in range(2)
    ]
    tu, a, ty, q, _ = lane_orders((8, 128), 1)
    af, qq = a.astype(F32) * 3.0, (q * q).astype(F32)
    third1 = jnp.where(sub1 < 3, sub1, sub1 - 3)
    b_row = jnp.where((third1 > 0) & (sub1 < 6), 1.0, 0.0)
    tv_row = jnp.where(third1 == 2, 1, 0)

    def radial_of(m, r):
        mag = jnp.sqrt(m * m + qq + r * r)
        acc = [jnp.zeros((8, 128), F32) for _ in range(2)]
        for b in range(NRBF):
            z = (mag - b * (K_CUTOFF / (NRBF - 1))) * (NRBF / K_CUTOFF)
            e = jnp.exp(-(z * z))
            for c in range(2):
                acc[c] = acc[c] + weights[c][b : b + 1, :] * e
        return acc

    zero1 = jnp.zeros((8, 128), F32)
    rad_0 = radial_of(af, r8)
    rad_p, rad_m = radial_of(af + 1.0, r8), radial_of(af - 1.0, r8)
    single_p, single_m = [
        jnp.where(sub1 < 3, v[0], v[1]) for v in (radial_of(af + b_row, zero1), radial_of(af - b_row, zero1))
    ]

    all_z.wait_recv()
    lax.fori_loop(1, ny, send_y, 0)

    all_y.wait_recv()
    _, a_r, _, q_r, used = lane_orders((LW, CHUNK), 0)
    codes = jnp.where(used, a_r * 9 + q_r, -1).astype(F32)
    b_sub = jnp.where(third == 0, 0.0, 1.0)
    b_sub = jnp.where(sub < 6, b_sub, -1.0)
    def count(*accs):
        for j in range(n_vec // CHUNK):
            m = mil_all[:, CHUNK * j : CHUNK * (j + 1)].astype(F32)
            mx, my, mz = [jnp.broadcast_to(m[i : i + 1, :], (8, CHUNK)) for i in range(3)]
            ma = jnp.round(mx * (1.0 / 3.0))
            mb = mx - 3.0 * ma
            ga, gb, gy, gz = [jnp.where(v < 0, -1.0, 1.0) for v in (ma, mb, my, mz)]
            code = jnp.abs(ma) * 9.0 + jnp.abs(my)
            hot_uy = jnp.where(codes == jnp.broadcast_to(code[0:1, :], (LW, CHUNK)), 1.0, 0.0).astype(BF16)
            ab, ar, br, aq, bq, qr = ga * gb, ga * gz, gb * gz, ga * gy, gb * gy, gy * gz
            az, absb = jnp.abs(mz), jnp.abs(mb)
            hz = jnp.where(az == orders, 1.0, 0.0)
            h1 = hz * absb
            h0 = hz - h1
            hs = jnp.where((az == 0.0) & (absb == b_sub), 1.0, 0.0)
            wr = jnp.concatenate(
                [h1, h1 * ab, h1 * ar, h1 * br, h1 * aq, h1 * bq, h1 * qr, h1 * (ab * qr)]
                + [h0, h0 * aq, h0 * ar, h0 * qr]
                + [hs, hs * ab, hs * aq, hs * bq],
                axis=0,
            ).astype(BF16)
            pltpu.matmul_push_rhs(
                jnp.concatenate([hot_uy[:, 0:256], hot_uy[:, 256:512]], axis=0), (j // 2) % 2, j % 2, transpose=True
            )
            pltpu.matmul_acc_lhs(accs[2 * (j % 2)], wr[:, 0:256], load_staged_rhs=(j // 2) % 2)
            pltpu.matmul_acc_lhs(accs[2 * (j % 2) + 1], wr[:, 256:512])
        counts_ref[...] = diagonal(accs)

    pl.run_scoped(count, *accumulators(128, 2))
    counts = counts_ref[...]
    w = [counts[8 * i : 8 * i + 8, :] for i in range(16)]

    def mixed(plus, minus, plain, crossed):
        half_s, half_d = 0.5 * (plus + minus), 0.5 * (plus - minus)
        return half_s * plain + half_d * crossed, half_s * crossed + half_d * plain

    same_uy = tu == ty
    plain, coefs = [], []
    for t in range(2):
        plain.append((w[8], signed(same_uy, w[9]), signed(tu == t, w[10]), signed(ty == t, w[11])))
    for c in range(2):
        c_0, c_ab = mixed(rad_p[c], rad_m[c], w[0], w[1])
        c_ar, c_br = mixed(rad_p[c], rad_m[c], w[2], w[3])
        c_aq, c_bq = mixed(rad_p[c], rad_m[c], w[4], w[5])
        c_qr, c_all = mixed(rad_p[c], rad_m[c], w[6], w[7])
        at = lambda types, x: [signed(types == t, x) for t in range(2)]
        coefs.append(
            (c_0, signed(same_uy, c_aq), at(tu, c_ar), at(ty, c_qr), at(tu, c_ab), at(ty, c_bq), c_br)
            + ([signed(tu != ty, c_all), signed(same_uy, c_all)],)
        )
    s_0, s_ab = mixed(single_p, single_m, w[12], w[13])
    s_aq, s_bq = mixed(single_p, single_m, w[14], w[15])
    s_aq, s_ab, s_bq = signed(same_uy, s_aq), signed(tu == tv_row, s_ab), signed(ty == tv_row, s_bq)

    all_g(0).wait_recv()
    grecv[ia] = gsend[...]
    g = grecv[0].astype(F32)
    for i in range(1, n_atom):
        g = g + grecv[i].astype(F32)

    rows = []
    for c in range(2):
        gb = [[g[48 * c + 16 * v + 8 * t : 48 * c + 16 * v + 8 * t + 8, :] for t in range(2)] for v in range(3)]
        gu = [[swap_u(x) for x in pair] for pair in gb]
        gy = [[swap_y(x) for x in pair] for pair in gb]
        guy = [[swap_u(x) for x in pair] for pair in gy]
        for t in range(2):
            p_0, p_aq, p_ar, p_qr = plain[t]
            h = p_0 * gb[0][t] + p_aq * guy[0][t] + p_ar * gu[0][1 - t] + p_qr * gy[0][1 - t]
            rows.append(h * rad_0[c])
        c_0, c_aq, c_ar, c_qr, c_ab, c_bq, c_br, c_all = coefs[c]
        for v in (1, 2):
            tv, o = v - 1, 3 - v
            for t in range(2):
                h = c_0 * gb[v][t] + c_aq * guy[v][t] + c_ar[t] * gu[v][1 - t] + c_qr[t] * gy[v][1 - t]
                h = h + c_ab[tv] * gu[o][t] + c_bq[tv] * gy[o][t]
                cross = c_br * gb[o][1 - t]
                h = h - cross if tv == t else h + cross
                rows.append(h + c_all[(tv + t) % 2] * guy[o][1 - t])
    g0 = g[96:104, :]
    over = jnp.where(third1 == 1, pltpu.roll(g0, 7, 0), pltpu.roll(g0, 1, 0))
    over = jnp.where(b_row > 0.0, over, 0.0)
    h = s_0 * g0 + s_aq * swap_u(swap_y(g0)) + s_ab * swap_u(over) + s_bq * swap_y(over)
    rows += [h, jnp.zeros((8, LW), F32)]
    h16 = jnp.concatenate(rows, axis=0).astype(BF16)
    hmat[...] = jnp.concatenate([h16, jnp.zeros_like(h16)], axis=1)
    hmat_b[...] = jnp.concatenate([jnp.zeros_like(h16), h16], axis=1)

    def m_copy(slot, to):
        return pltpu.make_async_remote_copy(
            src_ref=msgs.at[to],
            dst_ref=mrecv.at[slot],
            send_sem=m_send,
            recv_sem=m_recv,
            device_id=(ia, to),
            device_id_type=MESH,
        )

    def message_of(d, cols):
        zc, zs = zz[0:8, cols], zz[8:16, cols]
        vs = (None, vb[0:8, cols], vb[8:16, cols])
        single = d[96:104, :] * vv[:, cols]
        parts = []
        for c in range(2):
            s = jnp.where((sub < 3) == (c == 0), single, 0.0)
            for v in range(3):
                r = 48 * c + 16 * v
                e = d[r : r + 8, :] * zc + d[r + 8 : r + 16, :] * zs
                s = s + (e if v == 0 else e * vs[v])
            s = jnp.sum(s, axis=0, keepdims=True)
            parts += [s[:, 128 * i : 128 * (i + 1)] for i in range(CHUNK // 128)]
        return jnp.concatenate(parts, axis=0).astype(BF16)

    def pair_of(accs, k):
        return accs[4 * (k % 2) + 2 * (k // 2) : 4 * (k % 2) + 2 * (k // 2) + 2]

    def issue(accs, k, j):
        pltpu.matmul_push_rhs(jnp.concatenate([tile(yu, 2 * j), tile(yu, 2 * j + 1)], axis=0), k // 2, k % 2)
        pair = pair_of(accs, k)
        pltpu.matmul_acc_lhs(pair[0], hmat[...], load_staged_rhs=k // 2)
        pltpu.matmul_acc_lhs(pair[1], hmat_b[...])

    y_rows = [lax.rem(iy + ny // 2 + (k + 1) // 2 * (1 - 2 * (k % 2)), ny) * nz for k in range(ny)]

    def z_of(i):
        return lax.rem(iz + farther(i, nz), nz)

    def send_group(accs, z, following):
        for k in range(ny):
            j = y_rows[k] + z
            d = jnp.concatenate([pltpu.matmul_pop(v) for v in pair_of(accs, k)], axis=1)
            if following is not None:
                issue(accs, k, y_rows[k] + following)
            msgs[j] = message_of(d, pl.ds(pl.multiple_of(j * CHUNK, CHUNK), CHUNK))
            if following is not None or k < ny - 1:
                m_copy(ik, j).start()

    def send_all(*accs):
        first = z_of(0)
        for k in range(ny):
            issue(accs, k, y_rows[k] + first)

        def step(i, z):
            following = z_of(i + 1)
            send_group(accs, z, following)
            return following

        send_group(accs, lax.fori_loop(0, nz - 1, step, first), None)

    pl.run_scoped(send_all, *accumulators(SR, 4))
    mrecv[ik] = msgs[ik]
    up_t = up_ref[...].astype(F32).T.astype(BF16)
    up_pad[...] = jnp.concatenate([up_t, jnp.zeros((up_t.shape[0], 192), BF16)], axis=1)
    eye = iota((64, 64), 0) == iota((64, 64), 1)
    gain = jnp.sum(jnp.where(eye, jnp.broadcast_to(gain_ref[...], (64, 64)), 0.0), axis=1, keepdims=True)

    def all_messages():
        return pltpu.make_async_remote_copy(
            src_ref=mrecv.at[0 : n_ka - 1],
            dst_ref=mrecv.at[0 : n_ka - 1],
            send_sem=m_send,
            recv_sem=m_recv,
            device_id=(ia, ik),
            device_id_type=MESH,
        )

    all_messages().wait_recv()

    mflat[...] = mrecv[...].astype(F32).reshape(mflat.shape)
    message = jnp.concatenate(
        [mflat[pl.ds(i, 64, stride=4), :] for i in range(local // 128)], axis=1
    )
    mean_sq = jnp.sum(message * message, axis=0, keepdims=True) * (1.0 / 64.0)
    normed = (message * lax.rsqrt(mean_sq + 1e-06) * gain).astype(BF16)
    normed = jnp.concatenate([normed, jnp.zeros((192, local), BF16)], axis=0)

    def node_update(*accs):
        for i in range(2):
            pltpu.matmul_push_rhs(normed[:, 256 * i : 256 * i + 256], 0, i)
            pltpu.matmul_acc_lhs(accs[2 * i], up_pad[...], load_staged_rhs=0)
        for i in range(2):
            half = 0.5 * pltpu.matmul_pop(accs[2 * i])
            hidden = (half + half * jnp.tanh(half)).astype(BF16)
            pltpu.matmul_push_rhs(hidden, 1, i)
            pltpu.matmul_acc_lhs(accs[2 * i + 1], down_ref[...], load_staged_rhs=1)
        for i in range(2):
            part = slice(256 * i, 256 * i + 256)
            out_ref[:, part] = (feat_loc[:, part].astype(F32) + pltpu.matmul_pop(accs[2 * i + 1])).astype(BF16)

    pl.run_scoped(
        node_update, *[pltpu.ACC(i)((n, 256), F32) for i in range(2) for n in (up_pad.shape[0], 64)]
    )
    all_z.wait_send()
    all_y.wait_send()
    all_messages().wait_send()
    all_g(0).wait_send()


def solution(mesh):
    n_atom, n_ka = mesh.shape["atom"], mesh.shape["ka"]
    ny, nz = 4, n_ka // 4

    def body(positions, features, species, miller, species_table, filter_weight, norm_gain, up_weight, down_weight):
        channels, atoms = features.shape
        local = atoms // n_ka
        n_vectors = miller.shape[1] * n_ka
        hid = up_weight.shape[0]
        scaling = 1.0 / math.sqrt(atoms * n_atom * n_vectors)
        any_space = pl.BlockSpec(memory_space=pltpu.HBM)
        return pl.pallas_call(
            functools.partial(body_kernel, (n_atom, n_ka, ny, nz, atoms, scaling)),
            out_shape=jax.ShapeDtypeStruct((channels, local), BF16),
            in_specs=[any_space] * 9,
            out_specs=pl.BlockSpec(memory_space=pltpu.VMEM),
            scratch_shapes=[
                pltpu.VMEM((3, atoms), F32),
                pltpu.VMEM((1, atoms), jnp.int32),
                pltpu.VMEM((3, 128), jnp.int32),
                pltpu.VMEM((NSPEC, channels), F32),
                pltpu.VMEM((NRBF, channels), F32),
                pltpu.VMEM((1, channels), F32),
                pltpu.VMEM((channels, hid), BF16),
                pltpu.VMEM((channels, hid), BF16),
                pltpu.VMEM((8, atoms), BF16),
                pltpu.VMEM((channels, local), BF16),
                pltpu.VMEM((LW, atoms + PAD), BF16),
                pltpu.VMEM((SR, atoms + PAD), BF16),
                pltpu.VMEM((16, atoms + PAD), F32),
                pltpu.VMEM((16, atoms + PAD), F32),
                pltpu.VMEM((8, atoms + PAD), F32),
                pltpu.VMEM((16, CHUNK), F32),
                pltpu.VMEM((128, LW), F32),
                pltpu.VMEM((hid, 256), BF16),
                pltpu.VMEM((SR, 256), BF16),
                pltpu.VMEM((GR, LW), BF16),
                pltpu.VMEM((n_atom, GR, LW), BF16),
                pltpu.VMEM((8, n_vectors), BF16),
                pltpu.VMEM((SR, 256), BF16),
                pltpu.VMEM((n_ka, 8, 128), BF16),
                pltpu.VMEM((n_ka, 8, 128), BF16),
                pltpu.VMEM((n_ka * 8, 128), F32),
                pltpu.SemaphoreType.DMA((10,)),
                pltpu.SemaphoreType.DMA((2,)),
                pltpu.SemaphoreType.DMA((2,)),
                pltpu.SemaphoreType.DMA((1,)),
                pltpu.SemaphoreType.DMA((1,)),
                pltpu.SemaphoreType.DMA,
                pltpu.SemaphoreType.DMA,
            ],
            compiler_params=pltpu.CompilerParams(
                collective_id=0, has_side_effects=True, vmem_limit_bytes=24 * 1024 * 1024
            ),
            name="ewald",
        )(*[pltpu.with_memory_space_constraint(v, pltpu.HBM) for v in (
            positions,
            features,
            species.reshape(1, atoms),
            miller,
            species_table.T,
            filter_weight.T,
            norm_gain.reshape(1, channels),
            up_weight.T,
            down_weight,
        )])

    in_specs = (P(None, "atom"), P(None, "atom"), P("atom"), P(None, "ka"), P(), P(), P(), P(), P())
    out_specs = P(None, ("atom", "ka"))
    return jax.shard_map(body, mesh=mesh, in_specs=in_specs, out_specs=out_specs, check_vma=False)
```

```python
import functools
import math

import jax
import jax.numpy as jnp
from jax import lax
from jax.experimental import pallas as pl
from jax.experimental.pallas import tpu as pltpu
from jax.sharding import PartitionSpec as P

MESH = pl.DeviceIdType.MESH
F32, BF16 = jnp.float32, jnp.bfloat16
NRBF = 16
NSPEC = 8
MAXM = 8
LW = 128
SR = 112
GR = 104
CHUNK = 512
DEPTH = 8192
EARLY = 12
K_CUTOFF = 14.0

def _fit():
    import numpy as np

    n = 400
    u = 0.125 + 0.125 * np.cos(np.pi * (np.arange(n) + 0.5) / n)
    r = np.sqrt(u)
    c = np.polynomial.chebyshev.Chebyshev.fit(u, np.cos(2 * np.pi * r), 4, domain=[0, 0.25])
    s = np.polynomial.chebyshev.Chebyshev.fit(u, np.sin(2 * np.pi * r) / r, 4, domain=[0, 0.25])
    return (
        [float(v) for v in c.convert(kind=np.polynomial.Polynomial).coef],
        [float(v) for v in s.convert(kind=np.polynomial.Polynomial).coef],
    )


COS_COEF, SIN_COEF = _fit()


def poly(u, coef):
    acc = jnp.full_like(u, coef[-1])
    for c in coef[-2::-1]:
        acc = acc * u + c
    return acc


def harmonics(row, orders):
    t = row * orders
    r = t - jnp.round(t)
    u = r * r
    return poly(u, COS_COEF), r * poly(u, SIN_COEF)


def iota(shape, axis):
    return lax.broadcasted_iota(jnp.int32, shape, axis)


def lane_orders(shape, axis):
    lane = iota(shape, axis)
    main = lane < 112
    u = jnp.where(main, lane >> 4, lane - 112)
    tu = jnp.where((u >= 3) & (u < 6), 1, 0)
    a = jnp.where(u < 3, u + 1, jnp.where(u < 6, u - 2, 0))
    ty = jnp.where(main, (lane >> 3) & 1, 0)
    q = jnp.where(main, (lane & 7) + 1, 0)
    return tu, a, ty, q, lane < 119


def swap_y(x):
    lane = iota(x.shape, 1)
    s = jnp.where((lane & 8) == 0, pltpu.roll(x, 120, 1), pltpu.roll(x, 8, 1))
    return jnp.where(lane < 112, s, 0.0)


def swap_u(x):
    lane = iota(x.shape, 1)
    s = jnp.where(lane < 48, pltpu.roll(x, 80, 1), jnp.where(lane < 96, pltpu.roll(x, 48, 1), 0.0))
    s = jnp.where((lane >= 112) & (lane < 115), pltpu.roll(x, 125, 1), s)
    return jnp.where((lane >= 115) & (lane < 118), pltpu.roll(x, 3, 1), s)


def signed(same, w):
    return jnp.where(same, -w, w)


PAD = 128


def body_kernel(
    sizes,
    pos_hbm,
    feat_hbm,
    species_hbm,
    miller_hbm,
    tab_hbm,
    fw_hbm,
    gain_hbm,
    up_hbm,
    down_hbm,
    out_ref,
    pos_ref,
    species_ref,
    miller_ref,
    tab_ref,
    fw_ref,
    gain_ref,
    up_ref,
    down_ref,
    feat_blk,
    feat_loc,
    yu,
    sz,
    zz,
    vb,
    vv,
    xrows,
    gacc,
    gsend,
    grecv,
    mil_all,
    hmat,
    msgs,
    mrecv,
    mflat,
    local_sem,
    mil_send,
    mil_recv,
    g_send,
    g_recv,
    m_send,
    m_recv,
):
    n_atom, n_ka, ny, nz, atoms, scaling = sizes
    ia, ik = lax.axis_index("atom"), lax.axis_index("ka")
    local = atoms // n_ka
    n_chunks = atoms // CHUNK
    n_vec = n_ka * 128

    barrier = pltpu.get_barrier_semaphore()

    iy, iz = ik // nz, lax.rem(ik, nz)

    def along_y(d):
        return lax.rem(iy + d, ny) * nz + iz

    def along_z(d):
        return iy * nz + lax.rem(iz + d, nz)

    def greet_z(d, _):
        pl.semaphore_signal(barrier, inc=1, device_id=(ia, along_z(d)), device_id_type=MESH)
        return 0

    def greet_y(d, _):
        pl.semaphore_signal(barrier, inc=1, device_id=(ia, along_y(d)), device_id_type=MESH)
        return 0

    def greet_atom(d, _):
        pl.semaphore_signal(barrier, inc=1, device_id=(lax.rem(ia + d, n_atom), ik), device_id_type=MESH)
        return 0

    loads = []
    for i, (src, dst) in enumerate(
        [
            (pos_hbm, pos_ref),
            (species_hbm, species_ref),
            (feat_hbm.at[pl.ds(pl.multiple_of((ik // 4) * 8, 8), 8), :], feat_blk),
            (tab_hbm, tab_ref),
            (miller_hbm, miller_ref),
            (fw_hbm, fw_ref),
            (gain_hbm, gain_ref),
            (up_hbm, up_ref),
            (down_hbm, down_ref),
            (feat_hbm.at[:, pl.ds(pl.multiple_of(ik * local, local), local)], feat_loc),
        ]
    ):
        copy = pltpu.make_async_copy(src, dst, local_sem.at[i])
        copy.start()
        loads.append(copy)
    lax.fori_loop(1, nz, greet_z, 0)
    lax.fori_loop(1, ny, greet_y, 0)
    lax.fori_loop(1, n_atom, greet_atom, 0)

    gacc[...] = jnp.zeros_like(gacc)
    sub = iota((8, CHUNK), 0)
    orders = (sub + 1).astype(F32)
    third = jnp.where(sub < 3, sub, sub - 3)
    x_orders = jnp.where(sub < 6, 3 * third + 3, 1).astype(F32)
    for copy in loads[:5]:
        copy.wait()
    mil_all[:, pl.ds(pl.multiple_of(ik * 128, 128), 128)] = jnp.concatenate(
        [miller_ref[...].astype(F32), jnp.zeros((5, 128), F32)], axis=0
    ).astype(BF16)
    column = iota((NSPEC, 64), 1)
    tabs = [
        jnp.broadcast_to(
            jnp.sum(jnp.where(column == 2 * ik + c, tab_ref[...], 0.0), axis=1, keepdims=True), (8, CHUNK)
        )
        for c in range(2)
    ]
    which = [sub == lax.rem(2 * ik, 8) + c for c in range(2)]

    def row_of(i):
        return jnp.broadcast_to(xrows[i : i + 1, :], (8, CHUNK))

    def store(ref, r0, cols, upper, lower):
        ref[r0 : r0 + 16, cols] = jnp.concatenate([upper, lower], axis=0).astype(BF16)

    def gather_chunk(j, _):
        cols = pl.ds(pl.multiple_of(j * CHUNK, CHUNK), CHUNK)
        xc, xs = harmonics(jnp.broadcast_to(pos_ref[0:1, cols], (8, CHUNK)), x_orders)
        xrows[0:8, :] = xc
        xrows[8:16, :] = xs
        yc, ys = harmonics(jnp.broadcast_to(pos_ref[1:2, cols], (8, CHUNK)), orders)
        zc, zs = harmonics(jnp.broadcast_to(pos_ref[2:3, cols], (8, CHUNK)), orders)
        vc, vs = row_of(6), row_of(14)
        ones = jnp.where(third == 1, vc, jnp.where(third == 2, vs, 1.0))
        ones = jnp.where(sub < 6, ones, 0.0)
        zero = jnp.zeros((8, CHUNK), F32)
        zz[0:8, cols] = zc
        zz[8:16, cols] = zs
        vb[0:8, cols] = vc
        vb[8:16, cols] = vs
        vv[:, cols] = ones
        for i, r in enumerate((0, 1, 2, 11, 12, 13)):
            u = row_of(r)
            store(yu, 16 * i, cols, u * yc, u * ys)
        store(yu, 96, cols, yc, ys)
        store(
            yu, 112, cols, jnp.where(sub < 3, xc, jnp.where(sub < 6, xs, jnp.where(sub == 6, 1.0, 0.0))), zero
        )
        fb = feat_blk[:, cols].astype(F32)
        hot = jnp.broadcast_to(species_ref[0:1, cols], (8, CHUNK)) == sub
        sources = []
        for c in range(2):
            s = jnp.where(which[c], fb, 0.0) + jnp.where(hot, tabs[c], 0.0)
            s = jnp.broadcast_to(jnp.sum(s, axis=0, keepdims=True), (8, CHUNK))
            s = s.astype(BF16).astype(F32)
            sources.append(s)
            szc, szs = s * zc, s * zs
            store(sz, 48 * c, cols, szc, szs)
            store(sz, 48 * c + 16, cols, szc * vc, szs * vc)
            store(sz, 48 * c + 32, cols, szc * vs, szs * vs)
        store(sz, 96, cols, jnp.where(sub < 3, sources[0], sources[1]) * ones, zero)
        return 0

    def mil_copy(ref, to, stage):
        return pltpu.make_async_remote_copy(
            src_ref=ref,
            dst_ref=ref,
            send_sem=mil_send.at[stage],
            recv_sem=mil_recv.at[stage],
            device_id=(ia, to),
            device_id_type=MESH,
        )

    own = mil_all.at[:, pl.ds(pl.multiple_of(ik * 128, 128), 128)]
    own_row = mil_all.at[:, pl.ds(pl.multiple_of(iy * (nz * 128), nz * 128), nz * 128)]
    all_z = mil_copy(mil_all.at[:, 0 : (nz - 1) * 128], ik, 0)
    all_y = mil_copy(mil_all.at[:, 0 : (ny - 1) * nz * 128], ik, 1)

    def farther(k, n):
        return n // 2 + (1 - 2 * lax.rem(k, 2)) * ((k + 1) // 2)

    def send_z(i, _):
        mil_copy(own, along_z(farther(i, nz)), 0).start()
        return 0

    def send_y(d, _):
        mil_copy(own_row, along_y(d), 1).start()
        return 0

    lax.fori_loop(0, EARLY, gather_chunk, 0)
    pl.semaphore_wait(barrier, nz - 1 + ny - 1 + n_atom - 1)
    lax.fori_loop(0, nz - 1, send_z, 0)
    lax.fori_loop(EARLY, n_chunks, gather_chunk, 0)

    halves = ((0, SR, GR),)

    def g_copy(half, slot, to):
        lo, _, hi = halves[half]
        return pltpu.make_async_remote_copy(
            src_ref=gsend.at[lo:hi],
            dst_ref=grecv.at[slot, lo:hi],
            send_sem=g_send.at[half],
            recv_sem=g_recv.at[half],
            device_id=(to, ik),
            device_id_type=MESH,
        )

    def all_g(half):
        lo, _, hi = halves[half]
        part = grecv.at[0 : n_atom - 1, lo:hi]
        return pltpu.make_async_remote_copy(
            src_ref=part,
            dst_ref=part,
            send_sem=g_send.at[half],
            recv_sem=g_recv.at[half],
            device_id=(ia, ik),
            device_id_type=MESH,
        )

    for half, (lo, up_to, hi) in enumerate(halves):

        def add_products(j, _, lo=lo, up_to=up_to):
            cols = pl.ds(pl.multiple_of(j * DEPTH, DEPTH), DEPTH)
            gacc[lo:up_to, :] += lax.dot_general(
                sz[lo:up_to, cols], yu[:, cols], (((1,), (1,)), ((), ())), preferred_element_type=F32
            )
            return 0

        lax.fori_loop(0, atoms // DEPTH, add_products, 0)
        gsend[lo:hi, :] = gacc[lo:hi, :].astype(BF16)

        def send_g(i, _, half=half):
            g_copy(half, ia, lax.rem(ia + 1 + lax.rem(i + 2, n_atom - 1), n_atom)).start()
            return 0

        lax.fori_loop(0, n_atom - 1, send_g, 0)

    for copy in loads[5:]:
        copy.wait()
    sub1 = iota((8, 128), 0)
    r8 = (sub1 + 1).astype(F32)
    column = iota((NRBF, 64), 1)
    weights = [
        jnp.sum(jnp.where(column == 2 * ik + c, fw_ref[...], 0.0), axis=1, keepdims=True) * scaling
        for c in range(2)
    ]
    tu, a, ty, q, _ = lane_orders((8, 128), 1)
    af, qq = a.astype(F32) * 3.0, (q * q).astype(F32)
    third1 = jnp.where(sub1 < 3, sub1, sub1 - 3)
    b_row = jnp.where((third1 > 0) & (sub1 < 6), 1.0, 0.0)
    tv_row = jnp.where(third1 == 2, 1, 0)

    def radial_of(m, r):
        mag = jnp.sqrt(m * m + qq + r * r)
        acc = [jnp.zeros((8, 128), F32) for _ in range(2)]
        for b in range(NRBF):
            z = (mag - b * (K_CUTOFF / (NRBF - 1))) * (NRBF / K_CUTOFF)
            e = jnp.exp(-(z * z))
            for c in range(2):
                acc[c] = acc[c] + weights[c][b : b + 1, :] * e
        return acc

    zero1 = jnp.zeros((8, 128), F32)
    rad_0 = radial_of(af, r8)
    rad_p, rad_m = radial_of(af + 1.0, r8), radial_of(af - 1.0, r8)
    single_p, single_m = [
        jnp.where(sub1 < 3, v[0], v[1]) for v in (radial_of(af + b_row, zero1), radial_of(af - b_row, zero1))
    ]

    all_z.wait_recv()
    lax.fori_loop(1, ny, send_y, 0)

    all_y.wait_recv()
    _, a_r, _, q_r, used = lane_orders((LW, CHUNK), 0)
    codes = jnp.where(used, a_r * 9 + q_r, -1).astype(F32)
    b_sub = jnp.where(third == 0, 0.0, 1.0)
    b_sub = jnp.where(sub < 6, b_sub, -1.0)
    counts = jnp.zeros((128, LW), F32)
    for j in range(n_vec // CHUNK):
        m = mil_all[:, CHUNK * j : CHUNK * (j + 1)].astype(F32)
        mx, my, mz = [jnp.broadcast_to(m[i : i + 1, :], (8, CHUNK)) for i in range(3)]
        ma = jnp.round(mx * (1.0 / 3.0))
        mb = mx - 3.0 * ma
        ga, gb, gy, gz = [jnp.where(v < 0, -1.0, 1.0) for v in (ma, mb, my, mz)]
        code = jnp.abs(ma) * 9.0 + jnp.abs(my)
        hot_uy = jnp.where(codes == jnp.broadcast_to(code[0:1, :], (LW, CHUNK)), 1.0, 0.0).astype(BF16)
        ab, ar, br, aq, bq, qr = ga * gb, ga * gz, gb * gz, ga * gy, gb * gy, gy * gz
        az, absb = jnp.abs(mz), jnp.abs(mb)
        hz = jnp.where(az == orders, 1.0, 0.0)
        h1 = hz * absb
        h0 = hz - h1
        hs = jnp.where((az == 0.0) & (absb == b_sub), 1.0, 0.0)
        wr = jnp.concatenate(
            [h1, h1 * ab, h1 * ar, h1 * br, h1 * aq, h1 * bq, h1 * qr, h1 * (ab * qr)]
            + [h0, h0 * aq, h0 * ar, h0 * qr]
            + [hs, hs * ab, hs * aq, hs * bq],
            axis=0,
        ).astype(BF16)
        counts = counts + lax.dot_general(
            wr, hot_uy, (((1,), (1,)), ((), ())), preferred_element_type=F32
        )
    w = [counts[8 * i : 8 * i + 8, :] for i in range(16)]

    def mixed(plus, minus, plain, crossed):
        half_s, half_d = 0.5 * (plus + minus), 0.5 * (plus - minus)
        return half_s * plain + half_d * crossed, half_s * crossed + half_d * plain

    same_uy = tu == ty
    plain, coefs = [], []
    for t in range(2):
        plain.append((w[8], signed(same_uy, w[9]), signed(tu == t, w[10]), signed(ty == t, w[11])))
    for c in range(2):
        c_0, c_ab = mixed(rad_p[c], rad_m[c], w[0], w[1])
        c_ar, c_br = mixed(rad_p[c], rad_m[c], w[2], w[3])
        c_aq, c_bq = mixed(rad_p[c], rad_m[c], w[4], w[5])
        c_qr, c_all = mixed(rad_p[c], rad_m[c], w[6], w[7])
        at = lambda types, x: [signed(types == t, x) for t in range(2)]
        coefs.append(
            (c_0, signed(same_uy, c_aq), at(tu, c_ar), at(ty, c_qr), at(tu, c_ab), at(ty, c_bq), c_br)
            + ([signed(tu != ty, c_all), signed(same_uy, c_all)],)
        )
    s_0, s_ab = mixed(single_p, single_m, w[12], w[13])
    s_aq, s_bq = mixed(single_p, single_m, w[14], w[15])
    s_aq, s_ab, s_bq = signed(same_uy, s_aq), signed(tu == tv_row, s_ab), signed(ty == tv_row, s_bq)

    all_g(0).wait_recv()
    grecv[ia] = gsend[...]
    g = grecv[0].astype(F32)
    for i in range(1, n_atom):
        g = g + grecv[i].astype(F32)

    rows = []
    for c in range(2):
        gb = [[g[48 * c + 16 * v + 8 * t : 48 * c + 16 * v + 8 * t + 8, :] for t in range(2)] for v in range(3)]
        gu = [[swap_u(x) for x in pair] for pair in gb]
        gy = [[swap_y(x) for x in pair] for pair in gb]
        guy = [[swap_u(x) for x in pair] for pair in gy]
        for t in range(2):
            p_0, p_aq, p_ar, p_qr = plain[t]
            h = p_0 * gb[0][t] + p_aq * guy[0][t] + p_ar * gu[0][1 - t] + p_qr * gy[0][1 - t]
            rows.append(h * rad_0[c])
        c_0, c_aq, c_ar, c_qr, c_ab, c_bq, c_br, c_all = coefs[c]
        for v in (1, 2):
            tv, o = v - 1, 3 - v
            for t in range(2):
                h = c_0 * gb[v][t] + c_aq * guy[v][t] + c_ar[t] * gu[v][1 - t] + c_qr[t] * gy[v][1 - t]
                h = h + c_ab[tv] * gu[o][t] + c_bq[tv] * gy[o][t]
                cross = c_br * gb[o][1 - t]
                h = h - cross if tv == t else h + cross
                rows.append(h + c_all[(tv + t) % 2] * guy[o][1 - t])
    g0 = g[96:104, :]
    over = jnp.where(third1 == 1, pltpu.roll(g0, 7, 0), pltpu.roll(g0, 1, 0))
    over = jnp.where(b_row > 0.0, over, 0.0)
    h = s_0 * g0 + s_aq * swap_u(swap_y(g0)) + s_ab * swap_u(over) + s_bq * swap_y(over)
    rows += [h, jnp.zeros((8, LW), F32)]
    hmat[...] = jnp.concatenate(rows, axis=0).astype(BF16)

    def m_copy(slot, to):
        return pltpu.make_async_remote_copy(
            src_ref=msgs.at[to],
            dst_ref=mrecv.at[slot],
            send_sem=m_send,
            recv_sem=m_recv,
            device_id=(ia, to),
            device_id_type=MESH,
        )

    def message_of(d, cols):
        zc, zs = zz[0:8, cols], zz[8:16, cols]
        vs = (None, vb[0:8, cols], vb[8:16, cols])
        single = d[96:104, :] * vv[:, cols]
        parts = []
        for c in range(2):
            s = jnp.where((sub < 3) == (c == 0), single, 0.0)
            for v in range(3):
                r = 48 * c + 16 * v
                e = d[r : r + 8, :] * zc + d[r + 8 : r + 16, :] * zs
                s = s + (e if v == 0 else e * vs[v])
            s = jnp.sum(s, axis=0, keepdims=True)
            parts += [s[:, 128 * i : 128 * (i + 1)] for i in range(CHUNK // 128)]
        return jnp.concatenate(parts, axis=0).astype(BF16)

    y_rows = [lax.rem(iy + ny // 2 + (k + 1) // 2 * (1 - 2 * (k % 2)), ny) * nz for k in range(ny)]

    def send_messages(i, last):
        z = lax.rem(iz + farther(i, nz), nz)
        to = [y + z for y in y_rows]
        cols = [pl.ds(pl.multiple_of(j * CHUNK, CHUNK), CHUNK) for j in to]
        ds = [jnp.dot(hmat[...], yu[:, c], preferred_element_type=F32) for c in cols]
        for k in range(ny):
            msgs[to[k]] = message_of(ds[k], cols[k])
            if last is None or k < ny - 1:
                m_copy(ik, to[k]).start()

    def send_step(i, _):
        send_messages(i, None)
        return 0

    lax.fori_loop(0, nz - 1, send_step, 0)
    send_messages(nz - 1, True)
    mrecv[ik] = msgs[ik]
    eye = iota((64, 64), 0) == iota((64, 64), 1)
    gain = jnp.sum(jnp.where(eye, jnp.broadcast_to(gain_ref[...], (64, 64)), 0.0), axis=1, keepdims=True)

    def all_messages():
        return pltpu.make_async_remote_copy(
            src_ref=mrecv.at[0 : n_ka - 1],
            dst_ref=mrecv.at[0 : n_ka - 1],
            send_sem=m_send,
            recv_sem=m_recv,
            device_id=(ia, ik),
            device_id_type=MESH,
        )

    all_messages().wait_recv()

    mflat[...] = mrecv[...].astype(F32).reshape(mflat.shape)
    message = jnp.concatenate(
        [mflat[pl.ds(i, 64, stride=4), :] for i in range(local // 128)], axis=1
    )
    mean_sq = jnp.sum(message * message, axis=0, keepdims=True) * (1.0 / 64.0)
    normed = (message * lax.rsqrt(mean_sq + 1e-06) * gain).astype(BF16)
    hidden = lax.dot_general(up_ref[...], normed, (((0,), (0,)), ((), ())), preferred_element_type=F32)
    half = 0.5 * hidden
    hidden = (half + half * jnp.tanh(half)).astype(BF16)
    update = jnp.dot(down_ref[...], hidden, preferred_element_type=F32)
    out_ref[...] = (feat_loc[...].astype(F32) + update).astype(BF16)

    all_z.wait_send()
    all_y.wait_send()
    all_messages().wait_send()
    all_g(0).wait_send()


def solution(mesh):
    n_atom, n_ka = mesh.shape["atom"], mesh.shape["ka"]
    ny, nz = 4, n_ka // 4

    def body(positions, features, species, miller, species_table, filter_weight, norm_gain, up_weight, down_weight):
        channels, atoms = features.shape
        local = atoms // n_ka
        n_vectors = miller.shape[1] * n_ka
        hid = up_weight.shape[0]
        scaling = 1.0 / math.sqrt(atoms * n_atom * n_vectors)
        any_space = pl.BlockSpec(memory_space=pltpu.HBM)
        return pl.pallas_call(
            functools.partial(body_kernel, (n_atom, n_ka, ny, nz, atoms, scaling)),
            out_shape=jax.ShapeDtypeStruct((channels, local), BF16),
            in_specs=[any_space] * 9,
            out_specs=pl.BlockSpec(memory_space=pltpu.VMEM),
            scratch_shapes=[
                pltpu.VMEM((3, atoms), F32),
                pltpu.VMEM((1, atoms), jnp.int32),
                pltpu.VMEM((3, 128), jnp.int32),
                pltpu.VMEM((NSPEC, channels), F32),
                pltpu.VMEM((NRBF, channels), F32),
                pltpu.VMEM((1, channels), F32),
                pltpu.VMEM((channels, hid), BF16),
                pltpu.VMEM((channels, hid), BF16),
                pltpu.VMEM((8, atoms), BF16),
                pltpu.VMEM((channels, local), BF16),
                pltpu.VMEM((LW, atoms + PAD), BF16),
                pltpu.VMEM((SR, atoms + PAD), BF16),
                pltpu.VMEM((16, atoms + PAD), F32),
                pltpu.VMEM((16, atoms + PAD), F32),
                pltpu.VMEM((8, atoms + PAD), F32),
                pltpu.VMEM((16, CHUNK), F32),
                pltpu.VMEM((SR, LW), F32),
                pltpu.VMEM((GR, LW), BF16),
                pltpu.VMEM((n_atom, GR, LW), BF16),
                pltpu.VMEM((8, n_vectors), BF16),
                pltpu.VMEM((SR, LW), BF16),
                pltpu.VMEM((n_ka, 8, 128), BF16),
                pltpu.VMEM((n_ka, 8, 128), BF16),
                pltpu.VMEM((n_ka * 8, 128), F32),
                pltpu.SemaphoreType.DMA((10,)),
                pltpu.SemaphoreType.DMA((2,)),
                pltpu.SemaphoreType.DMA((2,)),
                pltpu.SemaphoreType.DMA((1,)),
                pltpu.SemaphoreType.DMA((1,)),
                pltpu.SemaphoreType.DMA,
                pltpu.SemaphoreType.DMA,
            ],
            compiler_params=pltpu.CompilerParams(
                collective_id=0, has_side_effects=True, vmem_limit_bytes=24 * 1024 * 1024
            ),
            name="ewald",
        )(*[pltpu.with_memory_space_constraint(v, pltpu.HBM) for v in (
            positions,
            features,
            species.reshape(1, atoms),
            miller,
            species_table.T,
            filter_weight.T,
            norm_gain.reshape(1, channels),
            up_weight.T,
            down_weight,
        )])

    in_specs = (P(None, "atom"), P(None, "atom"), P("atom"), P(None, "ka"), P(), P(), P(), P(), P())
    out_specs = P(None, ("atom", "ka"))
    return jax.shard_map(body, mesh=mesh, in_specs=in_specs, out_specs=out_specs, check_vma=False)
```
